32 devices in a mesh: expert: 8 (over z, x), fsdp: 4 (over y, core).
Axes of the slice: x: 2, y: 2, z: 4, core: 2. Of those that a mesh axis runs over, the one named last changes fastest.
Arguments:
- tokens_in: bfloat16 [25216, 768], P(('expert', 'fsdp')), may hold values from -6 to 6
- routes: int32 [2, 25216, 2], P(None, ('expert', 'fsdp')), may hold values from 0 to 31, all different within a row; in each aligned block of 788 rows (0 to 787, 788 to 1575, ..., all dimensions but the last counted through in order) at most 64 rows name the same one
- valid: int32 [2, 25216, 2], P(None, ('expert', 'fsdp')), may hold values 0 or 1
- qkv_weight: bfloat16 [2, 768, 2304], P(None, 'fsdp'), may hold values from -0.21875 to 0.21875
- out_weight: bfloat16 [2, 768, 768], P(None, 'fsdp'), may hold values from -1.75 to 1.75
- router_weight: bfloat16 [2, 768, 32], P(None, 'fsdp'), may hold values from -0.3125 to 0.3125
- norm_gain: bfloat16 [2, 2, 768], P(None, None, 'fsdp'), may hold values from 0.099609375 to 1.8984375
- norm_shift: bfloat16 [2, 2, 768], P(None, None, 'fsdp'), may hold values from -1.5 to 1.5
- expert_in: bfloat16 [2, 32, 768, 3072], P(None, 'expert', None, 'fsdp'), may hold values from -0.21875 to 0.21875
- expert_down: bfloat16 [2, 32, 768, 3072], P(None, 'expert', None, 'fsdp'), may hold values from -2.5 to 2.5
- cotangent: bfloat16 [25216, 768], P(('expert', 'fsdp')), may hold values from -6 to 6
Outputs:
- out: bfloat16 [25216, 768], P(('expert', 'fsdp'))
- grad_in: float32 [25216, 768], P(('expert', 'fsdp'))
- grad_qkv: float32 [2, 768, 2304], P(None, 'fsdp')
- grad_out_weight: float32 [2, 768, 768], P(None, 'fsdp')
- grad_router: float32 [2, 768, 32], P(None, 'fsdp')
- grad_gain: float32 [2, 2, 768], P(None, None, 'fsdp')
- grad_shift: float32 [2, 2, 768], P(None, None, 'fsdp')
- grad_expert_in: float32 [2, 32, 768, 3072], P(None, 'expert', None, 'fsdp')
- grad_expert_down: float32 [2, 32, 768, 3072], P(None, 'expert', None, 'fsdp')
The draws below stay inside these ranges and needn't reach their ends.
Inputs may be any that keep to these rules, and one draw needn't show every extreme that they name: `routes`: in each block, the 788 tokens of one device name no expert more than 64 times; some device names some expert exactly 64 times. A token's 2 experts differ.
All inputs are finite; a program needn't handle non-finite values. No bound on the sum of `valid` on one device may be relied on, other than what follows from the above.
Results may differ from the reference program's by a relative error of at most 0.025.
Values may be sent and summed in bfloat16 or wider, within the bound.
No kernel may reach another device: no remote copies, remote signals or barrier semaphores. Data moves between devices by JAX's collectives and lax.ppermute only.
A program may use at most 448 MiB of HBM per device.

```python
import math
import jax
import jax.numpy as jnp
import numpy as np
from jax import lax

D = 768
HEADS = 12
HEAD = 64
FF = 3072
EXPERTS = 32
TOP = 2
SEQ = 197
LAYERS = 2
TOK_DEV = 788
CAP = 64
IMAGES = 128
TOKENS = 25216
DEVICES = 32


def set_ends(drawn, rng, least, top_value):
    index_at = [jax.random.randint(jax.random.fold_in(rng, axis), (), 0, length) for axis, length in enumerate(drawn.shape)]
    main_axis = drawn.shape.index(max(drawn.shape))
    neighbour = index_at[:main_axis] + [(index_at[main_axis] + 1) % drawn.shape[main_axis]] + index_at[main_axis + 1:]
    return drawn.at[tuple(index_at)].set(least).at[tuple(neighbour)].set(top_value)


def levels(rng, shape, shards, low, top_value):
    def one(dim, parts):
        heights = jax.random.uniform(jax.random.fold_in(jax.random.fold_in(rng, 6), dim), (parts,), jnp.float32, low / len(shards), top_value / len(shards))
        return jnp.repeat(jnp.exp(heights), shape[dim] // parts).reshape((-1,) + (1,) * (len(shape) - dim - 1))

    level = one(*shards[0])
    for cut in shards[1:]:
        level = level * one(*cut)
    return level


def assign_block(stream_key, own, number, rows, count, top, reach, slope):
    order = jax.random.permutation(stream_key, count)
    crowded, ordinary = load_shares(count, rows * top, reach, slope, True), load_shares(count, rows * top, reach, slope, False)
    places = jnp.arange(count)

    def named(tallies, rotation):
        used = int((tallies > 0).sum())
        fixed = max(1, used // 4)
        shifted = fixed + (places - fixed + rotation * (used - fixed)) % max(1, count - fixed)
        return jnp.zeros((count,), jnp.int32).at[order[jnp.where(places < fixed, places, shifted)]].set(jnp.asarray(tallies, jnp.int32))

    tallies = jnp.where(number % 4 == 0, named(crowded, number // 4), named(ordinary, number - number // 4 - 1))
    mixed = jax.random.permutation(jax.random.fold_in(own, 3), count)
    source_of, sink = mixed[0:count // 2 * 2:2], mixed[1:count // 2 * 2:2]
    slack = jnp.minimum(tallies[source_of] - 1, reach - tallies[sink]) // 2
    slack = jnp.where((source_of == order[0]) | (sink == order[0]) | (tallies[sink] == 0), 0, jnp.maximum(slack, 0))
    shifted = jax.random.randint(jax.random.fold_in(own, 4), (count // 2,), 0, 1 << 20) % (slack + 1)
    tallies = tallies.at[source_of].add(-shifted).at[sink].add(shifted)
    items = jnp.searchsorted(jnp.cumsum(tallies), jnp.arange(rows * top), side="right").astype(jnp.int32)
    listing = items.reshape(top, rows).T
    listing = listing[jax.random.permutation(jax.random.fold_in(own, 1), rows)]
    rotation = jax.random.randint(jax.random.fold_in(own, 2), (rows, 1), 0, top)
    return jnp.take_along_axis(listing, (jnp.arange(top)[None, :] + rotation) % top, axis=1)


def load_shares(count, total, limit, skew, full):
    weights = [(1 << 20) // math.isqrt(grade ** skew) + 1 for grade in range(1, count + 1)]
    largest = limit if full else min(limit, max(-(-total // count), total * weights[0] // sum(weights)))
    least = 1 if total - largest >= count - 1 else 0
    given, rest = [largest] + [least] * (count - 1), total - largest - least * (count - 1)
    while rest > 0:
        free = [i for i in range(1, count) if given[i] < largest] or [i for i in range(1, count) if given[i] < limit]
        whole, left = sum([weights[i] for i in free]), rest
        for i in free:
            more = min(limit - given[i], max(1, left * weights[i] // whole), rest)
            given[i] = given[i] + more
            rest = rest - more
    return np.array(given)


def normal_values(key, extent, width, bound, pieces=(), held_as=jnp.bfloat16):
    drawn = jax.random.normal(key, extent, jnp.float32) * width
    if len(pieces) > 0:
        drawn = levels(key, extent, pieces, -0.22, 0.18) * drawn
    return jnp.clip(drawn, min=-bound, max=bound).astype(held_as)


def setup_inputs(seed: int = 0) -> dict:
    key_of = jax.random.split(jax.random.key(seed), 12)
    tokens_in = normal_values(key_of[0], (TOKENS, D), 1.0, 6.0, ((0, 32),))
    routes_keys = jax.random.split(jax.random.fold_in(key_of[1], 1), LAYERS * TOKENS // TOK_DEV)
    routes_turns = jax.random.permutation(jax.random.fold_in(key_of[1], 3), LAYERS * TOKENS // TOK_DEV)
    routes = jax.vmap(lambda own, number: assign_block(jax.random.fold_in(key_of[1], 2), own, number, TOK_DEV, EXPERTS, TOP, CAP, 2))(routes_keys, routes_turns).reshape((LAYERS, TOKENS, TOP))
    valid = set_ends((jax.random.randint(key_of[2], (LAYERS, TOKENS, TOP), 0, 8) < 7).astype(jnp.int32), jax.random.fold_in(key_of[2], 1), 0, 1)
    qkv_weight = normal_values(key_of[3], (LAYERS, D, 3 * D), D ** -0.5, 0.21875, ((1, 4),))
    out_weight = normal_values(key_of[4], (LAYERS, D, D), (D // 64) ** -0.5, 1.75, ((1, 4),))
    router_weight = normal_values(key_of[5], (LAYERS, D, EXPERTS), (D // 2) ** -0.5, 0.3125, ((1, 4),))
    norm_gain = jnp.clip(1.0 + 0.18 * jax.random.normal(key_of[6], (LAYERS, 2, D), jnp.float32), 0.099609375, 1.8984375).astype(jnp.bfloat16)
    norm_shift = normal_values(key_of[7], (LAYERS, 2, D), 0.3, 1.5, ((2, 4),))
    expert_in = normal_values(key_of[8], (LAYERS, EXPERTS, D, FF), D ** -0.5, 0.21875, ((1, 8), (3, 4)))
    expert_down = normal_values(key_of[9], (LAYERS, EXPERTS, D, FF), (max(FF // 512, 1)) ** -0.5, 2.5, ((1, 8), (3, 4)))
    cotangent = normal_values(key_of[10], (TOKENS, D), 1.0, 6.0, ((0, 32),))
    return {"tokens_in": tokens_in, "routes": routes, "valid": valid, "qkv_weight": qkv_weight, "out_weight": out_weight, "router_weight": router_weight, "norm_gain": norm_gain, "norm_shift": norm_shift, "expert_in": expert_in, "expert_down": expert_down, "cotangent": cotangent}


@jax.custom_vjp
def low(v):
    return lax.optimization_barrier(v.astype(jnp.bfloat16)).astype(jnp.float32)

@jax.custom_vjp
def low_back(v):
    return v

def low_keep(v):
    return (low(v), None)

def low_pass(kept, grad):
    return (grad,)

def back_keep(v):
    return (v, None)

def back_low(kept, grad):
    return (low(grad),)
low.defvjp(low_keep, low_pass)
low_back.defvjp(back_keep, back_low)
epsilon = 1e-06
gelu_coeff = 0.7978845608028654
highest = lax.Precision.HIGHEST

def gelu_tanh(pre_value):
    return 0.5 * pre_value * (1.0 + jnp.tanh(gelu_coeff * (pre_value + 0.044715 * pre_value * pre_value * pre_value)))

def layer_norm(stream, gain_row, shift_row):
    average = lax.optimization_barrier(jnp.mean(stream, -1, keepdims=True))
    centred = stream - average
    variance = lax.optimization_barrier(jnp.mean(centred * centred, -1, keepdims=True))
    return centred * lax.rsqrt(variance + epsilon) * gain_row + shift_row

def softmax_rows(scores):
    top_score = lax.optimization_barrier(jnp.max(scores, -1, keepdims=True))
    weights = jnp.exp(scores - top_score)
    return weights / lax.optimization_barrier(jnp.sum(weights, -1, keepdims=True))

def slot_table(route_rows):
    flat_routes = route_rows.reshape(DEVICES, TOK_DEV * TOP).astype(jnp.int32)
    one_hot = (flat_routes[:, :, None] == jnp.arange(EXPERTS, dtype=jnp.int32)[None, None, :]).astype(jnp.int32)
    earlier = jnp.cumsum(one_hot, axis=1, dtype=jnp.int32) - one_hot
    slot_index = lax.optimization_barrier(jnp.sum(earlier * one_hot, axis=2)).astype(jnp.int32)
    device_index = jnp.arange(DEVICES, dtype=jnp.int32)[:, None]
    return (device_index * CAP + slot_index).reshape(TOKENS, TOP).astype(jnp.int32)

def attend(qkv_block):
    query_rows = qkv_block[:, :, 0]
    key_rows = qkv_block[:, :, 1]
    value_rows = qkv_block[:, :, 2]
    scores = low_back(jnp.einsum('gqhd,gkhd->ghqk', query_rows, key_rows, precision=highest) * HEAD ** (-0.5))
    attn_probs = low(softmax_rows(scores))
    return jnp.einsum('ghqk,gkhd->gqhd', attn_probs, value_rows, precision=highest)

def expert_ffn(operands):
    token_rows, weight_in, weight_down = operands
    pre_act = low_back(jnp.dot(token_rows, weight_in, precision=highest))
    hidden = low(gelu_tanh(pre_act))
    return low(low_back(jnp.dot(hidden, weight_down.T, precision=highest)))

def make_forward(routes, places, valid_float):

    def forward(stream, qkv_w, out_w, router_w, gain_set, shift_set, ex_in, ex_down):
        block_images = 16
        for layer_index in range(LAYERS):
            normed_one = low(layer_norm(stream, gain_set[layer_index, 0], shift_set[layer_index, 0]))
            qkv_all = low_back(low(jnp.dot(normed_one, qkv_w[layer_index], precision=highest)))
            blocks = qkv_all.reshape(IMAGES // block_images, block_images, SEQ, 3, HEADS, HEAD)
            attended = lax.map(jax.checkpoint(attend), blocks).reshape(TOKENS, D)
            attended = low_back(low(attended))
            branch = low_back(jnp.dot(attended, out_w[layer_index], precision=highest))
            middle = stream + branch
            normed_two = low(layer_norm(middle, gain_set[layer_index, 1], shift_set[layer_index, 1]))
            logits = low_back(jnp.dot(normed_two, router_w[layer_index], precision=highest))
            router_probs = softmax_rows(logits)
            gate_values = jnp.take_along_axis(router_probs, routes[layer_index], axis=1) * valid_float[layer_index]
            buffer = jnp.zeros((EXPERTS, DEVICES * CAP, D), jnp.float32)
            buffer = buffer.at[routes[layer_index], places[layer_index]].add(normed_two[:, None, :] * valid_float[layer_index][:, :, None])
            buffer = low_back(buffer)
            expert_out = lax.map(jax.checkpoint(expert_ffn), (buffer, ex_in[layer_index], ex_down[layer_index]))
            picked = expert_out[routes[layer_index], places[layer_index]]
            stream = middle + lax.optimization_barrier(jnp.sum(gate_values[:, :, None] * picked, axis=1))
        return stream
    return forward

def reference(tokens_in, routes, valid, qkv_weight, out_weight, router_weight, norm_gain, norm_shift, expert_in, expert_down, cotangent):
    routes = routes.astype(jnp.int32)
    places = jnp.stack([slot_table(routes[layer_index]) for layer_index in range(LAYERS)])
    valid_float = valid.astype(jnp.float32)
    forward = make_forward(routes, places, valid_float)
    primals = tuple((operand.astype(jnp.float32) for operand in (tokens_in, qkv_weight, out_weight, router_weight, norm_gain, norm_shift, expert_in, expert_down)))
    result, pullback = jax.vjp(forward, *primals)
    grad_list = pullback(cotangent.astype(jnp.float32))
    return (result.astype(jnp.bfloat16), grad_list[0], grad_list[1], grad_list[2], grad_list[3], grad_list[4], grad_list[5], grad_list[6], grad_list[7])
```

```python
import jax
import jax.numpy as jnp
from jax import lax
from jax.experimental import pallas as pl
from jax.experimental.pallas import tpu as pltpu
from jax.sharding import PartitionSpec as P

HEADS = 12
HEAD = 64
SEQ = 197
SEQ_PAD = 256
CAP = 64
LANES = 128
BF = jnp.bfloat16
F32 = jnp.float32
EPS = 1e-06
GELU = 0.7978845608028654
CUBE = 0.044715
VMEM_LIMIT = 56 << 20
NEG = -1e30


def nn(left, right):
    return lax.dot_general(left, right, (((1,), (0,)), ((), ())), preferred_element_type=F32)


def nt(left, right):
    return lax.dot_general(left, right, (((1,), (1,)), ((), ())), preferred_element_type=F32)


def tn(left, right):
    return lax.dot_general(left, right, (((0,), (0,)), ((), ())), preferred_element_type=F32)


def gelu(u):
    return 0.5 * u * (1.0 + jnp.tanh(GELU * (u + CUBE * u * u * u)))


def gelu_both(u):
    square = u * u
    t = jnp.tanh(GELU * u * (1.0 + CUBE * square))
    half = 0.5 * (1.0 + t)
    return u * half, half + 0.5 * u * (1.0 - t * t) * (GELU * (1.0 + 3.0 * CUBE * square))


def normalise(v):
    centred = v - jnp.mean(v, -1, keepdims=True)
    inv = lax.rsqrt(jnp.mean(centred * centred, -1, keepdims=True) + EPS)
    return centred * inv, inv


def norm_pull(grad, hat, inv, gain):
    scaled = grad * gain
    pulled = inv * (
        scaled
        - jnp.mean(scaled, -1, keepdims=True)
        - hat * jnp.mean(scaled * hat, -1, keepdims=True)
    )
    return pulled, jnp.sum(grad * hat, 0, keepdims=True), jnp.sum(grad, 0, keepdims=True)


def resident(shape, index):
    return pl.BlockSpec(shape, index, pipeline_mode=pl.Buffered(1))


def fixed(array):
    zeros = (0,) * array.ndim
    return resident(array.shape, lambda i: zeros)


def per_image(*tail):
    zeros = (0,) * len(tail)
    return pl.BlockSpec((None,) + tail, lambda i: (i,) + zeros)


def cost(flops, byte_count, exps):
    return pl.CostEstimate(
        flops=int(flops), bytes_accessed=int(byte_count), transcendentals=int(exps)
    )


def params():
    return pltpu.CompilerParams(vmem_limit_bytes=VMEM_LIMIT)


def lanes(shape):
    return lax.broadcasted_iota(jnp.int32, shape, 1)


def pick_rows(columns, slots, start):
    hit = lanes((columns[0].shape[0], slots)) == columns[0] - start
    for column in columns[1:]:
        hit = hit | (lanes((column.shape[0], slots)) == column - start)
    return jnp.where(hit, 1.0, 0.0).astype(BF)


def place_rows(rows, slots, start):
    sub = lax.broadcasted_iota(jnp.int32, (slots, rows[0].shape[1]), 0)
    hit = sub == rows[0] - start
    for row in rows[1:]:
        hit = hit | (sub == row - start)
    return jnp.where(hit, 1.0, 0.0).astype(BF)


def norm_rows(pack_ref, width):
    tail = pack_ref[:, 4 * width :].astype(F32)
    return jnp.transpose(tail)


def block_forward(stream, pack, routes, pcol, prow, previous, want_rows, slots):
    images, seq, width = stream.shape
    chunks = 4 * width
    local = slots[0]
    span = slots[1]
    has_prev = previous is not None
    inputs = [stream, pack, routes, pcol, prow]
    specs = [per_image(seq, width), fixed(pack), per_image(seq, 2), per_image(seq, 2), fixed(prow)]
    if has_prev:
        inputs += list(previous[0]) + [previous[1], previous[2]]
        specs += [fixed(a) for a in previous[0]] + [per_image(seq, 2), per_image(seq, 2)]
    shapes, ospecs = [], []

    def out(shape, dtype, spec):
        shapes.append(jax.ShapeDtypeStruct(shape, dtype))
        ospecs.append(spec)

    out((images, seq, 3 * width), BF, per_image(seq, 3 * width))
    out((images, 16, seq), F32, per_image(16, seq))
    out((images, seq, width), BF, per_image(seq, width))
    out((images, seq, width), F32, per_image(seq, width))
    out((images, seq, 2), F32, per_image(seq, 2))
    if has_prev:
        out((images, seq, width), F32, per_image(seq, width))
        out((images, seq, width), BF, per_image(seq, width))
        out((images, seq, width), BF, per_image(seq, width))
    for _ in range(local):
        out((span, width), BF, resident((span, width), lambda i: (0, 0)))
    if want_rows:
        out((8, local * span), F32, resident((8, local * span), lambda i: (0, 0)))
    scratch = [pltpu.VMEM((images * SEQ_PAD, width), BF), pltpu.VMEM((LANES, width), F32)]

    def body(*refs):
        refs = list(refs)
        x_ref, pack_ref, routes_ref, pcol_ref, prow_ref = refs[:5]
        at = 5
        if has_prev:
            eo_refs = refs[at : at + local]
            old_pcol_ref, old_gate_ref = refs[at + local : at + local + 2]
            at += local + 2
        qkv_ref, lse_ref, a_ref, h_ref, gate_ref = refs[at : at + 5]
        at += 5
        if has_prev:
            xs_ref, pick0_ref, pick1_ref = refs[at : at + 3]
            at += 3
        disp_refs = refs[at : at + local]
        at += local
        if want_rows:
            grow_ref = refs[at]
        store, norm_ref = refs[-2:]
        i = pl.program_id(0)

        @pl.when(i == 0)
        def _():
            norm_ref[...] = norm_rows(pack_ref, width)
            store[...] = jnp.zeros_like(store)
            if want_rows:
                grow_ref[...] = jnp.zeros_like(grow_ref)

        x = x_ref[...].astype(F32)
        if has_prev:
            for k, pick_ref in enumerate((pick0_ref, pick1_ref)):
                picked = None
                for j in range(local):
                    hot = pick_rows([old_pcol_ref[:, k : k + 1]], span, j * span)
                    term = nn(hot, eo_refs[j][...])
                    picked = term if picked is None else picked + term
                pick_ref[...] = picked.astype(BF)
                x = x + old_gate_ref[:, k : k + 1] * picked
            xs_ref[...] = x
        hat, _ = normalise(x)
        n1 = (hat * norm_ref[32:33, :] + norm_ref[34:35, :]).astype(BF)
        for c in range(3):
            qkv_ref[:, c * width : (c + 1) * width] = nn(
                n1, pack_ref[:, c * width : (c + 1) * width]
            ).astype(BF)
        lane = lanes((seq, LANES))
        lse_ref[...] = jnp.zeros_like(lse_ref)
        for pair in range(HEADS // 2):
            lo = pair * LANES
            q = qkv_ref[:, lo : lo + LANES]
            k = qkv_ref[:, width + lo : width + lo + LANES]
            v = qkv_ref[:, 2 * width + lo : 2 * width + lo + LANES]
            parts = []
            for half in range(2):
                mine = (lane < HEAD) if half == 0 else (lane >= HEAD)
                scores = nt(k, jnp.where(mine, q, jnp.zeros_like(q))) * HEAD ** (-0.5)
                top = jnp.max(scores, 0, keepdims=True)
                weights = jnp.exp(scores - top)
                total = jnp.sum(weights, 0, keepdims=True)
                lse_ref[2 * pair + half : 2 * pair + half + 1, :] = top + jnp.log(total)
                probs = (weights * (1.0 / total)).astype(BF)
                parts.append(tn(probs, v))
            a_ref[:, lo : lo + LANES] = jnp.where(lane < HEAD, parts[0], parts[1]).astype(BF)
        h = x + nn(a_ref[...], pack_ref[:, 3 * width : 4 * width])
        h_ref[...] = h
        hat, _ = normalise(h)
        n2 = (hat * norm_ref[33:34, :] + norm_ref[35:36, :]).astype(BF)
        logits = nn(n2, pack_ref[:, chunks : chunks + LANES])
        logits = jnp.where(lane < 32, logits, NEG)
        weights = jnp.exp(logits - jnp.max(logits, -1, keepdims=True))
        probs = weights / jnp.sum(weights, -1, keepdims=True)
        gates = []
        for k in range(2):
            chosen = jnp.where(lane == routes_ref[:, k : k + 1], probs, 0.0)
            kept = jnp.where(pcol_ref[:, k : k + 1] >= 0, 1.0, 0.0)
            gates.append(jnp.sum(chosen, -1, keepdims=True) * kept)
            gate_ref[:, k : k + 1] = gates[k]
        store[pl.ds(pl.multiple_of(i * SEQ_PAD, SEQ_PAD), seq), :] = n2
        if want_rows:
            where = lanes((seq, local * span))
            spread = [jnp.where(where == pcol_ref[:, k : k + 1], gates[k], 0.0) for k in range(2)]
            grow_ref[0:1, :] += jnp.sum(spread[0] + spread[1], 0, keepdims=True)

        @pl.when(i == images - 1)
        def _():
            rows = [prow_ref[0:1, :], prow_ref[1:2, :]]
            for j in range(local):
                disp_refs[j][...] = nn(place_rows(rows, span, j * span), store[...]).astype(BF)

    tokens = images * seq
    flops = 2 * tokens * width * (4 * width + 128) + 4 * HEADS * tokens * 256 * 128
    flops += 2 * (1 + 2 * has_prev) * local * span * tokens * width
    results = pl.pallas_call(
        body,
        grid=(images,),
        in_specs=specs,
        out_specs=ospecs,
        out_shape=shapes,
        scratch_shapes=scratch,
        compiler_params=params(),
        cost_estimate=cost(2 * flops, 20 * tokens * width, HEADS * tokens * seq),
        name="block_forward",
    )(*inputs)
    kept = dict(zip(("qkv", "lse", "a", "h", "gate"), results[:5]))
    rest = results[5:]
    kept["x"] = stream
    if has_prev:
        kept["x"] = rest[0]
        kept["picks"] = (rest[1], rest[2])
        rest = rest[3:]
    return kept, rest[:local], rest[local:]


def dispatch(rows, prow, slots):
    images, seq, width = rows.shape
    local, span = slots

    def body(rows_ref, prow_ref, *refs):
        outs, store = refs[:local], refs[local]
        store[...] = jnp.zeros_like(store)
        for i in range(images):
            store[i * SEQ_PAD : i * SEQ_PAD + seq, :] = rows_ref[i]
        for j in range(local):
            hot = place_rows([prow_ref[0:1, :], prow_ref[1:2, :]], span, j * span)
            outs[j][...] = nn(hot, store[...]).astype(BF)

    whole = resident((span, width), lambda i: (0, 0))
    return pl.pallas_call(
        body,
        grid=(1,),
        in_specs=[fixed(rows), fixed(prow)],
        out_specs=[whole] * local,
        out_shape=[jax.ShapeDtypeStruct((span, width), BF)] * local,
        scratch_shapes=[pltpu.VMEM((images * SEQ_PAD, width), BF)],
        compiler_params=params(),
        cost_estimate=cost(4 * local * span * images * seq * width, 8 * local * span * width, 0),
        name="dispatch",
    )(rows, prow)


def route_places(routes, valid, owners, local):
    layers, images, seq, _ = routes.shape

    def body(routes_ref, valid_ref, pcol_ref, prow_ref):
        prow_ref[...] = jnp.full(prow_ref.shape, -1, jnp.int32)
        lane = lanes((seq, LANES))
        below = lax.broadcasted_iota(jnp.int32, (seq, seq), 0) > lanes((seq, seq))
        below = jnp.where(below, 1.0, 0.0).astype(BF)
        base = jnp.zeros((1, LANES), F32)
        for i in range(images):
            hot = [jnp.where(lane == routes_ref[i, :, k : k + 1], 1.0, 0.0) for k in range(2)]
            both = hot[0] + hot[1]
            earlier = nn(below, both.astype(BF)) + base
            base = base + jnp.sum(both, 0, keepdims=True)
            columns = jnp.full((seq, LANES), -1.0, F32)
            for k in range(2):
                slot = jnp.sum(hot[k] * earlier, -1, keepdims=True)
                expert = routes_ref[i, :, k : k + 1]
                owner = expert // local
                start = ((expert - owner * local) * owners + owner) * CAP
                place = jnp.where(valid_ref[i, :, k : k + 1] > 0, start.astype(F32) + slot, -1.0)
                pcol_ref[i, :, k : k + 1] = place.astype(jnp.int32)
                columns = jnp.where(lane == k, place, columns)
            padded = jnp.concatenate([columns, jnp.full((SEQ_PAD - seq, LANES), -1.0, F32)], 0)
            prow_ref[:, i * SEQ_PAD : (i + 1) * SEQ_PAD] = jnp.transpose(padded)[0:8, :].astype(jnp.int32)

    spec = pl.BlockSpec((None, images, seq, 2), lambda l: (l, 0, 0, 0))
    return pl.pallas_call(
        body,
        grid=(layers,),
        in_specs=[spec, spec],
        out_specs=[spec, pl.BlockSpec((None, 8, images * SEQ_PAD), lambda l: (l, 0, 0))],
        out_shape=[
            jax.ShapeDtypeStruct((layers, images, seq, 2), jnp.int32),
            jax.ShapeDtypeStruct((layers, 8, images * SEQ_PAD), jnp.int32),
        ],
        compiler_params=params(),
        cost_estimate=cost(2 * layers * images * seq * seq * LANES, 1 << 20, 0),
        name="route_places",
    )(routes, valid)


def combine_last(h, expert_rows, pcol, gate):
    images, seq, width = h.shape
    local = len(expert_rows)
    span = expert_rows[0].shape[0]

    def body(h_ref, pcol_ref, gate_ref, *refs):
        eo_refs, out_ref = refs[:local], refs[local]
        x = h_ref[...]
        for k in range(2):
            picked = None
            for j in range(local):
                term = nn(pick_rows([pcol_ref[:, k : k + 1]], span, j * span), eo_refs[j][...])
                picked = term if picked is None else picked + term
            x = x + gate_ref[:, k : k + 1] * picked
        out_ref[...] = x.astype(BF)

    return pl.pallas_call(
        body,
        grid=(images,),
        in_specs=[per_image(seq, width), per_image(seq, 2), per_image(seq, 2)]
        + [fixed(a) for a in expert_rows],
        out_specs=per_image(seq, width),
        out_shape=jax.ShapeDtypeStruct((images, seq, width), BF),
        compiler_params=params(),
        cost_estimate=cost(8 * local * span * images * seq * width, 20 * images * seq * width, 0),
        name="combine_last",
    )(h, pcol, gate, *expert_rows)


def block_backward(grad, kept, pack, routes, pcol, expert_grads, gate_grads, below, slots):
    images, seq, width = grad.shape
    local, span = slots
    has_below = below is not None
    has_gg = gate_grads is not None
    row3, row2 = per_image(seq, width), per_image(seq, 2)
    inputs = [grad, kept["x"], kept["h"], kept["qkv"], kept["lse"], pack, routes, pcol]
    specs = [row3, row3, row3, per_image(seq, 3 * width), per_image(16, seq), fixed(pack), row2, row2]
    inputs += list(expert_grads)
    specs += [fixed(a) for a in expert_grads]
    if has_gg:
        inputs.append(gate_grads)
        specs.append(fixed(gate_grads))
    else:
        inputs += list(kept["picks"])
        specs += [row3, row3]
    if has_below:
        inputs += [below[0], below[1]]
        specs += [row2, fixed(below[1])]
    shapes, ospecs = [], []

    def out(shape, dtype, spec):
        shapes.append(jax.ShapeDtypeStruct(shape, dtype))
        ospecs.append(spec)

    out((images, seq, width), F32, row3)
    out((images, seq, width), BF, row3)
    out((images, seq, 3 * width), BF, per_image(seq, 3 * width))
    out((images, seq, width), BF, row3)
    out((images, seq, width), BF, row3)
    out((images, seq, LANES), BF, per_image(seq, LANES))
    out((8, width), F32, resident((8, width), lambda i: (0, 0)))
    if has_below:
        for _ in range(local):
            out((span, width), BF, resident((span, width), lambda i: (0, 0)))
    scratch = [pltpu.VMEM((images * SEQ_PAD, width), BF)] * (2 if has_below else 0)
    scratch += [pltpu.VMEM((LANES, width), F32), pltpu.VMEM((seq, width), BF)]

    def body(*refs):
        refs = list(refs)
        grad_ref, x_ref, h_ref, qkv_ref, lse_ref, pack_ref, routes_ref, pcol_ref = refs[:8]
        at = 8
        gbuf_refs = refs[at : at + local]
        at += local
        if has_gg:
            gg_ref = refs[at]
            at += 1
        else:
            pick_refs = refs[at : at + 2]
            at += 2
        if has_below:
            below_gate_ref, below_prow_ref = refs[at : at + 2]
            at += 2
        gx_ref, gbr_ref, gqkv_ref, n1_ref, n2_ref, glog_ref, norms_ref = refs[at : at + 7]
        at += 7
        if has_below:
            geo_refs = refs[at : at + local]
            at += local
            stores = refs[at : at + 2]
        norm_ref, ga_ref = refs[-2:]
        i = pl.program_id(0)

        @pl.when(i == 0)
        def _():
            norm_ref[...] = norm_rows(pack_ref, width)
            norms_ref[...] = jnp.zeros_like(norms_ref)
            if has_below:
                for store in stores:
                    store[...] = jnp.zeros_like(store)

        lane = lanes((seq, LANES))
        gy = grad_ref[...].astype(F32)
        columns = [pcol_ref[:, 0:1], pcol_ref[:, 1:2]]
        gn2 = None
        for j in range(local):
            term = nn(pick_rows(columns, span, j * span), gbuf_refs[j][...])
            gn2 = term if gn2 is None else gn2 + term
        hat2, inv2 = normalise(h_ref[...])
        gain2 = norm_ref[33:34, :]
        n2 = (hat2 * gain2 + norm_ref[35:36, :]).astype(BF)
        n2_ref[...] = n2
        router = pack_ref[:, 4 * width : 4 * width + LANES]
        logits = jnp.where(lane < 32, nn(n2, router), NEG)
        weights = jnp.exp(logits - jnp.max(logits, -1, keepdims=True))
        probs = weights / jnp.sum(weights, -1, keepdims=True)
        gr = jnp.zeros_like(probs)
        for k in range(2):
            if has_gg:
                gg = 0.0
                for j in range(local):
                    hit = lanes((seq, span)) == columns[k] - j * span
                    gg = gg + jnp.sum(jnp.where(hit, gg_ref[j : j + 1, :], 0.0), -1, keepdims=True)
            else:
                gg = jnp.sum(gy * pick_refs[k][...].astype(F32), -1, keepdims=True)
            gg = jnp.where(columns[k] >= 0, gg, 0.0)
            gr = gr + jnp.where(lane == routes_ref[:, k : k + 1], gg, 0.0)
        glog = (probs * (gr - jnp.sum(probs * gr, -1, keepdims=True))).astype(BF)
        glog_ref[...] = glog
        gn2 = gn2 + nt(glog, jnp.where(lanes((width, LANES)) < 32, router, jnp.zeros_like(router)))
        pulled, ggain2, gshift2 = norm_pull(gn2, hat2, inv2, gain2)
        gh = gy + pulled
        gbr = gh.astype(BF)
        gbr_ref[...] = gbr
        ga_ref[...] = nt(gbr, pack_ref[:, 3 * width : 4 * width]).astype(BF)
        scale = HEAD ** (-0.5)
        for pair in range(HEADS // 2):
            lo = pair * LANES
            q = qkv_ref[:, lo : lo + LANES]
            k = qkv_ref[:, width + lo : width + lo + LANES]
            v = qkv_ref[:, 2 * width + lo : 2 * width + lo + LANES]
            ga = ga_ref[:, lo : lo + LANES]
            gq, gk, gv = None, None, None
            for half in range(2):
                mine = (lane < HEAD) if half == 0 else (lane >= HEAD)
                zero = jnp.zeros_like(q)
                qm, km, gam = jnp.where(mine, q, zero), jnp.where(mine, k, zero), jnp.where(mine, ga, zero)
                scores = nt(k, qm) * scale
                p = jnp.exp(scores - lse_ref[2 * pair + half : 2 * pair + half + 1, :])
                gp = nt(v, gam)
                gs = (p * (gp - jnp.sum(p * gp, 0, keepdims=True))).astype(BF)
                tv = nn(p.astype(BF), gam)
                tk = nn(gs, qm)
                tq = tn(gs, km)
                gq = tq if gq is None else gq + tq
                gk = tk if gk is None else gk + tk
                gv = tv if gv is None else gv + tv
            gqkv_ref[:, lo : lo + LANES] = (gq * scale).astype(BF)
            gqkv_ref[:, width + lo : width + lo + LANES] = (gk * scale).astype(BF)
            gqkv_ref[:, 2 * width + lo : 2 * width + lo + LANES] = gv.astype(BF)
        gn1 = nt(gqkv_ref[:, 0:width], pack_ref[:, 0:width])
        for c in range(1, 3):
            gn1 = gn1 + nt(gqkv_ref[:, c * width : (c + 1) * width], pack_ref[:, c * width : (c + 1) * width])
        hat1, inv1 = normalise(x_ref[...].astype(F32))
        gain1 = norm_ref[32:33, :]
        n1_ref[...] = (hat1 * gain1 + norm_ref[34:35, :]).astype(BF)
        pulled, ggain1, gshift1 = norm_pull(gn1, hat1, inv1, gain1)
        gx = gh + pulled
        gx_ref[...] = gx
        for r, row in enumerate((ggain1, ggain2, gshift1, gshift2)):
            norms_ref[r : r + 1, :] += row
        if has_below:
            at_row = pl.multiple_of(i * SEQ_PAD, SEQ_PAD)
            for k in range(2):
                stores[k][pl.ds(at_row, seq), :] = (below_gate_ref[:, k : k + 1] * gx).astype(BF)

            @pl.when(i == images - 1)
            def _():
                for j in range(local):
                    geo_refs[j][...] = (
                        nn(place_rows([below_prow_ref[0:1, :]], span, j * span), stores[0][...])
                        + nn(place_rows([below_prow_ref[1:2, :]], span, j * span), stores[1][...])
                    ).astype(BF)

    tokens = images * seq
    flops = 2 * tokens * width * (4 * width + 256) + 10 * HEADS * tokens * 256 * 128
    flops += 2 * (1 + 2 * has_below) * local * span * tokens * width
    results = pl.pallas_call(
        body,
        grid=(images,),
        in_specs=specs,
        out_specs=ospecs,
        out_shape=shapes,
        scratch_shapes=scratch,
        compiler_params=params(),
        cost_estimate=cost(2 * flops, 30 * tokens * width, HEADS * tokens * seq),
        name="block_backward",
    )(*inputs)
    named = dict(zip(("gx", "gbr", "gqkv", "n1", "n2", "glog", "norms"), results[:7]))
    return named, results[7:]


def dense_grads(named, attended):
    images, seq, width = attended.shape
    total = 4 * width + LANES
    step = 256

    def body(n1_ref, a_ref, n2_ref, gqkv_ref, gbr_ref, glog_ref, norms_ref, out_ref, rows, flip, wide):
        def load(ref, store, columns):
            store[...] = jnp.zeros_like(store)
            for i in range(images):
                store[i * SEQ_PAD : i * SEQ_PAD + seq, 0:columns] = ref[i]

        load(n1_ref, rows, width)
        flip[...] = jnp.transpose(rows[...])
        load(gqkv_ref, wide, 3 * width)
        for c in range(3 * width // step):
            out_ref[:, c * step : (c + 1) * step] = nn(flip[...], wide[:, c * step : (c + 1) * step]).astype(BF)
        load(a_ref, rows, width)
        flip[...] = jnp.transpose(rows[...])
        load(gbr_ref, wide, width)
        for c in range(width // step):
            at = 3 * width + c * step
            out_ref[:, at : at + step] = nn(flip[...], wide[:, c * step : (c + 1) * step]).astype(BF)
        load(n2_ref, rows, width)
        flip[...] = jnp.transpose(rows[...])
        load(glog_ref, wide, LANES)
        tail = nn(flip[...], wide[:, 0:LANES])
        norms = jnp.transpose(
            jnp.concatenate([jnp.zeros((32, width), F32), norms_ref[...], jnp.zeros((LANES - 40, width), F32)], 0)
        )
        out_ref[:, 4 * width :] = (tail + norms).astype(BF)

    arrays = [named["n1"], attended, named["n2"], named["gqkv"], named["gbr"], named["glog"], named["norms"]]
    tokens = images * seq
    return pl.pallas_call(
        body,
        grid=(1,),
        in_specs=[fixed(a) for a in arrays],
        out_specs=resident((width, total), lambda i: (0, 0)),
        out_shape=jax.ShapeDtypeStruct((width, total), BF),
        scratch_shapes=[
            pltpu.VMEM((images * SEQ_PAD, width), BF),
            pltpu.VMEM((width, images * SEQ_PAD), BF),
            pltpu.VMEM((images * SEQ_PAD, 3 * width), BF),
        ],
        compiler_params=params(),
        cost_estimate=cost(2 * tokens * width * total, 16 * tokens * width, 0),
        name="dense_grads",
    )(*arrays)


def ffn_forward(layer, j, xs, win, wdown):
    ny = len(xs)
    rows, width = xs[0].shape
    fs = win[0].shape[3]
    tile = min(256, rows)

    def body(*refs):
        xr, wi, wd, outs = refs[:ny], refs[ny : ny + 2], refs[ny + 2 : ny + 4], refs[ny + 4 :]
        for y in range(ny):
            total = None
            for s in range(2):
                hid = gelu(nn(xr[y][...], wi[s][...])).astype(BF)
                part = nt(hid, wd[s][...])
                total = part if total is None else total + part
            outs[y][...] = total.astype(outs[y].dtype)

    wspec = resident((None, None, width, fs), lambda t: (layer, j, 0, 0))
    rspec = pl.BlockSpec((tile, width), lambda t: (t, 0))
    return pl.pallas_call(
        body,
        grid=(rows // tile,),
        in_specs=[rspec] * ny + [wspec] * 4,
        out_specs=[rspec] * ny,
        out_shape=[jax.ShapeDtypeStruct((rows, width), F32 if y == 0 else BF) for y in range(ny)],
        compiler_params=params(),
        cost_estimate=cost(
            2 * 8 * ny * rows * width * fs, 8 * width * fs + 4 * ny * rows * width, 2 * ny * rows * fs
        ),
        name="ffn_forward",
    )(*xs, *win, *wdown)


def ffn_backward(layer, j, xs, gs, win, wdown, gates=None):
    ny = len(xs)
    rows, width = xs[0].shape
    fs = win[0].shape[3]
    fused = gates is not None

    def body(*refs):
        refs = list(refs)

        def take(n):
            taken = refs[:n]
            del refs[:n]
            return taken

        xr, gr, wi, wd = take(ny), take(ny), take(2), take(2)
        tr = take(ny) if fused else None
        gx, outs = take(ny), take(2)
        eo, gg = (take(ny), take(ny)) if fused else (None, None)
        acc = refs[0]
        for y in range(ny):
            x, g = xr[y][...], gr[y][...]
            gated = g
            if fused:
                gate = jnp.transpose(jnp.broadcast_to(tr[y][...], (8, rows)))[:, 0:1]
                gated = (gate * g.astype(F32)).astype(BF)
            back, part, dot = None, None, None
            for s in range(2):
                w1, w2 = wi[s][...], wd[s][...]
                hid, slope = gelu_both(nn(x, w1))
                hid = hid.astype(BF)
                ghid = nn(g, w2)
                if fused:
                    term = jnp.sum(hid.astype(F32) * ghid, -1, keepdims=True)
                    dot = term if dot is None else dot + term
                    term = nt(hid, w2)
                    part = term if part is None else part + term
                    ghid = gate * ghid
                gpre = (ghid * slope).astype(BF)
                term = nt(gpre, w1)
                back = term if back is None else back + term
                for n, grad in enumerate((tn(x, gpre), tn(gated, hid))):
                    if s == 0:
                        outs[0][n] = grad if y == 0 else outs[0][n] + grad
                    elif y < ny - 1:
                        acc[n] = grad if y == 0 else acc[n] + grad
                    else:
                        outs[1][n] = (grad if y == 0 else acc[n] + grad).astype(BF)
            gx[y][...] = back.astype(gx[y].dtype)
            if fused:
                eo[y][...] = part.astype(eo[y].dtype)
                gg[y][...] = jnp.transpose(jnp.broadcast_to(dot, (rows, LANES)))[0:1, :]

    wspec = resident((None, None, width, fs), lambda c: (layer, j, 0, 0))
    rspec = resident((rows, width), lambda c: (0, 0))
    lspec = resident((1, rows), lambda c: (0, 0))
    gspec = resident((2, width, fs), lambda c: (0, 0, 0))
    parts = [jax.ShapeDtypeStruct((rows, width), F32 if y == 0 else BF) for y in range(ny)]
    shapes = parts + [jax.ShapeDtypeStruct((2, width, fs), F32), jax.ShapeDtypeStruct((2, width, fs), BF)]
    if fused:
        shapes += parts + [jax.ShapeDtypeStruct((1, rows), F32)] * ny
    return pl.pallas_call(
        body,
        grid=(1,),
        in_specs=[rspec] * (2 * ny) + [wspec] * 4 + [lspec] * (ny if fused else 0),
        out_specs=[rspec] * ny + [gspec] * 2 + ([rspec] * ny + [lspec] * ny if fused else []),
        out_shape=shapes,
        scratch_shapes=[pltpu.VMEM((2, width, fs), F32)],
        compiler_params=params(),
        cost_estimate=cost(
            2 * (24 if fused else 20) * ny * rows * width * fs, 20 * width * fs + 8 * ny * rows * width, 2 * ny * rows * fs
        ),
        name="ffn_backward",
    )(*xs, *gs, *win, *wdown, *(gates if fused else ()))


def store_grads(layer, j, local, own, received, buffers):
    _, width, fs = own.shape
    tile = width // 4

    def body(own_ref, recv_ref, *refs):
        outs = refs[-2:]
        for n in range(2):
            outs[n][...] = own_ref[n] + recv_ref[n].astype(F32)

    pspec = pl.BlockSpec((2, tile, fs), lambda t: (0, t, 0))
    ospec = pl.BlockSpec((None, None, tile, fs), lambda t: (layer, j, t, 0))
    full = jax.ShapeDtypeStruct((2, local, width, fs), F32)
    extra = [] if buffers is None else list(buffers)
    return pl.pallas_call(
        body,
        grid=(4,),
        in_specs=[pspec, pspec] + [pl.BlockSpec(memory_space=pl.ANY)] * len(extra),
        out_specs=[ospec, ospec],
        out_shape=[full, full],
        input_output_aliases={} if buffers is None else {2: 0, 3: 1},
        compiler_params=params(),
        cost_estimate=cost(2 * width * fs, 20 * width * fs, 0),
        name="store_grads",
    )(own, received, *extra)


def rows_shift(count, shift):
    ys = count // 2
    return [(y * 2 + c, ((y + shift) % ys) * 2 + c) for y in range(ys) for c in range(2)]


def spread_rows(mine, count):
    return [mine] + [lax.ppermute(mine, "fsdp", rows_shift(count, s)) for s in range(1, count // 2)]


def return_parts(parts, count):
    return [parts[0]] + [
        lax.ppermute(parts[s], "fsdp", rows_shift(count, -s)) for s in range(1, count // 2)
    ]


def add_parts(parts):
    total = parts[0]
    for part in parts[1:]:
        total = total + part.astype(F32)
    return total.astype(BF)


def step(live, works):
    fresh = dict(live)
    for work in works:
        fresh.update(work(live))
    return lax.optimization_barrier(fresh)


def staged(live, count, stages, extras, pending=()):
    total = count + len(stages) - 1
    waiting = [(0, value) for value in pending]
    for t in range(total):
        works = [
            lambda now, stage=stage, j=t - s: stage(now, j)
            for s, stage in enumerate(stages)
            if 0 <= t - s < count
        ]
        for at, until, work in extras:
            if t == min(at, total - 1):
                if min(until, total - 1) <= t:
                    works.append(work)
                else:
                    waiting.append((until, work(live)))
        for until, value in waiting:
            if t == min(until, total - 1):
                works.append(lambda now, value=value: value)
        live = step(live, works)
    return live


def exchange(rows):
    return lax.all_to_all(rows, "expert", split_axis=0, concat_axis=0, tiled=True)


def swap_cores(array, count):
    return lax.ppermute(array, "fsdp", [(f, f ^ 1) for f in range(count)])


def shards(tokens_in, routes, valid, qkv_weight, out_weight, router_weight, norm_gain, norm_shift,
           expert_in, expert_down, cotangent):
    owners = lax.axis_size("expert")
    count = lax.axis_size("fsdp")
    local = expert_in.shape[1]
    layers = routes.shape[0]
    tokens, width = tokens_in.shape
    images = tokens // SEQ
    span = owners * CAP
    slots = (local, span)
    experts = router_weight.shape[2]

    packs = []
    for l in range(layers):
        shard = qkv_weight.shape[1]
        pieces = [qkv_weight[l], out_weight[l], router_weight[l], norm_gain[l].T, norm_shift[l].T]
        pieces.append(jnp.zeros((shard, LANES - experts - 4), BF))
        packs.append(jnp.concatenate(pieces, 1))
    win = (expert_in, swap_cores(expert_in, count))
    wdown = (expert_down, swap_cores(expert_down, count))

    def cut(array):
        return array.reshape(array.shape[:-2] + (images, SEQ, array.shape[-1]))

    route_cols = cut(routes)
    pcol, prow = route_places(route_cols, cut(valid), owners, local)
    cot = cut(cotangent)
    top = layers - 1

    def pick(record, *names):
        return {n: record[n] for n in names}

    def swap_y(now, name, out):
        return {out: spread_rows(now[name], count)}

    def send(now, name, out):
        return {out: exchange(now[name])}

    sent = dispatch(cot, prow[top], slots)
    live = {f"c{j}": rows for j, rows in enumerate(sent)}
    live = step(
        live,
        [
            lambda now: {"pack0": lax.all_gather(packs[0], "fsdp", axis=0, tiled=True)},
            lambda now: send(now, "c0", "g0"),
        ],
    )

    def enter(l):
        def work(now):
            previous = None
            stream = cut(tokens_in)
            if l > 0:
                previous = ([now[f"e{l - 1}_{j}"] for j in range(local)], pcol[l - 1], now[f"gate{l - 1}"])
                stream = now[f"h{l - 1}"]
            pack = now[f"pack{l}"]
            record, sent, rows = block_forward(
                stream, pack, route_cols[l], pcol[l], prow[l], previous, l == top, slots
            )
            out = {f"{name}{l}": value for name, value in record.items() if name != "picks"}
            if l > 0:
                out[f"picks{l - 1}"] = record["picks"]
            for j in range(local):
                out[f"s{l}_{j}"] = sent[j]
            if l == top:
                out["grow"] = rows[0][0:1, :]
            return out

        return work

    def come(l):
        return lambda now, j: send(now, f"s{l}_{j}", f"a{l}_{j}")

    def widen(l):
        return lambda now, j: swap_y(now, f"a{l}_{j}", f"x{l}_{j}")

    def back_y(now, name, out):
        return {out: add_parts(return_parts(now[name], count))}

    early = [j for j in range(local)]
    live["shards"] = packs[1:]
    before = live["shards"]
    live = step(
        live,
        [enter(0), lambda now: swap_y(now, "g0", "gy0")] + ([lambda now: send(now, "c1", "g1")] if local > 1 else []),
    )
    pending = [{f"pack{l + 1}": lax.all_gather(p, "fsdp", axis=0, tiled=True)} for l, p in enumerate(before)]
    for l in range(top):
        live = staged(
            live,
            local,
            [
                come(l),
                widen(l),
                lambda now, j, l=l: {f"p{l}_{j}": ffn_forward(l, j, now[f"x{l}_{j}"], win, wdown)},
                lambda now, j, l=l: back_y(now, f"p{l}_{j}", f"r{l}_{j}"),
                lambda now, j, l=l: send(now, f"r{l}_{j}", f"e{l}_{j}"),
            ],
            [],
            pending if l == 0 else (),
        )
        works = [enter(l + 1)]
        if l + 1 == top:
            works += [lambda now, j=j: send(now, f"c{j}", f"g{j}") for j in early[2:3]]
            works += [lambda now, j=j: swap_y(now, f"g{j}", f"gy{j}") for j in early[1:2]]
        live = step(live, works)

    def send_gates(now):
        rows = now["grow"].reshape(local, owners, CAP).transpose(1, 0, 2).reshape(owners, local * CAP)
        return {"ga": lax.all_to_all(rows, "expert", split_axis=0, concat_axis=0, tiled=True)}

    def widen_gates(now):
        rows = now["ga"].reshape(owners, local, CAP).transpose(1, 0, 2).reshape(local, span)
        return {"gates": spread_rows(rows, count)}

    def fused_rows(now, j):
        gates = [rows[j : j + 1] for rows in now["gates"]]
        ys = count // 2
        results = ffn_backward(top, j, now[f"x{top}_{j}"], now[f"gy{j}"], win, wdown, gates)
        return {
            f"q{top}_{j}": results[:ys],
            f"own{top}_{j}": results[ys],
            f"oth{top}_{j}": results[ys + 1],
            f"f{j}": results[ys + 2 : 2 * ys + 2],
            f"gg{j}": results[2 * ys + 2 :],
        }

    def plain_rows(l):
        def work(now, j):
            ys = count // 2
            results = ffn_backward(l, j, now[f"x{l}_{j}"], now[f"gy{l}_{j}"], win, wdown)
            return {f"q{l}_{j}": results[:ys], f"own{l}_{j}": results[ys], f"oth{l}_{j}": results[ys + 1]}

        return work

    def return_rows(l):
        def work(now, j):
            out = back_y(now, f"q{l}_{j}", f"t{l}_{j}")
            out[f"oth{l}_{j}"] = swap_cores(now[f"oth{l}_{j}"], count)
            return out

        return work

    def leave(l):
        return lambda now, j: send(now, f"t{l}_{j}", f"b{l}_{j}")

    def return_gg(now):
        rows = [jnp.concatenate([now[f"gg{j}"][y] for j in range(local)], 0) for y in range(count // 2)]
        parts = return_parts(rows, count)
        total = parts[0]
        for part in parts[1:]:
            total = total + part
        return {"ggr": total}

    def send_gg(now):
        rows = now["ggr"].reshape(local, owners, CAP).transpose(1, 0, 2).reshape(owners, local * CAP)
        rows = lax.all_to_all(rows, "expert", split_axis=0, concat_axis=0, tiled=True)
        return {"ggs": rows.reshape(owners, local, CAP).transpose(1, 0, 2).reshape(local, span)}

    def keep(l, js):
        def work(now):
            buffers = now.get("buffers")
            for j in js:
                buffers = store_grads(l, j, local, now[f"own{l}_{j}"], now[f"oth{l}_{j}"], buffers)
            return {"buffers": buffers}

        return work

    live = staged(
        live,
        local,
        [come(top), widen(top), fused_rows, return_rows(top), leave(top)],
        [(0, 0, send_gates)]
        + [(0, 0, lambda now, j=j: swap_y(now, f"g{j}", f"gy{j}")) for j in early[2:3]]
        + [(0, 0, lambda now, j=j: send(now, f"c{j}", f"g{j}")) for j in early[3:]]
        + [(1, 1, lambda now, j=j: swap_y(now, f"g{j}", f"gy{j}")) for j in early[3:]]
        + [(1, 1, widen_gates), (local + 2, local + 2, return_gg), (local + 3, local + 3, send_gg)],
    )

    def scatter_sum(packed):
        return lax.psum_scatter(packed, "fsdp", scatter_dimension=0, tiled=True)

    def back_block(l):
        def work(now):
            kept = {name: now[f"{name}{l}"] for name in ("x", "h", "qkv", "lse")}
            if l < top:
                kept["picks"] = now[f"picks{l}"]
            below = None if l == 0 else (now[f"gate{l - 1}"], prow[l - 1])
            pack = now[f"pack{l}"]
            named, geo = block_backward(
                cot if l == top else now["grad"], kept, pack, route_cols[l], pcol[l],
                [now[f"b{l}_{j}"] for j in range(local)], now["ggs"] if l == top else None, below, slots
            )
            out = {f"{name}{l}": value for name, value in named.items() if name != "gx"}
            out["grad"] = named["gx"]
            if l > 0:
                for j in range(local):
                    out[f"d{l - 1}_{j}"] = geo[j]
            return out

        return work

    def grads_of(now, l):
        named = {name: now[f"{name}{l}"] for name in ("n1", "n2", "gqkv", "gbr", "glog", "norms")}
        return dense_grads(named, now[f"a{l}"])

    live = step(live, [back_block(top)] + [lambda now, j=j: back_y(now, f"f{j}", f"fr{j}") for j in early[:2]])
    for l in reversed(range(top)):
        extras = [(0, 0, lambda now, l=l: {f"dense{l + 1}": grads_of(now, l + 1)})]
        extras += [(1 + n, 1 + n, keep(l + 1, early[2 * n : 2 * n + 2])) for n in range((local + 1) // 2)]
        extras += [
            (1, 4, lambda now, l=l: {f"share{l + 1}": scatter_sum(now[f"dense{l + 1}"])}),
        ]
        if l == 0:
            for j in early[2:]:
                at = 0 if j == 2 else local + 3
                extras.append((at, at, lambda now, j=j: back_y(now, f"f{j}", f"fr{j}")))
            for j in early[:2]:
                extras.append((3 + j, 3 + j, lambda now, j=j: send(now, f"fr{j}", f"e{top}_{j}")))
        live = staged(
            live,
            local,
            [
                lambda now, j, l=l: send(now, f"d{l}_{j}", f"m{l}_{j}"),
                lambda now, j, l=l: swap_y(now, f"m{l}_{j}", f"gy{l}_{j}"),
                plain_rows(l),
                return_rows(l),
                leave(l),
            ],
            extras,
        )
        live = step(live, [back_block(l)] + [lambda now, j=j: send(now, f"fr{j}", f"e{top}_{j}") for j in early[2:3]])
    live["dense0"] = grads_of(live, 0)
    for j in early[3:]:
        live.update(send(live, f"fr{j}", f"e{top}_{j}"))
    out = combine_last(live[f"h{top}"], [live[f"e{top}_{j}"] for j in range(local)], pcol[top], live[f"gate{top}"])
    live.update(keep(0, early)(live))
    buffers = live["buffers"]
    grad = live["grad"]
    live["share0"] = scatter_sum(live["dense0"])
    dense = [lax.psum(live[f"share{l}"], "expert").astype(F32) for l in range(layers)]

    both = jnp.stack(dense)
    at = 4 * width + experts
    return (
        out.reshape(tokens, width),
        grad.reshape(tokens, width),
        both[:, :, : 3 * width],
        both[:, :, 3 * width : 4 * width],
        both[:, :, 4 * width : at],
        jnp.swapaxes(both[:, :, at : at + 2], 1, 2),
        jnp.swapaxes(both[:, :, at + 2 : at + 4], 1, 2),
        buffers[0],
        buffers[1],
    )


def solution(mesh):
    everyone = ("expert", "fsdp")
    return jax.shard_map(
        shards,
        mesh=mesh,
        in_specs=(
            P(everyone, None),
            P(None, everyone, None),
            P(None, everyone, None),
            P(None, "fsdp", None),
            P(None, "fsdp", None),
            P(None, "fsdp", None),
            P(None, None, "fsdp"),
            P(None, None, "fsdp"),
            P(None, "expert", None, "fsdp"),
            P(None, "expert", None, "fsdp"),
            P(everyone, None),
        ),
        out_specs=(
            P(everyone, None),
            P(everyone, None),
            P(None, "fsdp", None),
            P(None, "fsdp", None),
            P(None, "fsdp", None),
            P(None, None, "fsdp"),
            P(None, None, "fsdp"),
            P(None, "expert", None, "fsdp"),
            P(None, "expert", None, "fsdp"),
        ),
        check_vma=False,
    )
```

```python
import jax
import jax.numpy as jnp
from jax import lax
from jax.experimental import pallas as pl
from jax.experimental.pallas import tpu as pltpu
from jax.sharding import PartitionSpec as P

HEADS = 12
HEAD = 64
SEQ = 197
SEQ_PAD = 256
CAP = 64
LANES = 128
BF = jnp.bfloat16
F32 = jnp.float32
EPS = 1e-06
GELU = 0.7978845608028654
CUBE = 0.044715
VMEM_LIMIT = 56 << 20
NEG = -1e30


def nn(left, right):
    return lax.dot_general(left, right, (((1,), (0,)), ((), ())), preferred_element_type=F32)


def nt(left, right):
    return lax.dot_general(left, right, (((1,), (1,)), ((), ())), preferred_element_type=F32)


def tn(left, right):
    return lax.dot_general(left, right, (((0,), (0,)), ((), ())), preferred_element_type=F32)


def gelu(u):
    return 0.5 * u * (1.0 + jnp.tanh(GELU * (u + CUBE * u * u * u)))


def gelu_both(u):
    square = u * u
    t = jnp.tanh(GELU * u * (1.0 + CUBE * square))
    half = 0.5 * (1.0 + t)
    return u * half, half + 0.5 * u * (1.0 - t * t) * (GELU * (1.0 + 3.0 * CUBE * square))


def normalise(v):
    centred = v - jnp.mean(v, -1, keepdims=True)
    inv = lax.rsqrt(jnp.mean(centred * centred, -1, keepdims=True) + EPS)
    return centred * inv, inv


def norm_pull(grad, hat, inv, gain):
    scaled = grad * gain
    pulled = inv * (
        scaled
        - jnp.mean(scaled, -1, keepdims=True)
        - hat * jnp.mean(scaled * hat, -1, keepdims=True)
    )
    return pulled, jnp.sum(grad * hat, 0, keepdims=True), jnp.sum(grad, 0, keepdims=True)


def resident(shape, index):
    return pl.BlockSpec(shape, index, pipeline_mode=pl.Buffered(1))


def fixed(array):
    zeros = (0,) * array.ndim
    return resident(array.shape, lambda i: zeros)


def per_image(*tail):
    zeros = (0,) * len(tail)
    return pl.BlockSpec((None,) + tail, lambda i: (i,) + zeros)


def cost(flops, byte_count, exps):
    return pl.CostEstimate(
        flops=int(flops), bytes_accessed=int(byte_count), transcendentals=int(exps)
    )


def params():
    return pltpu.CompilerParams(vmem_limit_bytes=VMEM_LIMIT)


def lanes(shape):
    return lax.broadcasted_iota(jnp.int32, shape, 1)


def pick_rows(columns, slots, start):
    hit = lanes((columns[0].shape[0], slots)) == columns[0] - start
    for column in columns[1:]:
        hit = hit | (lanes((column.shape[0], slots)) == column - start)
    return jnp.where(hit, 1.0, 0.0).astype(BF)


def place_rows(rows, slots, start):
    sub = lax.broadcasted_iota(jnp.int32, (slots, rows[0].shape[1]), 0)
    hit = sub == rows[0] - start
    for row in rows[1:]:
        hit = hit | (sub == row - start)
    return jnp.where(hit, 1.0, 0.0).astype(BF)


def norm_rows(pack_ref, width):
    tail = pack_ref[:, 4 * width :].astype(F32)
    return jnp.transpose(tail)


def block_forward(stream, pack, routes, pcol, prow, previous, want_rows, slots):
    images, seq, width = stream.shape
    chunks = 4 * width
    local = slots[0]
    span = slots[1]
    has_prev = previous is not None
    inputs = [stream, pack, routes, pcol, prow]
    specs = [per_image(seq, width), fixed(pack), per_image(seq, 2), per_image(seq, 2), fixed(prow)]
    if has_prev:
        inputs += list(previous[0]) + [previous[1], previous[2]]
        specs += [fixed(a) for a in previous[0]] + [per_image(seq, 2), per_image(seq, 2)]
    shapes, ospecs = [], []

    def out(shape, dtype, spec):
        shapes.append(jax.ShapeDtypeStruct(shape, dtype))
        ospecs.append(spec)

    out((images, seq, 3 * width), BF, per_image(seq, 3 * width))
    out((images, 16, seq), F32, per_image(16, seq))
    out((images, seq, width), BF, per_image(seq, width))
    out((images, seq, width), F32, per_image(seq, width))
    out((images, seq, 2), F32, per_image(seq, 2))
    if has_prev:
        out((images, seq, width), F32, per_image(seq, width))
        out((images, seq, width), BF, per_image(seq, width))
        out((images, seq, width), BF, per_image(seq, width))
    for _ in range(local):
        out((span, width), BF, resident((span, width), lambda i: (0, 0)))
    if want_rows:
        out((8, local * span), F32, resident((8, local * span), lambda i: (0, 0)))
    scratch = [pltpu.VMEM((images * SEQ_PAD, width), BF), pltpu.VMEM((LANES, width), F32)]

    def body(*refs):
        refs = list(refs)
        x_ref, pack_ref, routes_ref, pcol_ref, prow_ref = refs[:5]
        at = 5
        if has_prev:
            eo_refs = refs[at : at + local]
            old_pcol_ref, old_gate_ref = refs[at + local : at + local + 2]
            at += local + 2
        qkv_ref, lse_ref, a_ref, h_ref, gate_ref = refs[at : at + 5]
        at += 5
        if has_prev:
            xs_ref, pick0_ref, pick1_ref = refs[at : at + 3]
            at += 3
        disp_refs = refs[at : at + local]
        at += local
        if want_rows:
            grow_ref = refs[at]
        store, norm_ref = refs[-2:]
        i = pl.program_id(0)

        @pl.when(i == 0)
        def _():
            norm_ref[...] = norm_rows(pack_ref, width)
            store[...] = jnp.zeros_like(store)
            if want_rows:
                grow_ref[...] = jnp.zeros_like(grow_ref)

        x = x_ref[...].astype(F32)
        if has_prev:
            for k, pick_ref in enumerate((pick0_ref, pick1_ref)):
                picked = None
                for j in range(local):
                    hot = pick_rows([old_pcol_ref[:, k : k + 1]], span, j * span)
                    term = nn(hot, eo_refs[j][...])
                    picked = term if picked is None else picked + term
                pick_ref[...] = picked.astype(BF)
                x = x + old_gate_ref[:, k : k + 1] * picked
            xs_ref[...] = x
        hat, _ = normalise(x)
        n1 = (hat * norm_ref[32:33, :] + norm_ref[34:35, :]).astype(BF)
        for c in range(3):
            qkv_ref[:, c * width : (c + 1) * width] = nn(
                n1, pack_ref[:, c * width : (c + 1) * width]
            ).astype(BF)
        lane = lanes((seq, LANES))
        lse_ref[...] = jnp.zeros_like(lse_ref)
        for pair in range(HEADS // 2):
            lo = pair * LANES
            q = qkv_ref[:, lo : lo + LANES]
            k = qkv_ref[:, width + lo : width + lo + LANES]
            v = qkv_ref[:, 2 * width + lo : 2 * width + lo + LANES]
            parts = []
            for half in range(2):
                mine = (lane < HEAD) if half == 0 else (lane >= HEAD)
                scores = nt(k, jnp.where(mine, q, jnp.zeros_like(q))) * HEAD ** (-0.5)
                top = jnp.max(scores, 0, keepdims=True)
                weights = jnp.exp(scores - top)
                total = jnp.sum(weights, 0, keepdims=True)
                lse_ref[2 * pair + half : 2 * pair + half + 1, :] = top + jnp.log(total)
                probs = (weights * (1.0 / total)).astype(BF)
                parts.append(tn(probs, v))
            a_ref[:, lo : lo + LANES] = jnp.where(lane < HEAD, parts[0], parts[1]).astype(BF)
        h = x + nn(a_ref[...], pack_ref[:, 3 * width : 4 * width])
        h_ref[...] = h
        hat, _ = normalise(h)
        n2 = (hat * norm_ref[33:34, :] + norm_ref[35:36, :]).astype(BF)
        logits = nn(n2, pack_ref[:, chunks : chunks + LANES])
        logits = jnp.where(lane < 32, logits, NEG)
        weights = jnp.exp(logits - jnp.max(logits, -1, keepdims=True))
        probs = weights / jnp.sum(weights, -1, keepdims=True)
        gates = []
        for k in range(2):
            chosen = jnp.where(lane == routes_ref[:, k : k + 1], probs, 0.0)
            kept = jnp.where(pcol_ref[:, k : k + 1] >= 0, 1.0, 0.0)
            gates.append(jnp.sum(chosen, -1, keepdims=True) * kept)
            gate_ref[:, k : k + 1] = gates[k]
        store[pl.ds(pl.multiple_of(i * SEQ_PAD, SEQ_PAD), seq), :] = n2
        if want_rows:
            where = lanes((seq, local * span))
            spread = [jnp.where(where == pcol_ref[:, k : k + 1], gates[k], 0.0) for k in range(2)]
            grow_ref[0:1, :] += jnp.sum(spread[0] + spread[1], 0, keepdims=True)

        @pl.when(i == images - 1)
        def _():
            rows = [prow_ref[0:1, :], prow_ref[1:2, :]]
            for j in range(local):
                disp_refs[j][...] = nn(place_rows(rows, span, j * span), store[...]).astype(BF)

    tokens = images * seq
    flops = 2 * tokens * width * (4 * width + 128) + 4 * HEADS * tokens * 256 * 128
    flops += 2 * (1 + 2 * has_prev) * local * span * tokens * width
    results = pl.pallas_call(
        body,
        grid=(images,),
        in_specs=specs,
        out_specs=ospecs,
        out_shape=shapes,
        scratch_shapes=scratch,
        compiler_params=params(),
        cost_estimate=cost(2 * flops, 20 * tokens * width, HEADS * tokens * seq),
        name="block_forward",
    )(*inputs)
    kept = dict(zip(("qkv", "lse", "a", "h", "gate"), results[:5]))
    rest = results[5:]
    kept["x"] = stream
    if has_prev:
        kept["x"] = rest[0]
        kept["picks"] = (rest[1], rest[2])
        rest = rest[3:]
    return kept, rest[:local], rest[local:]


def dispatch(rows, prow, slots, groups):
    images, seq, width = rows.shape
    span = slots[1]
    owners = span // CAP

    def body(rows_ref, prow_ref, *refs):
        outs, store = refs[:-1], refs[-1]
        store[...] = jnp.zeros_like(store)
        for i in range(images):
            store[i * SEQ_PAD : i * SEQ_PAD + seq, :] = rows_ref[i]
        for out, group in zip(outs, groups):
            for n, j in enumerate(group):
                hot = place_rows([prow_ref[0:1, :], prow_ref[1:2, :]], span, j * span)
                out[:, n] = nn(hot, store[...]).astype(BF).reshape(owners, CAP, width)

    shapes = [(owners, len(group), CAP, width) for group in groups]
    return pl.pallas_call(
        body,
        grid=(1,),
        in_specs=[fixed(rows), fixed(prow)],
        out_specs=[resident(shape, lambda i: (0, 0, 0, 0)) for shape in shapes],
        out_shape=[jax.ShapeDtypeStruct(shape, BF) for shape in shapes],
        scratch_shapes=[pltpu.VMEM((images * SEQ_PAD, width), BF)],
        compiler_params=params(),
        cost_estimate=cost(4 * slots[0] * span * images * seq * width, 8 * slots[0] * span * width, 0),
        name="dispatch",
    )(rows, prow)


def route_places(routes, valid, owners, local):
    layers, images, seq, _ = routes.shape

    def body(routes_ref, valid_ref, pcol_ref, prow_ref):
        prow_ref[...] = jnp.full(prow_ref.shape, -1, jnp.int32)
        lane = lanes((seq, LANES))
        below = lax.broadcasted_iota(jnp.int32, (seq, seq), 0) > lanes((seq, seq))
        below = jnp.where(below, 1.0, 0.0).astype(BF)
        base = jnp.zeros((1, LANES), F32)
        for i in range(images):
            hot = [jnp.where(lane == routes_ref[i, :, k : k + 1], 1.0, 0.0) for k in range(2)]
            both = hot[0] + hot[1]
            earlier = nn(below, both.astype(BF)) + base
            base = base + jnp.sum(both, 0, keepdims=True)
            columns = jnp.full((seq, LANES), -1.0, F32)
            for k in range(2):
                slot = jnp.sum(hot[k] * earlier, -1, keepdims=True)
                expert = routes_ref[i, :, k : k + 1]
                owner = expert // local
                start = ((expert - owner * local) * owners + owner) * CAP
                place = jnp.where(valid_ref[i, :, k : k + 1] > 0, start.astype(F32) + slot, -1.0)
                pcol_ref[i, :, k : k + 1] = place.astype(jnp.int32)
                columns = jnp.where(lane == k, place, columns)
            padded = jnp.concatenate([columns, jnp.full((SEQ_PAD - seq, LANES), -1.0, F32)], 0)
            prow_ref[:, i * SEQ_PAD : (i + 1) * SEQ_PAD] = jnp.transpose(padded)[0:8, :].astype(jnp.int32)

    spec = pl.BlockSpec((None, images, seq, 2), lambda l: (l, 0, 0, 0))
    return pl.pallas_call(
        body,
        grid=(layers,),
        in_specs=[spec, spec],
        out_specs=[spec, pl.BlockSpec((None, 8, images * SEQ_PAD), lambda l: (l, 0, 0))],
        out_shape=[
            jax.ShapeDtypeStruct((layers, images, seq, 2), jnp.int32),
            jax.ShapeDtypeStruct((layers, 8, images * SEQ_PAD), jnp.int32),
        ],
        compiler_params=params(),
        cost_estimate=cost(2 * layers * images * seq * seq * LANES, 1 << 20, 0),
        name="route_places",
    )(routes, valid)


def combine_last(h, expert_rows, pcol, gate):
    images, seq, width = h.shape
    owners = expert_rows[0].shape[0]
    span = owners * CAP
    where = [(a, n) for a, array in enumerate(expert_rows) for n in range(array.shape[1])]
    local = len(where)

    def body(h_ref, pcol_ref, gate_ref, *refs):
        eo_refs, out_ref = refs[:-1], refs[-1]
        x = h_ref[...]
        for k in range(2):
            picked = None
            for j in range(local):
                rows = eo_refs[where[j][0]][:, where[j][1]].reshape(span, width)
                term = nn(pick_rows([pcol_ref[:, k : k + 1]], span, j * span), rows)
                picked = term if picked is None else picked + term
            x = x + gate_ref[:, k : k + 1] * picked
        out_ref[...] = x.astype(BF)

    return pl.pallas_call(
        body,
        grid=(images,),
        in_specs=[per_image(seq, width), per_image(seq, 2), per_image(seq, 2)]
        + [fixed(a) for a in expert_rows],
        out_specs=per_image(seq, width),
        out_shape=jax.ShapeDtypeStruct((images, seq, width), BF),
        compiler_params=params(),
        cost_estimate=cost(8 * local * span * images * seq * width, 20 * images * seq * width, 0),
        name="combine_last",
    )(h, pcol, gate, *expert_rows)


def block_backward(grad, kept, pack, routes, pcol, expert_grads, gate_grads, below, slots):
    images, seq, width = grad.shape
    local, span = slots
    has_below = below is not None
    has_gg = gate_grads is not None
    row3, row2 = per_image(seq, width), per_image(seq, 2)
    inputs = [grad, kept["x"], kept["h"], kept["qkv"], kept["lse"], pack, routes, pcol]
    specs = [row3, row3, row3, per_image(seq, 3 * width), per_image(16, seq), fixed(pack), row2, row2]
    inputs += list(expert_grads)
    specs += [fixed(a) for a in expert_grads]
    if has_gg:
        inputs.append(gate_grads)
        specs.append(fixed(gate_grads))
    else:
        inputs += list(kept["picks"])
        specs += [row3, row3]
    if has_below:
        inputs += [below[0], below[1]]
        specs += [row2, fixed(below[1])]
    shapes, ospecs = [], []

    def out(shape, dtype, spec):
        shapes.append(jax.ShapeDtypeStruct(shape, dtype))
        ospecs.append(spec)

    out((images, seq, width), F32, row3)
    out((images, seq, width), BF, row3)
    out((images, seq, 3 * width), BF, per_image(seq, 3 * width))
    out((images, seq, width), BF, row3)
    out((images, seq, width), BF, row3)
    out((images, seq, LANES), BF, per_image(seq, LANES))
    out((8, width), F32, resident((8, width), lambda i: (0, 0)))
    if has_below:
        for _ in range(local):
            out((span, width), BF, resident((span, width), lambda i: (0, 0)))
    scratch = [pltpu.VMEM((images * SEQ_PAD, width), BF)] * (2 if has_below else 0)
    scratch += [pltpu.VMEM((LANES, width), F32), pltpu.VMEM((seq, width), BF)]

    def body(*refs):
        refs = list(refs)
        grad_ref, x_ref, h_ref, qkv_ref, lse_ref, pack_ref, routes_ref, pcol_ref = refs[:8]
        at = 8
        gbuf_refs = refs[at : at + local]
        at += local
        if has_gg:
            gg_ref = refs[at]
            at += 1
        else:
            pick_refs = refs[at : at + 2]
            at += 2
        if has_below:
            below_gate_ref, below_prow_ref = refs[at : at + 2]
            at += 2
        gx_ref, gbr_ref, gqkv_ref, n1_ref, n2_ref, glog_ref, norms_ref = refs[at : at + 7]
        at += 7
        if has_below:
            geo_refs = refs[at : at + local]
            at += local
            stores = refs[at : at + 2]
        norm_ref, ga_ref = refs[-2:]
        i = pl.program_id(0)

        @pl.when(i == 0)
        def _():
            norm_ref[...] = norm_rows(pack_ref, width)
            norms_ref[...] = jnp.zeros_like(norms_ref)
            if has_below:
                for store in stores:
                    store[...] = jnp.zeros_like(store)

        lane = lanes((seq, LANES))
        gy = grad_ref[...].astype(F32)
        columns = [pcol_ref[:, 0:1], pcol_ref[:, 1:2]]
        gn2 = None
        for j in range(local):
            term = nn(pick_rows(columns, span, j * span), gbuf_refs[j][...])
            gn2 = term if gn2 is None else gn2 + term
        hat2, inv2 = normalise(h_ref[...])
        gain2 = norm_ref[33:34, :]
        n2 = (hat2 * gain2 + norm_ref[35:36, :]).astype(BF)
        n2_ref[...] = n2
        router = pack_ref[:, 4 * width : 4 * width + LANES]
        logits = jnp.where(lane < 32, nn(n2, router), NEG)
        weights = jnp.exp(logits - jnp.max(logits, -1, keepdims=True))
        probs = weights / jnp.sum(weights, -1, keepdims=True)
        gr = jnp.zeros_like(probs)
        for k in range(2):
            if has_gg:
                gg = 0.0
                for j in range(local):
                    hit = lanes((seq, span)) == columns[k] - j * span
                    gg = gg + jnp.sum(jnp.where(hit, gg_ref[j : j + 1, :], 0.0), -1, keepdims=True)
            else:
                gg = jnp.sum(gy * pick_refs[k][...].astype(F32), -1, keepdims=True)
            gg = jnp.where(columns[k] >= 0, gg, 0.0)
            gr = gr + jnp.where(lane == routes_ref[:, k : k + 1], gg, 0.0)
        glog = (probs * (gr - jnp.sum(probs * gr, -1, keepdims=True))).astype(BF)
        glog_ref[...] = glog
        gn2 = gn2 + nt(glog, jnp.where(lanes((width, LANES)) < 32, router, jnp.zeros_like(router)))
        pulled, ggain2, gshift2 = norm_pull(gn2, hat2, inv2, gain2)
        gh = gy + pulled
        gbr = gh.astype(BF)
        gbr_ref[...] = gbr
        ga_ref[...] = nt(gbr, pack_ref[:, 3 * width : 4 * width]).astype(BF)
        scale = HEAD ** (-0.5)
        for pair in range(HEADS // 2):
            lo = pair * LANES
            q = qkv_ref[:, lo : lo + LANES]
            k = qkv_ref[:, width + lo : width + lo + LANES]
            v = qkv_ref[:, 2 * width + lo : 2 * width + lo + LANES]
            ga = ga_ref[:, lo : lo + LANES]
            gq, gk, gv = None, None, None
            for half in range(2):
                mine = (lane < HEAD) if half == 0 else (lane >= HEAD)
                zero = jnp.zeros_like(q)
                qm, km, gam = jnp.where(mine, q, zero), jnp.where(mine, k, zero), jnp.where(mine, ga, zero)
                scores = nt(k, qm) * scale
                p = jnp.exp(scores - lse_ref[2 * pair + half : 2 * pair + half + 1, :])
                gp = nt(v, gam)
                gs = (p * (gp - jnp.sum(p * gp, 0, keepdims=True))).astype(BF)
                tv = nn(p.astype(BF), gam)
                tk = nn(gs, qm)
                tq = tn(gs, km)
                gq = tq if gq is None else gq + tq
                gk = tk if gk is None else gk + tk
                gv = tv if gv is None else gv + tv
            gqkv_ref[:, lo : lo + LANES] = (gq * scale).astype(BF)
            gqkv_ref[:, width + lo : width + lo + LANES] = (gk * scale).astype(BF)
            gqkv_ref[:, 2 * width + lo : 2 * width + lo + LANES] = gv.astype(BF)
        gn1 = nt(gqkv_ref[:, 0:width], pack_ref[:, 0:width])
        for c in range(1, 3):
            gn1 = gn1 + nt(gqkv_ref[:, c * width : (c + 1) * width], pack_ref[:, c * width : (c + 1) * width])
        hat1, inv1 = normalise(x_ref[...].astype(F32))
        gain1 = norm_ref[32:33, :]
        n1_ref[...] = (hat1 * gain1 + norm_ref[34:35, :]).astype(BF)
        pulled, ggain1, gshift1 = norm_pull(gn1, hat1, inv1, gain1)
        gx = gh + pulled
        gx_ref[...] = gx
        for r, row in enumerate((ggain1, ggain2, gshift1, gshift2)):
            norms_ref[r : r + 1, :] += row
        if has_below:
            at_row = pl.multiple_of(i * SEQ_PAD, SEQ_PAD)
            for k in range(2):
                stores[k][pl.ds(at_row, seq), :] = (below_gate_ref[:, k : k + 1] * gx).astype(BF)

            @pl.when(i == images - 1)
            def _():
                for j in range(local):
                    geo_refs[j][...] = (
                        nn(place_rows([below_prow_ref[0:1, :]], span, j * span), stores[0][...])
                        + nn(place_rows([below_prow_ref[1:2, :]], span, j * span), stores[1][...])
                    ).astype(BF)

    tokens = images * seq
    flops = 2 * tokens * width * (4 * width + 256) + 10 * HEADS * tokens * 256 * 128
    flops += 2 * (1 + 2 * has_below) * local * span * tokens * width
    results = pl.pallas_call(
        body,
        grid=(images,),
        in_specs=specs,
        out_specs=ospecs,
        out_shape=shapes,
        scratch_shapes=scratch,
        compiler_params=params(),
        cost_estimate=cost(2 * flops, 30 * tokens * width, HEADS * tokens * seq),
        name="block_backward",
    )(*inputs)
    named = dict(zip(("gx", "gbr", "gqkv", "n1", "n2", "glog", "norms"), results[:7]))
    return named, results[7:]


def dense_grads(named, attended, blocks=None):
    images, seq, width = attended.shape
    total = 4 * width + LANES
    step = 256
    if blocks is None:
        core, count, shapes = jnp.zeros((1,), jnp.int32), 1, [(width, total)]
    else:
        core, count = blocks
        shapes = [(count // 2, width // count, total)] * 2

    def body(core_ref, n1_ref, a_ref, n2_ref, gqkv_ref, gbr_ref, glog_ref, norms_ref, *refs):
        outs, (rows, flip, wide, extra_ref) = refs[: len(shapes)], refs[len(shapes) :]

        def multiply(columns, source, extra=None):
            right = wide[:, source]
            if blocks is None:
                value = nn(flip[...], right)
                outs[0][:, columns] = (value if extra is None else value + extra[...]).astype(BF)
                return
            height = width // count
            for which in range(2):
                c = core_ref[0] if which == 0 else 1 - core_ref[0]
                for y in range(count // 2):
                    at = pl.ds(pl.multiple_of((2 * y + c) * height, 16), height)
                    value = nn(flip[at, :], right)
                    outs[which][y, :, columns] = (value if extra is None else value + extra[at, :]).astype(BF)

        def load(ref, store, columns):
            store[...] = jnp.zeros_like(store)
            for i in range(images):
                store[i * SEQ_PAD : i * SEQ_PAD + seq, 0:columns] = ref[i]

        load(n1_ref, rows, width)
        flip[...] = jnp.transpose(rows[...])
        load(gqkv_ref, wide, 3 * width)
        for c in range(3 * width // step):
            multiply(slice(c * step, (c + 1) * step), slice(c * step, (c + 1) * step))
        load(a_ref, rows, width)
        flip[...] = jnp.transpose(rows[...])
        load(gbr_ref, wide, width)
        for c in range(width // step):
            multiply(slice(3 * width + c * step, 3 * width + (c + 1) * step), slice(c * step, (c + 1) * step))
        load(n2_ref, rows, width)
        flip[...] = jnp.transpose(rows[...])
        load(glog_ref, wide, LANES)
        extra_ref[...] = jnp.transpose(
            jnp.concatenate([jnp.zeros((32, width), F32), norms_ref[...], jnp.zeros((LANES - 40, width), F32)], 0)
        )
        multiply(slice(4 * width, total), slice(0, LANES), extra_ref)

    arrays = [named["n1"], attended, named["n2"], named["gqkv"], named["gbr"], named["glog"], named["norms"]]
    tokens = images * seq
    return pl.pallas_call(
        body,
        grid=(1,),
        in_specs=[pl.BlockSpec(memory_space=pltpu.SMEM)] + [fixed(a) for a in arrays],
        out_specs=[resident(shape, lambda i, n=len(shape): (0,) * n) for shape in shapes],
        out_shape=[jax.ShapeDtypeStruct(shape, BF) for shape in shapes],
        scratch_shapes=[
            pltpu.VMEM((images * SEQ_PAD, width), BF),
            pltpu.VMEM((width, images * SEQ_PAD), BF),
            pltpu.VMEM((images * SEQ_PAD, 3 * width), BF),
            pltpu.VMEM((width, LANES), F32),
        ],
        compiler_params=params(),
        cost_estimate=cost(2 * tokens * width * total, 16 * tokens * width, 0),
        name="dense_grads",
    )(core, *arrays)


def ffn_forward(layer, j, xs, win, wdown):
    ny = len(xs)
    rows, width = xs[0].shape
    fs = win[0].shape[3]
    tile = min(256, rows)

    def body(*refs):
        xr, wi, wd, outs = refs[:ny], refs[ny : ny + 2], refs[ny + 2 : ny + 4], refs[ny + 4 :]
        for y in range(ny):
            total = None
            for s in range(2):
                hid = gelu(nn(xr[y][...], wi[s][...])).astype(BF)
                part = nt(hid, wd[s][...])
                total = part if total is None else total + part
            outs[y][...] = total.astype(outs[y].dtype)

    wspec = resident((None, None, width, fs), lambda t: (layer, j, 0, 0))
    rspec = pl.BlockSpec((tile, width), lambda t: (t, 0))
    return pl.pallas_call(
        body,
        grid=(rows // tile,),
        in_specs=[rspec] * ny + [wspec] * 4,
        out_specs=[rspec] * ny,
        out_shape=[jax.ShapeDtypeStruct((rows, width), F32 if y == 0 else BF) for y in range(ny)],
        compiler_params=params(),
        cost_estimate=cost(
            2 * 8 * ny * rows * width * fs, 8 * width * fs + 4 * ny * rows * width, 2 * ny * rows * fs
        ),
        name="ffn_forward",
    )(*xs, *win, *wdown)


def ffn_backward(layer, j, xs, gs, n, win, wdown, gates=None):
    ny = len(xs)
    rows, width = xs[0].shape
    fs = win[0].shape[3]
    fused = gates is not None

    def body(*refs):
        refs = list(refs)

        def take(n):
            taken = refs[:n]
            del refs[:n]
            return taken

        xr, gr, wi, wd = take(ny), take(ny), take(2), take(2)
        tr = take(ny) if fused else None
        gx, outs = take(ny), take(2)
        eo, gg = (take(ny), take(ny)) if fused else (None, None)
        acc = refs[0]
        for y in range(ny):
            x, g = xr[y][...], gr[y][...].reshape(rows, width)
            gated = g
            if fused:
                gate = jnp.transpose(jnp.broadcast_to(tr[y][...], (8, rows)))[:, 0:1]
                gated = (gate * g.astype(F32)).astype(BF)
            back, part, dot = None, None, None
            for s in range(2):
                w1, w2 = wi[s][...], wd[s][...]
                hid, slope = gelu_both(nn(x, w1))
                hid = hid.astype(BF)
                ghid = nn(g, w2)
                if fused:
                    term = jnp.sum(hid.astype(F32) * ghid, -1, keepdims=True)
                    dot = term if dot is None else dot + term
                    term = nt(hid, w2)
                    part = term if part is None else part + term
                    ghid = gate * ghid
                gpre = (ghid * slope).astype(BF)
                term = nt(gpre, w1)
                back = term if back is None else back + term
                for m, grad in enumerate((tn(x, gpre), tn(gated, hid))):
                    if s == 0:
                        outs[0][m] = grad if y == 0 else outs[0][m] + grad
                    elif y < ny - 1:
                        acc[m] = grad if y == 0 else acc[m] + grad
                    else:
                        outs[1][m] = (grad if y == 0 else acc[m] + grad).astype(BF)
            gx[y][...] = back.astype(gx[y].dtype)
            if fused:
                eo[y][...] = part.astype(eo[y].dtype)
                gg[y][...] = jnp.transpose(jnp.broadcast_to(dot, (rows, LANES)))[0:1, :]

    wspec = resident((None, None, width, fs), lambda c: (layer, j, 0, 0))
    rspec = resident((rows, width), lambda c: (0, 0))
    uspec = resident((rows // CAP, None, CAP, width), lambda c: (0, n, 0, 0))
    lspec = resident((1, rows), lambda c: (0, 0))
    gspec = resident((2, width, fs), lambda c: (0, 0, 0))
    parts = [jax.ShapeDtypeStruct((rows, width), F32 if y == 0 else BF) for y in range(ny)]
    shapes = parts + [jax.ShapeDtypeStruct((2, width, fs), F32), jax.ShapeDtypeStruct((2, width, fs), BF)]
    if fused:
        shapes += parts + [jax.ShapeDtypeStruct((1, rows), F32)] * ny
    return pl.pallas_call(
        body,
        grid=(1,),
        in_specs=[rspec] * ny + [uspec] * ny + [wspec] * 4 + [lspec] * (ny if fused else 0),
        out_specs=[rspec] * ny + [gspec] * 2 + ([rspec] * ny + [lspec] * ny if fused else []),
        out_shape=shapes,
        scratch_shapes=[pltpu.VMEM((2, width, fs), F32)],
        compiler_params=params(),
        cost_estimate=cost(
            2 * (24 if fused else 20) * ny * rows * width * fs, 20 * width * fs + 8 * ny * rows * width, 2 * ny * rows * fs
        ),
        name="ffn_backward",
    )(*xs, *gs, *win, *wdown, *(gates if fused else ()))


def store_grads(layer, j, local, own, received, buffers):
    _, width, fs = own.shape
    tile = width // 4

    def body(own_ref, recv_ref, *refs):
        outs = refs[-2:]
        for n in range(2):
            outs[n][...] = own_ref[n] + recv_ref[n].astype(F32)

    pspec = pl.BlockSpec((2, tile, fs), lambda t: (0, t, 0))
    ospec = pl.BlockSpec((None, None, tile, fs), lambda t: (layer, j, t, 0))
    full = jax.ShapeDtypeStruct((2, local, width, fs), F32)
    extra = [] if buffers is None else list(buffers)
    return pl.pallas_call(
        body,
        grid=(4,),
        in_specs=[pspec, pspec] + [pl.BlockSpec(memory_space=pl.ANY)] * len(extra),
        out_specs=[ospec, ospec],
        out_shape=[full, full],
        input_output_aliases={} if buffers is None else {2: 0, 3: 1},
        compiler_params=params(),
        cost_estimate=cost(2 * width * fs, 20 * width * fs, 0),
        name="store_grads",
    )(own, received, *extra)


def rows_shift(count, shift):
    ys = count // 2
    return [(y * 2 + c, ((y + shift) % ys) * 2 + c) for y in range(ys) for c in range(2)]


def spread_rows(mine, count):
    return [mine] + [lax.ppermute(mine, "fsdp", rows_shift(count, s)) for s in range(1, count // 2)]


def return_parts(parts, count):
    return [parts[0]] + [
        lax.ppermute(parts[s], "fsdp", rows_shift(count, -s)) for s in range(1, count // 2)
    ]


def add_parts(parts):
    total = parts[0]
    for part in parts[1:]:
        total = total + part.astype(F32)
    return total.astype(BF)


def step(live, works):
    fresh = dict(live)
    for work in works:
        fresh.update(work(live))
    return lax.optimization_barrier(fresh)


def staged(live, count, stages, extras, pending=()):
    total = count + len(stages) - 1
    waiting = [(0, value) for value in pending]
    for t in range(total):
        works = [
            lambda now, stage=stage, j=t - s: stage(now, j)
            for s, stage in enumerate(stages)
            if 0 <= t - s < count
        ]
        for at, until, work in extras:
            if t == min(at, total - 1):
                if min(until, total - 1) <= t:
                    works.append(work)
                else:
                    waiting.append((until, work(live)))
        for until, value in waiting:
            if t == min(until, total - 1):
                works.append(lambda now, value=value: value)
        live = step(live, works)
    return live


def exchange(rows):
    return lax.all_to_all(rows, "expert", split_axis=0, concat_axis=0, tiled=True)


def swap_cores(array, count):
    return lax.ppermute(array, "fsdp", [(f, f ^ 1) for f in range(count)])


def shards(tokens_in, routes, valid, qkv_weight, out_weight, router_weight, norm_gain, norm_shift,
           expert_in, expert_down, cotangent):
    owners = lax.axis_size("expert")
    count = lax.axis_size("fsdp")
    local = expert_in.shape[1]
    layers = routes.shape[0]
    tokens, width = tokens_in.shape
    images = tokens // SEQ
    span = owners * CAP
    slots = (local, span)
    experts = router_weight.shape[2]

    packs = []
    for l in range(layers):
        shard = qkv_weight.shape[1]
        pieces = [qkv_weight[l], out_weight[l], router_weight[l], norm_gain[l].T, norm_shift[l].T]
        pieces.append(jnp.zeros((shard, LANES - experts - 4), BF))
        packs.append(jnp.concatenate(pieces, 1))
    win = (expert_in, swap_cores(expert_in, count))
    wdown = (expert_down, swap_cores(expert_down, count))

    def cut(array):
        return array.reshape(array.shape[:-2] + (images, SEQ, array.shape[-1]))

    route_cols = cut(routes)
    pcol, prow = route_places(route_cols, cut(valid), owners, local)
    cot = cut(cotangent)
    top = layers - 1

    def pick(record, *names):
        return {n: record[n] for n in names}

    def swap_y(now, name, out):
        return {out: spread_rows(now[name], count)}

    def send(now, name, out):
        return {out: exchange(now[name])}

    groups = [list(range(j, min(j + 2, local))) for j in range(0, local, 2)]
    where = {j: (g, n) for g, group in enumerate(groups) for n, j in enumerate(group)}
    live = {f"c{g}": rows for g, rows in enumerate(dispatch(cot, prow[top], slots, groups))}
    start = live
    live = step(
        live,
        [
            lambda now: {"pack0": lax.all_gather(packs[0], "fsdp", axis=0, tiled=True)},
        ],
    )
    sending = send(start, "c0", "g0")

    def enter(l):
        def work(now):
            previous = None
            stream = cut(tokens_in)
            if l > 0:
                previous = ([now[f"e{l - 1}_{j}"] for j in range(local)], pcol[l - 1], now[f"gate{l - 1}"])
                stream = now[f"h{l - 1}"]
            pack = now[f"pack{l}"]
            record, sent, rows = block_forward(
                stream, pack, route_cols[l], pcol[l], prow[l], previous, l == top, slots
            )
            out = {f"{name}{l}": value for name, value in record.items() if name != "picks"}
            if l > 0:
                out[f"picks{l - 1}"] = record["picks"]
            for j in range(local):
                out[f"s{l}_{j}"] = sent[j]
            if l == top:
                out["grow"] = rows[0][0:1, :]
            return out

        return work

    def come(l):
        return lambda now, j: send(now, f"s{l}_{j}", f"a{l}_{j}")

    def widen(l):
        return lambda now, j: swap_y(now, f"a{l}_{j}", f"x{l}_{j}")

    def back_y(now, name, out):
        return {out: add_parts(return_parts(now[name], count))}

    early = [j for j in range(local)]
    live["shards"] = packs[1:]
    before = live["shards"]
    live = step(
        live,
        [enter(0), lambda now: sending],
    )
    pending = [{f"pack{l + 1}": lax.all_gather(p, "fsdp", axis=0, tiled=True)} for l, p in enumerate(before)]
    for l in range(top):
        live = staged(
            live,
            local,
            [
                come(l),
                widen(l),
                lambda now, j, l=l: {f"p{l}_{j}": ffn_forward(l, j, now[f"x{l}_{j}"], win, wdown)},
                lambda now, j, l=l: back_y(now, f"p{l}_{j}", f"r{l}_{j}"),
                lambda now, j, l=l: send(now, f"r{l}_{j}", f"e{l}_{j}"),
            ],
            [],
            pending if l == 0 else (),
        )
        works = [enter(l + 1)]
        if l + 1 == top:
            works += [lambda now, g=g: send(now, f"c{g}", f"g{g}") for g in range(1, len(groups))]
            works.append(lambda now: swap_y(now, "g0", "gy0"))
        live = step(live, works)

    def send_gates(now):
        rows = now["grow"].reshape(local, owners, CAP).transpose(1, 0, 2).reshape(owners, local * CAP)
        return {"ga": lax.all_to_all(rows, "expert", split_axis=0, concat_axis=0, tiled=True)}

    def widen_gates(now):
        rows = now["ga"].reshape(owners, local, CAP).transpose(1, 0, 2).reshape(local, span)
        return {"gates": spread_rows(rows, count)}

    def fused_rows(now, j):
        gates = [rows[j : j + 1] for rows in now["gates"]]
        ys = count // 2
        g, n = where[j]
        results = ffn_backward(top, j, now[f"x{top}_{j}"], now[f"gy{g}"], n, win, wdown, gates)
        return {
            f"q{top}_{j}": results[:ys],
            f"own{top}_{j}": results[ys],
            f"oth{top}_{j}": results[ys + 1],
            f"f{j}": results[ys + 2 : 2 * ys + 2],
            f"gg{j}": results[2 * ys + 2 :],
        }

    def plain_rows(l):
        def work(now, j):
            ys = count // 2
            gs = [rows.reshape(owners, 1, CAP, width) for rows in now[f"gy{l}_{j}"]]
            results = ffn_backward(l, j, now[f"x{l}_{j}"], gs, 0, win, wdown)
            return {f"q{l}_{j}": results[:ys], f"own{l}_{j}": results[ys], f"oth{l}_{j}": results[ys + 1]}

        return work

    def return_rows(l):
        def work(now, j):
            out = back_y(now, f"q{l}_{j}", f"t{l}_{j}")
            out[f"oth{l}_{j}"] = swap_cores(now[f"oth{l}_{j}"], count)
            return out

        return work

    def leave(l):
        return lambda now, j: send(now, f"t{l}_{j}", f"b{l}_{j}")

    def return_gg(now):
        rows = [jnp.concatenate([now[f"gg{j}"][y] for j in range(local)], 0) for y in range(count // 2)]
        parts = return_parts(rows, count)
        total = parts[0]
        for part in parts[1:]:
            total = total + part
        return {"ggr": total}

    def send_gg(now):
        rows = now["ggr"].reshape(local, owners, CAP).transpose(1, 0, 2).reshape(owners, local * CAP)
        rows = lax.all_to_all(rows, "expert", split_axis=0, concat_axis=0, tiled=True)
        return {"ggs": rows.reshape(owners, local, CAP).transpose(1, 0, 2).reshape(local, span)}

    def keep(l, js):
        def work(now):
            buffers = now.get("buffers")
            for j in js:
                buffers = store_grads(l, j, local, now[f"own{l}_{j}"], now[f"oth{l}_{j}"], buffers)
            return {"buffers": buffers}

        return work

    live = staged(
        live,
        local,
        [come(top), widen(top), fused_rows, return_rows(top), leave(top)],
        [(0, 0, send_gates)]
        + [(0, 0, lambda now, g=g: swap_y(now, f"g{g}", f"gy{g}")) for g in range(1, len(groups))]
        + [(1, 1, widen_gates), (local + 2, local + 2, return_gg), (local + 3, local + 3, send_gg)]
        + [(local + 3, local + 3, lambda now, j=j: back_y(now, f"f{j}", f"fr{j}")) for j in early[:2]],
    )

    def scatter_sum(packed):
        return lax.psum_scatter(packed, "fsdp", scatter_dimension=0, tiled=True)

    def scatter_all(rows):
        return lax.psum_scatter(rows, "expert", scatter_dimension=0, tiled=True)

    def back_block(l):
        def work(now):
            kept = {name: now[f"{name}{l}"] for name in ("x", "h", "qkv", "lse")}
            if l < top:
                kept["picks"] = now[f"picks{l}"]
            below = None if l == 0 else (now[f"gate{l - 1}"], prow[l - 1])
            pack = now[f"pack{l}"]
            named, geo = block_backward(
                cot if l == top else now["grad"], kept, pack, route_cols[l], pcol[l],
                [now[f"b{l}_{j}"] for j in range(local)], now["ggs"] if l == top else None, below, slots
            )
            out = {f"{name}{l}": value for name, value in named.items() if name != "gx"}
            out["grad"] = named["gx"]
            if l > 0:
                for j in range(local):
                    out[f"d{l - 1}_{j}"] = geo[j]
            return out

        return work

    def grads_of(now, l, blocks=None):
        named = {name: now[f"{name}{l}"] for name in ("n1", "n2", "gqkv", "gbr", "glog", "norms")}
        return dense_grads(named, now[f"a{l}"], blocks)

    def send_eo(js):
        def work(now):
            rows = jnp.stack([now[f"fr{j}"].reshape(owners, CAP, width) for j in js], 1)
            return {f"eo{js[0]}": exchange(rows)}

        return work

    live = step(
        live, [back_block(top), send_eo(early[:2])] + [lambda now, j=j: back_y(now, f"f{j}", f"fr{j}") for j in early[2:]]
    )
    for l in reversed(range(top)):
        extras = [(0, 0, lambda now, l=l: {f"dense{l + 1}": grads_of(now, l + 1)[0]})]
        extras += [(0, 0, keep(l + 1, early[:1])), (1, 1, keep(l + 1, early[1:]))]
        extras.append((1, local - 1, lambda now, l=l: {f"share{l + 1}": scatter_sum(now[f"dense{l + 1}"])}))
        extras.append((local, local + 2, lambda now, l=l: {f"piece{l + 1}": scatter_all(now[f"share{l + 1}"])}))
        live = staged(
            live,
            local,
            [
                lambda now, j, l=l: send(now, f"d{l}_{j}", f"m{l}_{j}"),
                lambda now, j, l=l: swap_y(now, f"m{l}_{j}", f"gy{l}_{j}"),
                plain_rows(l),
                return_rows(l),
                leave(l),
            ],
            extras,
        )
        full = {f"full{l + 1}": lax.all_gather(live[f"piece{l + 1}"], "expert", axis=0, tiled=True)}
        live = step(live, [back_block(l), lambda now, full=full: full] + ([send_eo([2])] if l == 0 and local > 2 else []))

    ys = count // 2
    place = lax.axis_index("fsdp")
    y_at, core_at = place // 2, place % 2
    kept_rows, others = grads_of(live, 0, (core_at.reshape(1), count))
    live["kept"], live["others"] = kept_rows, others
    first = [lambda now: {"others": swap_cores(now["others"], count)}]
    later = send_eo(early[3:])(live) if local > 3 else {}
    live = step(live, first)
    pair = live["kept"].astype(F32) + live["others"].astype(F32)
    total = lax.dynamic_index_in_dim(pair, y_at, 0, False)
    live["mine"] = total
    live["out_rows"] = [
        lax.dynamic_index_in_dim(pair, (y_at + s) % ys, 0, False).astype(BF) for s in range(1, ys)
    ]
    live = step(
        live,
        [
            lambda now: {
                "in_rows": [
                    lax.ppermute(rows, "fsdp", rows_shift(count, s)) for s, rows in zip(range(1, ys), now["out_rows"])
                ]
            },
            keep(0, early[:2]),
            lambda now: later,
        ],
    )
    total = live["mine"]
    for rows in live["in_rows"]:
        total = total + rows.astype(F32)
    height, columns = total.shape
    live["mine"] = total.astype(BF).reshape(owners, height // owners, columns)
    def finish(now):
        return {"out": combine_last(now[f"h{top}"], eo, pcol[top], now[f"gate{top}"])}

    eo = [live[f"eo{j}"] for j in early if f"eo{j}" in live]
    live = step(live, [lambda now: send(now, "mine", "mine"), keep(0, early[2:]), finish])
    total = jnp.sum(live["mine"].astype(F32), 0).astype(BF)
    live["mine"] = jnp.broadcast_to(total[None], (owners,) + total.shape)
    live["grad"] = live["grad"].reshape(tokens, width)
    live["out"] = live["out"].reshape(tokens, width)
    live = step(live, [lambda now: send(now, "mine", "mine")])
    out = live["out"]
    buffers = live["buffers"]
    grad = live["grad"]
    dense = [live["mine"].reshape(height, columns).astype(F32)]
    dense.append(live["full1"].astype(F32))

    both = jnp.stack(dense)
    at = 4 * width + experts
    return (
        out,
        grad,
        both[:, :, : 3 * width],
        both[:, :, 3 * width : 4 * width],
        both[:, :, 4 * width : at],
        jnp.swapaxes(both[:, :, at : at + 2], 1, 2),
        jnp.swapaxes(both[:, :, at + 2 : at + 4], 1, 2),
        buffers[0],
        buffers[1],
    )


def solution(mesh):
    everyone = ("expert", "fsdp")
    return jax.shard_map(
        shards,
        mesh=mesh,
        in_specs=(
            P(everyone, None),
            P(None, everyone, None),
            P(None, everyone, None),
            P(None, "fsdp", None),
            P(None, "fsdp", None),
            P(None, "fsdp", None),
            P(None, None, "fsdp"),
            P(None, None, "fsdp"),
            P(None, "expert", None, "fsdp"),
            P(None, "expert", None, "fsdp"),
            P(everyone, None),
        ),
        out_specs=(
            P(everyone, None),
            P(everyone, None),
            P(None, "fsdp", None),
            P(None, "fsdp", None),
            P(None, "fsdp", None),
            P(None, None, "fsdp"),
            P(None, None, "fsdp"),
            P(None, "expert", None, "fsdp"),
            P(None, "expert", None, "fsdp"),
        ),
        check_vma=False,
    )
```

```python
import jax
import jax.numpy as jnp
from jax import lax
from jax.experimental import pallas as pl
from jax.experimental.pallas import tpu as pltpu
from jax.sharding import PartitionSpec as P

HEADS = 12
HEAD = 64
SEQ = 197
SEQ_PAD = 256
CAP = 64
LANES = 128
BF = jnp.bfloat16
F32 = jnp.float32
EPS = 1e-06
GELU = 0.7978845608028654
CUBE = 0.044715
VMEM_LIMIT = 56 << 20
NEG = -1e30


def nn(left, right):
    return lax.dot_general(left, right, (((1,), (0,)), ((), ())), preferred_element_type=F32)


def nt(left, right):
    return lax.dot_general(left, right, (((1,), (1,)), ((), ())), preferred_element_type=F32)


def tn(left, right):
    return lax.dot_general(left, right, (((0,), (0,)), ((), ())), preferred_element_type=F32)


def gelu(u):
    return 0.5 * u * (1.0 + jnp.tanh(GELU * (u + CUBE * u * u * u)))


def gelu_both(u):
    square = u * u
    t = jnp.tanh(GELU * u * (1.0 + CUBE * square))
    half = 0.5 * (1.0 + t)
    return u * half, half + 0.5 * u * (1.0 - t * t) * (GELU * (1.0 + 3.0 * CUBE * square))


def normalise(v):
    centred = v - jnp.mean(v, -1, keepdims=True)
    inv = lax.rsqrt(jnp.mean(centred * centred, -1, keepdims=True) + EPS)
    return centred * inv, inv


def norm_pull(grad, hat, inv, gain):
    scaled = grad * gain
    pulled = inv * (
        scaled
        - jnp.mean(scaled, -1, keepdims=True)
        - hat * jnp.mean(scaled * hat, -1, keepdims=True)
    )
    return pulled, jnp.sum(grad * hat, 0, keepdims=True), jnp.sum(grad, 0, keepdims=True)


def resident(shape, index):
    return pl.BlockSpec(shape, index, pipeline_mode=pl.Buffered(1))


def fixed(array):
    zeros = (0,) * array.ndim
    return resident(array.shape, lambda i: zeros)


def per_image(*tail):
    zeros = (0,) * len(tail)
    return pl.BlockSpec((None,) + tail, lambda i: (i,) + zeros)


def cost(flops, byte_count, exps):
    return pl.CostEstimate(
        flops=int(flops), bytes_accessed=int(byte_count), transcendentals=int(exps)
    )


def params():
    return pltpu.CompilerParams(vmem_limit_bytes=VMEM_LIMIT)


def lanes(shape):
    return lax.broadcasted_iota(jnp.int32, shape, 1)


def pick_rows(columns, slots, start):
    hit = lanes((columns[0].shape[0], slots)) == columns[0] - start
    for column in columns[1:]:
        hit = hit | (lanes((column.shape[0], slots)) == column - start)
    return jnp.where(hit, 1.0, 0.0).astype(BF)


def place_rows(rows, slots, start):
    sub = lax.broadcasted_iota(jnp.int32, (slots, rows[0].shape[1]), 0)
    hit = sub == rows[0] - start
    for row in rows[1:]:
        hit = hit | (sub == row - start)
    return jnp.where(hit, 1.0, 0.0).astype(BF)


def norm_rows(pack_ref, width):
    tail = pack_ref[:, 4 * width :].astype(F32)
    return jnp.transpose(tail)


def block_forward(stream, pack, routes, pcol, prow, previous, want_rows, slots):
    images, seq, width = stream.shape
    chunks = 4 * width
    local = slots[0]
    span = slots[1]
    has_prev = previous is not None
    inputs = [stream, pack, routes, pcol, prow]
    specs = [per_image(seq, width), fixed(pack), per_image(seq, 2), per_image(seq, 2), fixed(prow)]
    if has_prev:
        inputs += list(previous[0]) + [previous[1], previous[2]]
        specs += [fixed(a) for a in previous[0]] + [per_image(seq, 2), per_image(seq, 2)]
    shapes, ospecs = [], []

    def out(shape, dtype, spec):
        shapes.append(jax.ShapeDtypeStruct(shape, dtype))
        ospecs.append(spec)

    out((images, seq, 3 * width), BF, per_image(seq, 3 * width))
    out((images, 16, seq), F32, per_image(16, seq))
    out((images, seq, width), BF, per_image(seq, width))
    out((images, seq, width), F32, per_image(seq, width))
    out((images, seq, 2), F32, per_image(seq, 2))
    if has_prev:
        out((images, seq, width), F32, per_image(seq, width))
        out((images, seq, width), BF, per_image(seq, width))
        out((images, seq, width), BF, per_image(seq, width))
    for _ in range(local):
        out((span, width), BF, resident((span, width), lambda i: (0, 0)))
    if want_rows:
        out((8, local * span), F32, resident((8, local * span), lambda i: (0, 0)))
    scratch = [pltpu.VMEM((images * SEQ_PAD, width), BF), pltpu.VMEM((LANES, width), F32)]

    def body(*refs):
        refs = list(refs)
        x_ref, pack_ref, routes_ref, pcol_ref, prow_ref = refs[:5]
        at = 5
        if has_prev:
            eo_refs = refs[at : at + local]
            old_pcol_ref, old_gate_ref = refs[at + local : at + local + 2]
            at += local + 2
        qkv_ref, lse_ref, a_ref, h_ref, gate_ref = refs[at : at + 5]
        at += 5
        if has_prev:
            xs_ref, pick0_ref, pick1_ref = refs[at : at + 3]
            at += 3
        disp_refs = refs[at : at + local]
        at += local
        if want_rows:
            grow_ref = refs[at]
        store, norm_ref = refs[-2:]
        i = pl.program_id(0)

        @pl.when(i == 0)
        def _():
            norm_ref[...] = norm_rows(pack_ref, width)
            store[...] = jnp.zeros_like(store)
            if want_rows:
                grow_ref[...] = jnp.zeros_like(grow_ref)

        x = x_ref[...].astype(F32)
        if has_prev:
            for k, pick_ref in enumerate((pick0_ref, pick1_ref)):
                picked = None
                for j in range(local):
                    hot = pick_rows([old_pcol_ref[:, k : k + 1]], span, j * span)
                    term = nn(hot, eo_refs[j][...])
                    picked = term if picked is None else picked + term
                pick_ref[...] = picked.astype(BF)
                x = x + old_gate_ref[:, k : k + 1] * picked
            xs_ref[...] = x
        hat, _ = normalise(x)
        n1 = (hat * norm_ref[32:33, :] + norm_ref[34:35, :]).astype(BF)
        for c in range(3):
            qkv_ref[:, c * width : (c + 1) * width] = nn(
                n1, pack_ref[:, c * width : (c + 1) * width]
            ).astype(BF)
        lane = lanes((seq, LANES))
        lse_ref[...] = jnp.zeros_like(lse_ref)
        for pair in range(HEADS // 2):
            lo = pair * LANES
            q = qkv_ref[:, lo : lo + LANES]
            k = qkv_ref[:, width + lo : width + lo + LANES]
            v = qkv_ref[:, 2 * width + lo : 2 * width + lo + LANES]
            parts = []
            for half in range(2):
                mine = (lane < HEAD) if half == 0 else (lane >= HEAD)
                scores = nt(k, jnp.where(mine, q, jnp.zeros_like(q))) * HEAD ** (-0.5)
                top = jnp.max(scores, 0, keepdims=True)
                weights = jnp.exp(scores - top)
                total = jnp.sum(weights, 0, keepdims=True)
                lse_ref[2 * pair + half : 2 * pair + half + 1, :] = top + jnp.log(total)
                probs = (weights * (1.0 / total)).astype(BF)
                parts.append(tn(probs, v))
            a_ref[:, lo : lo + LANES] = jnp.where(lane < HEAD, parts[0], parts[1]).astype(BF)
        h = x + nn(a_ref[...], pack_ref[:, 3 * width : 4 * width])
        h_ref[...] = h
        hat, _ = normalise(h)
        n2 = (hat * norm_ref[33:34, :] + norm_ref[35:36, :]).astype(BF)
        logits = nn(n2, pack_ref[:, chunks : chunks + LANES])
        logits = jnp.where(lane < 32, logits, NEG)
        weights = jnp.exp(logits - jnp.max(logits, -1, keepdims=True))
        probs = weights / jnp.sum(weights, -1, keepdims=True)
        gates = []
        for k in range(2):
            chosen = jnp.where(lane == routes_ref[:, k : k + 1], probs, 0.0)
            kept = jnp.where(pcol_ref[:, k : k + 1] >= 0, 1.0, 0.0)
            gates.append(jnp.sum(chosen, -1, keepdims=True) * kept)
            gate_ref[:, k : k + 1] = gates[k]
        store[pl.ds(pl.multiple_of(i * SEQ_PAD, SEQ_PAD), seq), :] = n2
        if want_rows:
            where = lanes((seq, local * span))
            spread = [jnp.where(where == pcol_ref[:, k : k + 1], gates[k], 0.0) for k in range(2)]
            grow_ref[0:1, :] += jnp.sum(spread[0] + spread[1], 0, keepdims=True)

        @pl.when(i == images - 1)
        def _():
            rows = [prow_ref[0:1, :], prow_ref[1:2, :]]
            for j in range(local):
                disp_refs[j][...] = nn(place_rows(rows, span, j * span), store[...]).astype(BF)

    tokens = images * seq
    flops = 2 * tokens * width * (4 * width + 128) + 4 * HEADS * tokens * 256 * 128
    flops += 2 * (1 + 2 * has_prev) * local * span * tokens * width
    results = pl.pallas_call(
        body,
        grid=(images,),
        in_specs=specs,
        out_specs=ospecs,
        out_shape=shapes,
        scratch_shapes=scratch,
        compiler_params=params(),
        cost_estimate=cost(2 * flops, 20 * tokens * width, HEADS * tokens * seq),
        name="block_forward",
    )(*inputs)
    kept = dict(zip(("qkv", "lse", "a", "h", "gate"), results[:5]))
    rest = results[5:]
    kept["x"] = stream
    if has_prev:
        kept["x"] = rest[0]
        kept["picks"] = (rest[1], rest[2])
        rest = rest[3:]
    return kept, rest[:local], rest[local:]


def dispatch(rows, prow, slots, groups):
    images, seq, width = rows.shape
    span = slots[1]
    owners = span // CAP

    def body(rows_ref, prow_ref, *refs):
        outs, store = refs[:-1], refs[-1]
        store[...] = jnp.zeros_like(store)
        for i in range(images):
            store[i * SEQ_PAD : i * SEQ_PAD + seq, :] = rows_ref[i]
        for out, group in zip(outs, groups):
            for n, j in enumerate(group):
                hot = place_rows([prow_ref[0:1, :], prow_ref[1:2, :]], span, j * span)
                out[:, n] = nn(hot, store[...]).astype(BF).reshape(owners, CAP, width)

    shapes = [(owners, len(group), CAP, width) for group in groups]
    return pl.pallas_call(
        body,
        grid=(1,),
        in_specs=[fixed(rows), fixed(prow)],
        out_specs=[resident(shape, lambda i: (0, 0, 0, 0)) for shape in shapes],
        out_shape=[jax.ShapeDtypeStruct(shape, BF) for shape in shapes],
        scratch_shapes=[pltpu.VMEM((images * SEQ_PAD, width), BF)],
        compiler_params=params(),
        cost_estimate=cost(4 * slots[0] * span * images * seq * width, 8 * slots[0] * span * width, 0),
        name="dispatch",
    )(rows, prow)


def route_places(routes, valid, owners, local):
    layers, images, seq, _ = routes.shape

    def body(routes_ref, valid_ref, pcol_ref, prow_ref):
        prow_ref[...] = jnp.full(prow_ref.shape, -1, jnp.int32)
        lane = lanes((seq, LANES))
        below = lax.broadcasted_iota(jnp.int32, (seq, seq), 0) > lanes((seq, seq))
        below = jnp.where(below, 1.0, 0.0).astype(BF)
        base = jnp.zeros((1, LANES), F32)
        for i in range(images):
            hot = [jnp.where(lane == routes_ref[i, :, k : k + 1], 1.0, 0.0) for k in range(2)]
            both = hot[0] + hot[1]
            earlier = nn(below, both.astype(BF)) + base
            base = base + jnp.sum(both, 0, keepdims=True)
            columns = jnp.full((seq, LANES), -1.0, F32)
            for k in range(2):
                slot = jnp.sum(hot[k] * earlier, -1, keepdims=True)
                expert = routes_ref[i, :, k : k + 1]
                owner = expert // local
                start = ((expert - owner * local) * owners + owner) * CAP
                place = jnp.where(valid_ref[i, :, k : k + 1] > 0, start.astype(F32) + slot, -1.0)
                pcol_ref[i, :, k : k + 1] = place.astype(jnp.int32)
                columns = jnp.where(lane == k, place, columns)
            padded = jnp.concatenate([columns, jnp.full((SEQ_PAD - seq, LANES), -1.0, F32)], 0)
            prow_ref[:, i * SEQ_PAD : (i + 1) * SEQ_PAD] = jnp.transpose(padded)[0:8, :].astype(jnp.int32)

    spec = pl.BlockSpec((None, images, seq, 2), lambda l: (l, 0, 0, 0))
    return pl.pallas_call(
        body,
        grid=(layers,),
        in_specs=[spec, spec],
        out_specs=[spec, pl.BlockSpec((None, 8, images * SEQ_PAD), lambda l: (l, 0, 0))],
        out_shape=[
            jax.ShapeDtypeStruct((layers, images, seq, 2), jnp.int32),
            jax.ShapeDtypeStruct((layers, 8, images * SEQ_PAD), jnp.int32),
        ],
        compiler_params=params(),
        cost_estimate=cost(2 * layers * images * seq * seq * LANES, 1 << 20, 0),
        name="route_places",
    )(routes, valid)


def combine_last(h, expert_rows, pcol, gate):
    images, seq, width = h.shape
    owners = expert_rows[0].shape[0]
    span = owners * CAP
    where = [(a, n) for a, array in enumerate(expert_rows) for n in range(array.shape[1])]
    local = len(where)

    def body(h_ref, pcol_ref, gate_ref, *refs):
        eo_refs, out_ref = refs[:-1], refs[-1]
        x = h_ref[...]
        for k in range(2):
            picked = None
            for j in range(local):
                rows = eo_refs[where[j][0]][:, where[j][1]].reshape(span, width)
                term = nn(pick_rows([pcol_ref[:, k : k + 1]], span, j * span), rows)
                picked = term if picked is None else picked + term
            x = x + gate_ref[:, k : k + 1] * picked
        out_ref[...] = x.astype(BF)

    return pl.pallas_call(
        body,
        grid=(images,),
        in_specs=[per_image(seq, width), per_image(seq, 2), per_image(seq, 2)]
        + [fixed(a) for a in expert_rows],
        out_specs=per_image(seq, width),
        out_shape=jax.ShapeDtypeStruct((images, seq, width), BF),
        compiler_params=params(),
        cost_estimate=cost(8 * local * span * images * seq * width, 20 * images * seq * width, 0),
        name="combine_last",
    )(h, pcol, gate, *expert_rows)


def block_backward(grad, kept, pack, routes, pcol, expert_grads, gate_grads, below, slots):
    images, seq, width = grad.shape
    local, span = slots
    has_below = below is not None
    has_gg = gate_grads is not None
    row3, row2 = per_image(seq, width), per_image(seq, 2)
    inputs = [grad, kept["x"], kept["h"], kept["qkv"], kept["lse"], pack, routes, pcol]
    specs = [row3, row3, row3, per_image(seq, 3 * width), per_image(16, seq), fixed(pack), row2, row2]
    inputs += list(expert_grads)
    specs += [fixed(a) for a in expert_grads]
    if has_gg:
        inputs.append(gate_grads)
        specs.append(fixed(gate_grads))
    else:
        inputs += list(kept["picks"])
        specs += [row3, row3]
    if has_below:
        inputs += [below[0], below[1]]
        specs += [row2, fixed(below[1])]
    shapes, ospecs = [], []

    def out(shape, dtype, spec):
        shapes.append(jax.ShapeDtypeStruct(shape, dtype))
        ospecs.append(spec)

    out((images, seq, width), F32, row3)
    out((images, seq, width), BF, row3)
    out((images, seq, 3 * width), BF, per_image(seq, 3 * width))
    out((images, seq, width), BF, row3)
    out((images, seq, width), BF, row3)
    out((images, seq, LANES), BF, per_image(seq, LANES))
    out((8, width), F32, resident((8, width), lambda i: (0, 0)))
    if has_below:
        for _ in range(local):
            out((span, width), BF, resident((span, width), lambda i: (0, 0)))
    scratch = [pltpu.VMEM((images * SEQ_PAD, width), BF)] * (2 if has_below else 0)
    scratch += [pltpu.VMEM((LANES, width), F32), pltpu.VMEM((seq, width), BF)]

    def body(*refs):
        refs = list(refs)
        grad_ref, x_ref, h_ref, qkv_ref, lse_ref, pack_ref, routes_ref, pcol_ref = refs[:8]
        at = 8
        gbuf_refs = refs[at : at + local]
        at += local
        if has_gg:
            gg_ref = refs[at]
            at += 1
        else:
            pick_refs = refs[at : at + 2]
            at += 2
        if has_below:
            below_gate_ref, below_prow_ref = refs[at : at + 2]
            at += 2
        gx_ref, gbr_ref, gqkv_ref, n1_ref, n2_ref, glog_ref, norms_ref = refs[at : at + 7]
        at += 7
        if has_below:
            geo_refs = refs[at : at + local]
            at += local
            stores = refs[at : at + 2]
        norm_ref, ga_ref = refs[-2:]
        i = pl.program_id(0)

        @pl.when(i == 0)
        def _():
            norm_ref[...] = norm_rows(pack_ref, width)
            norms_ref[...] = jnp.zeros_like(norms_ref)
            if has_below:
                for store in stores:
                    store[...] = jnp.zeros_like(store)

        lane = lanes((seq, LANES))
        gy = grad_ref[...].astype(F32)
        columns = [pcol_ref[:, 0:1], pcol_ref[:, 1:2]]
        gn2 = None
        for j in range(local):
            term = nn(pick_rows(columns, span, j * span), gbuf_refs[j][...])
            gn2 = term if gn2 is None else gn2 + term
        hat2, inv2 = normalise(h_ref[...])
        gain2 = norm_ref[33:34, :]
        n2 = (hat2 * gain2 + norm_ref[35:36, :]).astype(BF)
        n2_ref[...] = n2
        router = pack_ref[:, 4 * width : 4 * width + LANES]
        logits = jnp.where(lane < 32, nn(n2, router), NEG)
        weights = jnp.exp(logits - jnp.max(logits, -1, keepdims=True))
        probs = weights / jnp.sum(weights, -1, keepdims=True)
        gr = jnp.zeros_like(probs)
        for k in range(2):
            if has_gg:
                gg = 0.0
                for j in range(local):
                    hit = lanes((seq, span)) == columns[k] - j * span
                    gg = gg + jnp.sum(jnp.where(hit, gg_ref[j : j + 1, :], 0.0), -1, keepdims=True)
            else:
                gg = jnp.sum(gy * pick_refs[k][...].astype(F32), -1, keepdims=True)
            gg = jnp.where(columns[k] >= 0, gg, 0.0)
            gr = gr + jnp.where(lane == routes_ref[:, k : k + 1], gg, 0.0)
        glog = (probs * (gr - jnp.sum(probs * gr, -1, keepdims=True))).astype(BF)
        glog_ref[...] = glog
        gn2 = gn2 + nt(glog, jnp.where(lanes((width, LANES)) < 32, router, jnp.zeros_like(router)))
        pulled, ggain2, gshift2 = norm_pull(gn2, hat2, inv2, gain2)
        gh = gy + pulled
        gbr = gh.astype(BF)
        gbr_ref[...] = gbr
        ga_ref[...] = nt(gbr, pack_ref[:, 3 * width : 4 * width]).astype(BF)
        scale = HEAD ** (-0.5)
        for pair in range(HEADS // 2):
            lo = pair * LANES
            q = qkv_ref[:, lo : lo + LANES]
            k = qkv_ref[:, width + lo : width + lo + LANES]
            v = qkv_ref[:, 2 * width + lo : 2 * width + lo + LANES]
            ga = ga_ref[:, lo : lo + LANES]
            gq, gk, gv = None, None, None
            for half in range(2):
                mine = (lane < HEAD) if half == 0 else (lane >= HEAD)
                zero = jnp.zeros_like(q)
                qm, km, gam = jnp.where(mine, q, zero), jnp.where(mine, k, zero), jnp.where(mine, ga, zero)
                scores = nt(k, qm) * scale
                p = jnp.exp(scores - lse_ref[2 * pair + half : 2 * pair + half + 1, :])
                gp = nt(v, gam)
                gs = (p * (gp - jnp.sum(p * gp, 0, keepdims=True))).astype(BF)
                tv = nn(p.astype(BF), gam)
                tk = nn(gs, qm)
                tq = tn(gs, km)
                gq = tq if gq is None else gq + tq
                gk = tk if gk is None else gk + tk
                gv = tv if gv is None else gv + tv
            gqkv_ref[:, lo : lo + LANES] = (gq * scale).astype(BF)
            gqkv_ref[:, width + lo : width + lo + LANES] = (gk * scale).astype(BF)
            gqkv_ref[:, 2 * width + lo : 2 * width + lo + LANES] = gv.astype(BF)
        gn1 = nt(gqkv_ref[:, 0:width], pack_ref[:, 0:width])
        for c in range(1, 3):
            gn1 = gn1 + nt(gqkv_ref[:, c * width : (c + 1) * width], pack_ref[:, c * width : (c + 1) * width])
        hat1, inv1 = normalise(x_ref[...].astype(F32))
        gain1 = norm_ref[32:33, :]
        n1_ref[...] = (hat1 * gain1 + norm_ref[34:35, :]).astype(BF)
        pulled, ggain1, gshift1 = norm_pull(gn1, hat1, inv1, gain1)
        gx = gh + pulled
        gx_ref[...] = gx
        for r, row in enumerate((ggain1, ggain2, gshift1, gshift2)):
            norms_ref[r : r + 1, :] += row
        if has_below:
            at_row = pl.multiple_of(i * SEQ_PAD, SEQ_PAD)
            for k in range(2):
                stores[k][pl.ds(at_row, seq), :] = (below_gate_ref[:, k : k + 1] * gx).astype(BF)

            @pl.when(i == images - 1)
            def _():
                for j in range(local):
                    geo_refs[j][...] = (
                        nn(place_rows([below_prow_ref[0:1, :]], span, j * span), stores[0][...])
                        + nn(place_rows([below_prow_ref[1:2, :]], span, j * span), stores[1][...])
                    ).astype(BF)

    tokens = images * seq
    flops = 2 * tokens * width * (4 * width + 256) + 10 * HEADS * tokens * 256 * 128
    flops += 2 * (1 + 2 * has_below) * local * span * tokens * width
    results = pl.pallas_call(
        body,
        grid=(images,),
        in_specs=specs,
        out_specs=ospecs,
        out_shape=shapes,
        scratch_shapes=scratch,
        compiler_params=params(),
        cost_estimate=cost(2 * flops, 30 * tokens * width, HEADS * tokens * seq),
        name="block_backward",
    )(*inputs)
    named = dict(zip(("gx", "gbr", "gqkv", "n1", "n2", "glog", "norms"), results[:7]))
    return named, results[7:]


def backward_head(grad, kept, pack, routes, pcol, expert_grads, slots):
    images, seq, width = grad.shape
    local, span = slots
    has_gg = False
    row3, row2 = per_image(seq, width), per_image(seq, 2)
    inputs = [grad, kept["h"], pack, routes, pcol] + list(expert_grads) + list(kept["picks"])
    specs = [row3, row3, fixed(pack), row2, row2] + [fixed(a) for a in expert_grads] + [row3, row3]

    def body(grad_ref, h_ref, pack_ref, routes_ref, pcol_ref, *refs):
        gbuf_refs, pick_refs = refs[:local], refs[local : local + 2]
        gh_ref, gbr_ref, n2_ref, glog_ref, norms_ref, norm_ref = refs[local + 2 :]
        gg_ref = None
        i = pl.program_id(0)

        @pl.when(i == 0)
        def _():
            norm_ref[...] = norm_rows(pack_ref, width)
            norms_ref[...] = jnp.zeros_like(norms_ref)

        lane = lanes((seq, LANES))
        gy = grad_ref[...].astype(F32)
        columns = [pcol_ref[:, 0:1], pcol_ref[:, 1:2]]
        gn2 = None
        for j in range(local):
            term = nn(pick_rows(columns, span, j * span), gbuf_refs[j][...])
            gn2 = term if gn2 is None else gn2 + term
        hat2, inv2 = normalise(h_ref[...])
        gain2 = norm_ref[33:34, :]
        n2 = (hat2 * gain2 + norm_ref[35:36, :]).astype(BF)
        n2_ref[...] = n2
        router = pack_ref[:, 4 * width : 4 * width + LANES]
        logits = jnp.where(lane < 32, nn(n2, router), NEG)
        weights = jnp.exp(logits - jnp.max(logits, -1, keepdims=True))
        probs = weights / jnp.sum(weights, -1, keepdims=True)
        gr = jnp.zeros_like(probs)
        for k in range(2):
            if has_gg:
                gg = 0.0
                for j in range(local):
                    hit = lanes((seq, span)) == columns[k] - j * span
                    gg = gg + jnp.sum(jnp.where(hit, gg_ref[j : j + 1, :], 0.0), -1, keepdims=True)
            else:
                gg = jnp.sum(gy * pick_refs[k][...].astype(F32), -1, keepdims=True)
            gg = jnp.where(columns[k] >= 0, gg, 0.0)
            gr = gr + jnp.where(lane == routes_ref[:, k : k + 1], gg, 0.0)
        glog = (probs * (gr - jnp.sum(probs * gr, -1, keepdims=True))).astype(BF)
        glog_ref[...] = glog
        gn2 = gn2 + nt(glog, jnp.where(lanes((width, LANES)) < 32, router, jnp.zeros_like(router)))
        pulled, ggain2, gshift2 = norm_pull(gn2, hat2, inv2, gain2)
        gh = gy + pulled
        gbr = gh.astype(BF)
        gbr_ref[...] = gbr
        gh_ref[...] = gh
        norms_ref[1:2, :] += ggain2
        norms_ref[3:4, :] += gshift2

    tokens = images * seq
    whole = resident((8, width), lambda i: (0, 0))
    wide = jax.ShapeDtypeStruct((images, seq, width), BF)
    results = pl.pallas_call(
        body,
        grid=(images,),
        in_specs=specs,
        out_specs=[row3, row3, row3, per_image(seq, LANES), whole],
        out_shape=[
            jax.ShapeDtypeStruct((images, seq, width), F32), wide, wide,
            jax.ShapeDtypeStruct((images, seq, LANES), BF), jax.ShapeDtypeStruct((8, width), F32),
        ],
        scratch_shapes=[pltpu.VMEM((LANES, width), F32)],
        compiler_params=params(),
        cost_estimate=cost(4 * local * span * tokens * width, 20 * tokens * width, tokens * LANES),
        name="backward_head",
    )(*inputs)
    return dict(zip(("gh", "gbr", "n2", "glog", "norms"), results))


def backward_rest(head, kept, pack):
    images, seq, width = head["gh"].shape
    row3, row9 = per_image(seq, width), per_image(seq, 3 * width)

    def body(gh_ref, gbr_ref, x_ref, qkv_ref, lse_ref, pack_ref, gx_ref, gqkv_ref, n1_ref, norms_ref, norm_ref, ga_ref):
        i = pl.program_id(0)

        @pl.when(i == 0)
        def _():
            norm_ref[...] = norm_rows(pack_ref, width)
            norms_ref[...] = jnp.zeros_like(norms_ref)

        lane = lanes((seq, LANES))
        ga_ref[...] = nt(gbr_ref[...], pack_ref[:, 3 * width : 4 * width]).astype(BF)
        scale = HEAD ** (-0.5)
        for pair in range(HEADS // 2):
            lo = pair * LANES
            q = qkv_ref[:, lo : lo + LANES]
            k = qkv_ref[:, width + lo : width + lo + LANES]
            v = qkv_ref[:, 2 * width + lo : 2 * width + lo + LANES]
            ga = ga_ref[:, lo : lo + LANES]
            gq, gk, gv = None, None, None
            for half in range(2):
                mine = (lane < HEAD) if half == 0 else (lane >= HEAD)
                zero = jnp.zeros_like(q)
                qm, km, gam = jnp.where(mine, q, zero), jnp.where(mine, k, zero), jnp.where(mine, ga, zero)
                scores = nt(k, qm) * scale
                p = jnp.exp(scores - lse_ref[2 * pair + half : 2 * pair + half + 1, :])
                gp = nt(v, gam)
                gs = (p * (gp - jnp.sum(p * gp, 0, keepdims=True))).astype(BF)
                tv = nn(p.astype(BF), gam)
                tk = nn(gs, qm)
                tq = tn(gs, km)
                gq = tq if gq is None else gq + tq
                gk = tk if gk is None else gk + tk
                gv = tv if gv is None else gv + tv
            gqkv_ref[:, lo : lo + LANES] = (gq * scale).astype(BF)
            gqkv_ref[:, width + lo : width + lo + LANES] = (gk * scale).astype(BF)
            gqkv_ref[:, 2 * width + lo : 2 * width + lo + LANES] = gv.astype(BF)
        gn1 = nt(gqkv_ref[:, 0:width], pack_ref[:, 0:width])
        for c in range(1, 3):
            gn1 = gn1 + nt(gqkv_ref[:, c * width : (c + 1) * width], pack_ref[:, c * width : (c + 1) * width])
        hat1, inv1 = normalise(x_ref[...].astype(F32))
        gain1 = norm_ref[32:33, :]
        n1_ref[...] = (hat1 * gain1 + norm_ref[34:35, :]).astype(BF)
        pulled, ggain1, gshift1 = norm_pull(gn1, hat1, inv1, gain1)
        gx_ref[...] = gh_ref[...] + pulled
        norms_ref[0:1, :] += ggain1
        norms_ref[2:3, :] += gshift1

    tokens = images * seq
    flops = 2 * tokens * width * 4 * width + 10 * HEADS * tokens * 256 * 128
    results = pl.pallas_call(
        body,
        grid=(images,),
        in_specs=[row3, row3, row3, row9, per_image(16, seq), fixed(pack)],
        out_specs=[row3, row9, row3, resident((8, width), lambda i: (0, 0))],
        out_shape=[
            jax.ShapeDtypeStruct((images, seq, width), F32),
            jax.ShapeDtypeStruct((images, seq, 3 * width), BF),
            jax.ShapeDtypeStruct((images, seq, width), BF),
            jax.ShapeDtypeStruct((8, width), F32),
        ],
        scratch_shapes=[pltpu.VMEM((LANES, width), F32), pltpu.VMEM((seq, width), BF)],
        compiler_params=params(),
        cost_estimate=cost(2 * flops, 24 * tokens * width, HEADS * tokens * seq),
        name="backward_rest",
    )(head["gh"], head["gbr"], kept["x"], kept["qkv"], kept["lse"], pack)
    return dict(zip(("gx", "gqkv", "n1", "norms"), results))


def dense_grads(parts, tail, norms, blocks=None):
    images, seq, width = parts[0][0].shape
    widths = [right.shape[2] for _, right in parts]
    total = sum(widths) + LANES
    step = 256
    if blocks is None:
        core, count, shapes = jnp.zeros((1,), jnp.int32), 1, [(width, total)]
    else:
        core, count = blocks
        shapes = [(count // 2, width // count, total)] * 2
    pairs = list(parts) + ([] if tail is None else [tail])

    def body(core_ref, norms_ref, *refs):
        refs = list(refs)
        pair_refs = [(refs[2 * n], refs[2 * n + 1]) for n in range(len(pairs))]
        outs, (rows, flip, wide, extra_ref) = refs[2 * len(pairs) : -4], refs[-4:]

        def load(ref, store, columns):
            store[...] = jnp.zeros_like(store)
            for i in range(images):
                store[i * SEQ_PAD : i * SEQ_PAD + seq, 0:columns] = ref[i]

        def multiply(columns, source, extra=None):
            def value(at):
                found = nn(flip[at, :], wide[:, source]) if source is not None else None
                if extra is None:
                    return found
                return extra[at, :] if found is None else found + extra[at, :]

            if blocks is None:
                outs[0][:, columns] = value(slice(None)).astype(BF)
                return
            height = width // count
            for which in range(2):
                c = core_ref[0] if which == 0 else 1 - core_ref[0]
                for y in range(count // 2):
                    at = pl.ds(pl.multiple_of((2 * y + c) * height, 16), height)
                    outs[which][y, :, columns] = value(at).astype(BF)

        begin = 0
        for (left, right), size in zip(pair_refs, widths):
            load(left, rows, width)
            flip[...] = jnp.transpose(rows[...])
            load(right, wide, size)
            for c in range(size // step):
                multiply(slice(begin + c * step, begin + (c + 1) * step), slice(c * step, (c + 1) * step))
            begin += size
        extra_ref[...] = jnp.transpose(
            jnp.concatenate([jnp.zeros((32, width), F32), norms_ref[...], jnp.zeros((LANES - 40, width), F32)], 0)
        )
        if tail is not None:
            load(pair_refs[-1][0], rows, width)
            flip[...] = jnp.transpose(rows[...])
            load(pair_refs[-1][1], wide, LANES)
        multiply(slice(begin, total), None if tail is None else slice(0, LANES), extra_ref)

    arrays = [norms] + [array for pair in pairs for array in pair]
    tokens = images * seq
    return pl.pallas_call(
        body,
        grid=(1,),
        in_specs=[pl.BlockSpec(memory_space=pltpu.SMEM)] + [fixed(a) for a in arrays],
        out_specs=[resident(shape, lambda i, n=len(shape): (0,) * n) for shape in shapes],
        out_shape=[jax.ShapeDtypeStruct(shape, BF) for shape in shapes],
        scratch_shapes=[
            pltpu.VMEM((images * SEQ_PAD, width), BF),
            pltpu.VMEM((width, images * SEQ_PAD), BF),
            pltpu.VMEM((images * SEQ_PAD, max(widths)), BF),
            pltpu.VMEM((width, LANES), F32),
        ],
        compiler_params=params(),
        cost_estimate=cost(2 * tokens * width * total, 16 * tokens * width, 0),
        name="dense_grads",
    )(core, *arrays)


def ffn_forward(layer, j, xs, win, wdown):
    ny = len(xs)
    rows, width = xs[0].shape
    fs = win[0].shape[3]
    tile = min(256, rows)

    def body(*refs):
        xr, wi, wd, outs = refs[:ny], refs[ny : ny + 2], refs[ny + 2 : ny + 4], refs[ny + 4 :]
        for y in range(ny):
            total = None
            for s in range(2):
                hid = gelu(nn(xr[y][...], wi[s][...])).astype(BF)
                part = nt(hid, wd[s][...])
                total = part if total is None else total + part
            outs[y][...] = total.astype(outs[y].dtype)

    wspec = resident((None, None, width, fs), lambda t: (layer, j, 0, 0))
    rspec = pl.BlockSpec((tile, width), lambda t: (t, 0))
    return pl.pallas_call(
        body,
        grid=(rows // tile,),
        in_specs=[rspec] * ny + [wspec] * 4,
        out_specs=[rspec] * ny,
        out_shape=[jax.ShapeDtypeStruct((rows, width), F32 if y == 0 else BF) for y in range(ny)],
        compiler_params=params(),
        cost_estimate=cost(
            2 * 8 * ny * rows * width * fs, 8 * width * fs + 4 * ny * rows * width, 2 * ny * rows * fs
        ),
        name="ffn_forward",
    )(*xs, *win, *wdown)


def ffn_backward(layer, j, xs, gs, n, win, wdown, gates=None):
    ny = len(xs)
    rows, width = xs[0].shape
    fs = win[0].shape[3]
    fused = gates is not None

    def body(*refs):
        refs = list(refs)

        def take(n):
            taken = refs[:n]
            del refs[:n]
            return taken

        xr, gr, wi, wd = take(ny), take(ny), take(2), take(2)
        tr = take(ny) if fused else None
        gx, outs = take(ny), take(2)
        eo, gg = (take(ny), take(ny)) if fused else (None, None)
        acc = refs[0]
        for y in range(ny):
            x, g = xr[y][...], gr[y][...].reshape(rows, width)
            gated = g
            if fused:
                gate = jnp.transpose(jnp.broadcast_to(tr[y][...], (8, rows)))[:, 0:1]
                gated = (gate * g.astype(F32)).astype(BF)
            back, part, dot = None, None, None
            for s in range(2):
                w1, w2 = wi[s][...], wd[s][...]
                hid, slope = gelu_both(nn(x, w1))
                hid = hid.astype(BF)
                ghid = nn(g, w2)
                if fused:
                    term = jnp.sum(hid.astype(F32) * ghid, -1, keepdims=True)
                    dot = term if dot is None else dot + term
                    term = nt(hid, w2)
                    part = term if part is None else part + term
                    ghid = gate * ghid
                gpre = (ghid * slope).astype(BF)
                term = nt(gpre, w1)
                back = term if back is None else back + term
                for m, grad in enumerate((tn(x, gpre), tn(gated, hid))):
                    if s == 0:
                        outs[0][m] = grad if y == 0 else outs[0][m] + grad
                    elif y < ny - 1:
                        acc[m] = grad if y == 0 else acc[m] + grad
                    else:
                        outs[1][m] = (grad if y == 0 else acc[m] + grad).astype(BF)
            gx[y][...] = back.astype(gx[y].dtype)
            if fused:
                eo[y][...] = part.astype(eo[y].dtype)
                gg[y][...] = jnp.transpose(jnp.broadcast_to(dot, (rows, LANES)))[0:1, :]

    wspec = resident((None, None, width, fs), lambda c: (layer, j, 0, 0))
    rspec = resident((rows, width), lambda c: (0, 0))
    uspec = resident((rows // CAP, None, CAP, width), lambda c: (0, n, 0, 0))
    lspec = resident((1, rows), lambda c: (0, 0))
    gspec = resident((2, width, fs), lambda c: (0, 0, 0))
    parts = [jax.ShapeDtypeStruct((rows, width), F32 if y == 0 else BF) for y in range(ny)]
    shapes = parts + [jax.ShapeDtypeStruct((2, width, fs), F32), jax.ShapeDtypeStruct((2, width, fs), BF)]
    if fused:
        shapes += parts + [jax.ShapeDtypeStruct((1, rows), F32)] * ny
    return pl.pallas_call(
        body,
        grid=(1,),
        in_specs=[rspec] * ny + [uspec] * ny + [wspec] * 4 + [lspec] * (ny if fused else 0),
        out_specs=[rspec] * ny + [gspec] * 2 + ([rspec] * ny + [lspec] * ny if fused else []),
        out_shape=shapes,
        scratch_shapes=[pltpu.VMEM((2, width, fs), F32)],
        compiler_params=params(),
        cost_estimate=cost(
            2 * (24 if fused else 20) * ny * rows * width * fs, 20 * width * fs + 8 * ny * rows * width, 2 * ny * rows * fs
        ),
        name="ffn_backward",
    )(*xs, *gs, *win, *wdown, *(gates if fused else ()))


def store_grads(layer, j, local, own, received, buffers):
    _, width, fs = own.shape
    tile = width // 4

    def body(own_ref, recv_ref, *refs):
        outs = refs[-2:]
        for n in range(2):
            outs[n][...] = own_ref[n] + recv_ref[n].astype(F32)

    pspec = pl.BlockSpec((2, tile, fs), lambda t: (0, t, 0))
    ospec = pl.BlockSpec((None, None, tile, fs), lambda t: (layer, j, t, 0))
    full = jax.ShapeDtypeStruct((2, local, width, fs), F32)
    extra = [] if buffers is None else list(buffers)
    return pl.pallas_call(
        body,
        grid=(4,),
        in_specs=[pspec, pspec] + [pl.BlockSpec(memory_space=pl.ANY)] * len(extra),
        out_specs=[ospec, ospec],
        out_shape=[full, full],
        input_output_aliases={} if buffers is None else {2: 0, 3: 1},
        compiler_params=params(),
        cost_estimate=cost(2 * width * fs, 20 * width * fs, 0),
        name="store_grads",
    )(own, received, *extra)


def rows_shift(count, shift):
    ys = count // 2
    return [(y * 2 + c, ((y + shift) % ys) * 2 + c) for y in range(ys) for c in range(2)]


def spread_rows(mine, count):
    return [mine] + [lax.ppermute(mine, "fsdp", rows_shift(count, s)) for s in range(1, count // 2)]


def return_parts(parts, count):
    return [parts[0]] + [
        lax.ppermute(parts[s], "fsdp", rows_shift(count, -s)) for s in range(1, count // 2)
    ]


def add_parts(parts):
    total = parts[0]
    for part in parts[1:]:
        total = total + part.astype(F32)
    return total.astype(BF)


def step(live, works):
    fresh = dict(live)
    for work in works:
        fresh.update(work(live))
    return lax.optimization_barrier(fresh)


def staged(live, count, stages, extras, pending=()):
    total = count + len(stages) - 1
    waiting = [(0, value) for value in pending]
    for t in range(total):
        works = [
            lambda now, stage=stage, j=t - s: stage(now, j)
            for s, stage in enumerate(stages)
            if 0 <= t - s < count
        ]
        for at, until, work in extras:
            if t == min(at, total - 1):
                if until <= t:
                    works.append(work)
                else:
                    waiting.append((until, work(live)))
        for until, value in waiting:
            if t == until:
                works.append(lambda now, value=value: value)
        live = step(live, works)
    return live, {name: v for until, value in waiting if until >= total for name, v in value.items()}


def exchange(rows):
    return lax.all_to_all(rows, "expert", split_axis=0, concat_axis=0, tiled=True)


def swap_cores(array, count):
    return lax.ppermute(array, "fsdp", [(f, f ^ 1) for f in range(count)])


def shards(tokens_in, routes, valid, qkv_weight, out_weight, router_weight, norm_gain, norm_shift,
           expert_in, expert_down, cotangent):
    owners = lax.axis_size("expert")
    count = lax.axis_size("fsdp")
    local = expert_in.shape[1]
    layers = routes.shape[0]
    tokens, width = tokens_in.shape
    images = tokens // SEQ
    span = owners * CAP
    slots = (local, span)
    experts = router_weight.shape[2]

    packs = []
    for l in range(layers):
        shard = qkv_weight.shape[1]
        pieces = [qkv_weight[l], out_weight[l], router_weight[l], norm_gain[l].T, norm_shift[l].T]
        pieces.append(jnp.zeros((shard, LANES - experts - 4), BF))
        packs.append(jnp.concatenate(pieces, 1))
    win = (expert_in, swap_cores(expert_in, count))
    wdown = (expert_down, swap_cores(expert_down, count))

    def cut(array):
        return array.reshape(array.shape[:-2] + (images, SEQ, array.shape[-1]))

    route_cols = cut(routes)
    pcol, prow = route_places(route_cols, cut(valid), owners, local)
    cot = cut(cotangent)
    top = layers - 1

    def pick(record, *names):
        return {n: record[n] for n in names}

    def swap_y(now, name, out):
        return {out: spread_rows(now[name], count)}

    def send(now, name, out):
        return {out: exchange(now[name])}

    groups = [list(range(j, min(j + 2, local))) for j in range(0, local, 2)]
    where = {j: (g, n) for g, group in enumerate(groups) for n, j in enumerate(group)}
    live = {f"c{g}": rows for g, rows in enumerate(dispatch(cot, prow[top], slots, groups))}
    start = live
    live = step(
        live,
        [
            lambda now: {"pack0": lax.all_gather(packs[0], "fsdp", axis=0, tiled=True)},
        ],
    )
    sending = send(start, "c0", "g0")

    def enter(l):
        def work(now):
            previous = None
            stream = cut(tokens_in)
            if l > 0:
                previous = ([now[f"e{l - 1}_{j}"] for j in range(local)], pcol[l - 1], now[f"gate{l - 1}"])
                stream = now[f"h{l - 1}"]
            pack = now[f"pack{l}"]
            record, sent, rows = block_forward(
                stream, pack, route_cols[l], pcol[l], prow[l], previous, l == top, slots
            )
            out = {f"{name}{l}": value for name, value in record.items() if name != "picks"}
            if l > 0:
                out[f"picks{l - 1}"] = record["picks"]
            for j in range(local):
                out[f"s{l}_{j}"] = sent[j]
            if l == top:
                out["grow"] = rows[0][0:1, :]
            return out

        return work

    def come(l):
        return lambda now, j: send(now, f"s{l}_{j}", f"a{l}_{j}")

    def widen(l):
        return lambda now, j: swap_y(now, f"a{l}_{j}", f"x{l}_{j}")

    def back_y(now, name, out):
        return {out: add_parts(return_parts(now[name], count))}

    early = [j for j in range(local)]
    live["shards"] = packs[1:]
    before = live["shards"]
    live = step(
        live,
        [enter(0), lambda now: sending],
    )
    pending = [{f"pack{l + 1}": lax.all_gather(p, "fsdp", axis=0, tiled=True)} for l, p in enumerate(before)]
    for l in range(top):
        live, unjoined = staged(
            live,
            local,
            [
                come(l),
                widen(l),
                lambda now, j, l=l: {f"p{l}_{j}": ffn_forward(l, j, now[f"x{l}_{j}"], win, wdown)},
                lambda now, j, l=l: back_y(now, f"p{l}_{j}", f"r{l}_{j}"),
                lambda now, j, l=l: send(now, f"r{l}_{j}", f"e{l}_{j}"),
            ],
            [],
            pending if l == 0 else (),
        )
        works = [enter(l + 1)]
        if l + 1 == top:
            works += [lambda now, g=g: send(now, f"c{g}", f"g{g}") for g in range(1, len(groups))]
            works.append(lambda now: swap_y(now, "g0", "gy0"))
        live = step(live, works)

    def send_gates(now):
        rows = now["grow"].reshape(local, owners, CAP).transpose(1, 0, 2).reshape(owners, local * CAP)
        return {"ga": lax.all_to_all(rows, "expert", split_axis=0, concat_axis=0, tiled=True)}

    def widen_gates(now):
        rows = now["ga"].reshape(owners, local, CAP).transpose(1, 0, 2).reshape(local, span)
        return {"gates": spread_rows(rows, count)}

    def fused_rows(now, j):
        gates = [rows[j : j + 1] for rows in now["gates"]]
        ys = count // 2
        g, n = where[j]
        results = ffn_backward(top, j, now[f"x{top}_{j}"], now[f"gy{g}"], n, win, wdown, gates)
        return {
            f"q{top}_{j}": results[:ys],
            f"own{top}_{j}": results[ys],
            f"oth{top}_{j}": results[ys + 1],
            f"f{j}": results[ys + 2 : 2 * ys + 2],
            f"gg{j}": results[2 * ys + 2 :],
        }

    def plain_rows(l):
        def work(now, j):
            ys = count // 2
            gs = [rows.reshape(owners, 1, CAP, width) for rows in now[f"gy{l}_{j}"]]
            results = ffn_backward(l, j, now[f"x{l}_{j}"], gs, 0, win, wdown)
            return {f"q{l}_{j}": results[:ys], f"own{l}_{j}": results[ys], f"oth{l}_{j}": results[ys + 1]}

        return work

    def return_rows(l):
        def work(now, j):
            out = back_y(now, f"q{l}_{j}", f"t{l}_{j}")
            out[f"oth{l}_{j}"] = swap_cores(now[f"oth{l}_{j}"], count)
            return out

        return work

    def leave(l):
        return lambda now, j: send(now, f"t{l}_{j}", f"b{l}_{j}")

    def return_gg(now):
        rows = [jnp.concatenate([now[f"gg{j}"][y] for j in range(local)], 0) for y in range(count // 2)]
        parts = return_parts(rows, count)
        total = parts[0]
        for part in parts[1:]:
            total = total + part
        return {"ggr": total}

    def send_gg(now):
        rows = now["ggr"].reshape(local, owners, CAP).transpose(1, 0, 2).reshape(owners, local * CAP)
        rows = lax.all_to_all(rows, "expert", split_axis=0, concat_axis=0, tiled=True)
        return {"ggs": rows.reshape(owners, local, CAP).transpose(1, 0, 2).reshape(local, span)}

    def keep(l, js):
        def work(now):
            buffers = now.get("buffers")
            for j in js:
                buffers = store_grads(l, j, local, now[f"own{l}_{j}"], now[f"oth{l}_{j}"], buffers)
            return {"buffers": buffers}

        return work

    live, unjoined = staged(
        live,
        local,
        [come(top), widen(top), fused_rows, return_rows(top), leave(top)],
        [(0, 0, send_gates)]
        + [(0, 0, lambda now, g=g: swap_y(now, f"g{g}", f"gy{g}")) for g in range(1, len(groups))]
        + [(1, 1, widen_gates), (local + 2, local + 2, return_gg), (local + 3, local + 3, send_gg)]
        + [(local + 3, local + 3, lambda now, j=j: back_y(now, f"f{j}", f"fr{j}")) for j in early[:2]],
    )

    def scatter_sum(packed):
        return lax.psum_scatter(packed, "fsdp", scatter_dimension=0, tiled=True)

    def gather_all(rows):
        return lax.all_gather(rows, "expert", axis=0, tiled=True)

    def scatter_all(rows):
        return lax.psum_scatter(rows, "expert", scatter_dimension=0, tiled=True)

    def back_block(l):
        def work(now):
            kept = {name: now[f"{name}{l}"] for name in ("x", "h", "qkv", "lse")}
            if l < top:
                kept["picks"] = now[f"picks{l}"]
            below = None if l == 0 else (now[f"gate{l - 1}"], prow[l - 1])
            pack = now[f"pack{l}"]
            named, geo = block_backward(
                cot if l == top else now["grad"], kept, pack, route_cols[l], pcol[l],
                [now[f"b{l}_{j}"] for j in range(local)], now["ggs"] if l == top else None, below, slots
            )
            out = {f"{name}{l}": value for name, value in named.items() if name != "gx"}
            out["grad"] = named["gx"]
            if l > 0:
                for j in range(local):
                    out[f"d{l - 1}_{j}"] = geo[j]
            return out

        return work

    def grads_of(now, l):
        parts = [(now[f"n1{l}"], now[f"gqkv{l}"]), (now[f"a{l}"], now[f"gbr{l}"])]
        return dense_grads(parts, (now[f"n2{l}"], now[f"glog{l}"]), now[f"norms{l}"])

    def stack_eo(now, js):
        return jnp.stack([now[f"fr{j}"].reshape(owners, CAP, width) for j in js], 1)

    def send_eo(js):
        return lambda now: {f"eo{js[0]}": exchange(stack_eo(now, js))}

    live = step(
        live, [back_block(top), send_eo(early[:2])] + [lambda now, j=j: back_y(now, f"f{j}", f"fr{j}") for j in early[2:]]
    )
    for l in reversed(range(top)):
        extras = [(0, 0, lambda now, l=l: {f"dense{l + 1}": grads_of(now, l + 1)[0]})]
        extras += [(local + 2, local + 2, keep(l + 1, early[:1])), (1, 1, keep(l + 1, early[1:]))]
        if l == 0 and local > 2:
            extras.append((local + 3, local + 3, lambda now: {"frs": stack_eo(now, early[2:])}))
        extras.append((1, local - 1, lambda now, l=l: {f"share{l + 1}": scatter_sum(now[f"dense{l + 1}"])}))
        extras.append((local, local + 2, lambda now, l=l: {f"piece{l + 1}": scatter_all(now[f"share{l + 1}"])}))
        extras.append((local + 3, local + 4, lambda now, l=l: {f"full{l + 1}": gather_all(now[f"piece{l + 1}"])}))
        live, unjoined = staged(
            live,
            local,
            [
                lambda now, j, l=l: send(now, f"d{l}_{j}", f"m{l}_{j}"),
                lambda now, j, l=l: swap_y(now, f"m{l}_{j}", f"gy{l}_{j}"),
                plain_rows(l),
                return_rows(l),
                leave(l),
            ],
            extras,
        )

    ys = count // 2
    place = lax.axis_index("fsdp")
    y_at, core_at = place // 2, place % 2
    blocks = (core_at.reshape(1), count)

    def head(now):
        kept = {"h": now["h0"], "picks": now["picks0"]}
        rows = [now[f"b0_{j}"] for j in range(local)]
        named = backward_head(now["grad"], kept, now["pack0"], route_cols[0], pcol[0], rows, slots)
        return {f"{name}0": value for name, value in named.items()}

    def rest(now):
        kept = {name: now[f"{name}0"] for name in ("x", "qkv", "lse")}
        named = backward_rest({"gh": now["gh0"], "gbr": now["gbr0"]}, kept, now["pack0"])
        return {"gqkv0": named["gqkv"], "n10": named["n1"], "norms1st": named["norms"], "grad": named["gx"]}

    def core_swap(tag):
        return lambda now: {f"other{tag}": swap_cores(now[f"other{tag}"], count)}

    def add_cores(now, tag):
        pair = now[f"kept{tag}"].astype(F32) + now[f"other{tag}"].astype(F32)
        now[f"mine{tag}"] = lax.dynamic_index_in_dim(pair, y_at, 0, False)
        now[f"away{tag}"] = [
            lax.dynamic_index_in_dim(pair, (y_at + s) % ys, 0, False).astype(BF) for s in range(1, ys)
        ]

    def swap_dense(tag):
        def work(now):
            rows = zip(range(1, ys), now[f"away{tag}"])
            return {f"near{tag}": [lax.ppermute(r, "fsdp", rows_shift(count, s)) for s, r in rows]}

        return work

    def add_near(now, tag):
        total = now[f"mine{tag}"]
        for rows in now[f"near{tag}"]:
            total = total + rows.astype(F32)
        now[f"mine{tag}"] = total.astype(BF).reshape(owners, total.shape[0] // owners, total.shape[1])

    def add_far(now, tag):
        total = jnp.sum(now[f"mine{tag}"].astype(F32), 0).astype(BF)
        now[f"mine{tag}"] = jnp.broadcast_to(total[None], (owners,) + total.shape)

    def finish(now):
        eo = [now[f"eo{j}"] for j in early if f"eo{j}" in now]
        return {"out": combine_last(now[f"h{top}"], eo, pcol[top], now[f"gate{top}"])}

    later = send(live, "frs", "eo2") if local > 2 else {}
    live = step(live, [head])
    live["keptA"], live["otherA"] = dense_grads(
        [(live["a0"], live["gbr0"])], (live["n20"], live["glog0"]), live["norms0"], blocks
    )
    live = step(live, [core_swap("A"), rest, lambda now: unjoined])
    add_cores(live, "A")

    def grads_q(now):
        kept, other = dense_grads([(now["n10"], now["gqkv0"])], None, now["norms1st"], blocks)
        return {"keptQ": kept, "otherQ": other}

    live = step(live, [swap_dense("A"), grads_q])
    add_near(live, "A")
    apart = dict(live)
    live = step(live, [core_swap("Q"), lambda now: later])
    apart.update(send(apart, "mineA", "mineA"))
    add_far(apart, "A")
    apart = send(apart, "mineA", "mineA")
    add_cores(live, "Q")
    live = step(live, [swap_dense("Q"), lambda now: apart, keep(0, early[:2])])
    add_near(live, "Q")
    live = step(live, [lambda now: send(now, "mineQ", "mineQ"), keep(0, early[2:]), finish])
    add_far(live, "Q")
    live["grad"] = live["grad"].reshape(tokens, width)
    live["out"] = live["out"].reshape(tokens, width)
    height = width // count
    at = 4 * width + experts
    rest_of = [live[f"full{l}"] for l in range(1, layers)]

    def together(first, begin, end):
        return jnp.stack([first.astype(F32)] + [rows[:, begin:end].astype(F32) for rows in rest_of])

    def unpack(now):
        soon = now["mineA"].reshape(height, width + LANES)
        return {
            "g_out": together(soon[:, :width], 3 * width, 4 * width),
            "g_router": together(soon[:, width : width + experts], 4 * width, at),
            "g_norms": together(soon[:, width + experts : width + experts + 4], at, at + 4),
        }

    live = step(live, [lambda now: send(now, "mineQ", "mineQ"), unpack])
    out = live["out"]
    buffers = live["buffers"]
    grad = live["grad"]
    late = live["mineQ"].reshape(height, 3 * width + LANES)
    norms = live["g_norms"].at[0].add(late[:, 3 * width + experts : 3 * width + experts + 4].astype(F32))
    norms = jnp.swapaxes(norms, 1, 2)
    return (
        out,
        grad,
        together(late[:, : 3 * width], 0, 3 * width),
        live["g_out"],
        live["g_router"],
        norms[:, :2],
        norms[:, 2:],
        buffers[0],
        buffers[1],
    )


def solution(mesh):
    everyone = ("expert", "fsdp")
    return jax.shard_map(
        shards,
        mesh=mesh,
        in_specs=(
            P(everyone, None),
            P(None, everyone, None),
            P(None, everyone, None),
            P(None, "fsdp", None),
            P(None, "fsdp", None),
            P(None, "fsdp", None),
            P(None, None, "fsdp"),
            P(None, None, "fsdp"),
            P(None, "expert", None, "fsdp"),
            P(None, "expert", None, "fsdp"),
            P(everyone, None),
        ),
        out_specs=(
            P(everyone, None),
            P(everyone, None),
            P(None, "fsdp", None),
            P(None, "fsdp", None),
            P(None, "fsdp", None),
            P(None, None, "fsdp"),
            P(None, None, "fsdp"),
            P(None, "expert", None, "fsdp"),
            P(None, "expert", None, "fsdp"),
        ),
        check_vma=False,
    )
```

```python
import jax
import jax.numpy as jnp
from jax import lax
from jax.experimental import pallas as pl
from jax.experimental.pallas import tpu as pltpu
from jax.sharding import PartitionSpec as P

HEADS = 12
HEAD = 64
SEQ = 197
SEQ_PAD = 256
CAP = 64
LANES = 128
BF = jnp.bfloat16
F32 = jnp.float32
EPS = 1e-06
GELU = 0.7978845608028654
CUBE = 0.044715
VMEM_LIMIT = 56 << 20
NEG = -1e30


def nn(left, right):
    return lax.dot_general(left, right, (((1,), (0,)), ((), ())), preferred_element_type=F32)


def nt(left, right):
    return lax.dot_general(left, right, (((1,), (1,)), ((), ())), preferred_element_type=F32)


def tn(left, right):
    return lax.dot_general(left, right, (((0,), (0,)), ((), ())), preferred_element_type=F32)


def gelu(u):
    return 0.5 * u * (1.0 + jnp.tanh(GELU * (u + CUBE * u * u * u)))


def gelu_both(u):
    square = u * u
    t = jnp.tanh(GELU * u * (1.0 + CUBE * square))
    half = 0.5 * (1.0 + t)
    return u * half, half + 0.5 * u * (1.0 - t * t) * (GELU * (1.0 + 3.0 * CUBE * square))


def normalise(v):
    centred = v - jnp.mean(v, -1, keepdims=True)
    inv = lax.rsqrt(jnp.mean(centred * centred, -1, keepdims=True) + EPS)
    return centred * inv, inv


def norm_pull(grad, hat, inv, gain):
    scaled = grad * gain
    pulled = inv * (
        scaled
        - jnp.mean(scaled, -1, keepdims=True)
        - hat * jnp.mean(scaled * hat, -1, keepdims=True)
    )
    return pulled, jnp.sum(grad * hat, 0, keepdims=True), jnp.sum(grad, 0, keepdims=True)


def resident(shape, index):
    return pl.BlockSpec(shape, index, pipeline_mode=pl.Buffered(1))


def fixed(array):
    zeros = (0,) * array.ndim
    return resident(array.shape, lambda i: zeros)


def per_image(*tail):
    zeros = (0,) * len(tail)
    return pl.BlockSpec((None,) + tail, lambda i: (i,) + zeros)


def cost(flops, byte_count, exps):
    return pl.CostEstimate(
        flops=int(flops), bytes_accessed=int(byte_count), transcendentals=int(exps)
    )


def params():
    return pltpu.CompilerParams(vmem_limit_bytes=VMEM_LIMIT)


def lanes(shape):
    return lax.broadcasted_iota(jnp.int32, shape, 1)


def pick_rows(columns, slots, start):
    hit = lanes((columns[0].shape[0], slots)) == columns[0] - start
    for column in columns[1:]:
        hit = hit | (lanes((column.shape[0], slots)) == column - start)
    return jnp.where(hit, 1.0, 0.0).astype(BF)


def place_rows(rows, slots, start):
    sub = lax.broadcasted_iota(jnp.int32, (slots, rows[0].shape[1]), 0)
    hit = sub == rows[0] - start
    for row in rows[1:]:
        hit = hit | (sub == row - start)
    return jnp.where(hit, 1.0, 0.0).astype(BF)


def norm_rows(pack_ref, width):
    tail = pack_ref[:, 4 * width :].astype(F32)
    return jnp.transpose(tail)


def block_forward(stream, pack, routes, pcol, prow, previous, want_rows, slots):
    images, seq, width = stream.shape
    chunks = 4 * width
    local = slots[0]
    span = slots[1]
    has_prev = previous is not None
    inputs = [stream, pack, routes, pcol, prow]
    specs = [per_image(seq, width), fixed(pack), per_image(seq, 2), per_image(seq, 2), fixed(prow)]
    if has_prev:
        inputs += [previous[0], previous[1], previous[2], *previous[3]]
        specs += [fixed(previous[0]), per_image(seq, 2), per_image(seq, 2), per_image(seq, width), per_image(seq, width)]
    shapes, ospecs = [], []

    def out(shape, dtype, spec):
        shapes.append(jax.ShapeDtypeStruct(shape, dtype))
        ospecs.append(spec)

    out((images, seq, 3 * width), BF, per_image(seq, 3 * width))
    out((images, 16, seq), F32, per_image(16, seq))
    out((images, seq, width), BF, per_image(seq, width))
    out((images, seq, width), F32, per_image(seq, width))
    out((images, seq, 2), F32, per_image(seq, 2))
    if has_prev:
        out((images, seq, width), F32, per_image(seq, width))
        out((images, seq, width), BF, per_image(seq, width))
        out((images, seq, width), BF, per_image(seq, width))
    out((span, width), BF, resident((span, width), lambda i: (0, 0)))
    out((images * SEQ_PAD, width), BF, resident((images * SEQ_PAD, width), lambda i: (0, 0)))
    if want_rows:
        out((8, local * span), F32, resident((8, local * span), lambda i: (0, 0)))
    scratch = [pltpu.VMEM((LANES, width), F32)]

    def body(*refs):
        refs = list(refs)
        x_ref, pack_ref, routes_ref, pcol_ref, prow_ref = refs[:5]
        at = 5
        if has_prev:
            eo_ref, old_pcol_ref, old_gate_ref, *part_refs = refs[at : at + 5]
            at += 5
        qkv_ref, lse_ref, a_ref, h_ref, gate_ref = refs[at : at + 5]
        at += 5
        if has_prev:
            xs_ref, pick0_ref, pick1_ref = refs[at : at + 3]
            at += 3
        disp_ref, store = refs[at : at + 2]
        at += 2
        if want_rows:
            grow_ref = refs[at]
        norm_ref = refs[-1]
        i = pl.program_id(0)

        @pl.when(i == 0)
        def _():
            norm_ref[...] = norm_rows(pack_ref, width)
            store[...] = jnp.zeros_like(store)
            if want_rows:
                grow_ref[...] = jnp.zeros_like(grow_ref)

        x = x_ref[...].astype(F32)
        if has_prev:
            for k, pick_ref in enumerate((pick0_ref, pick1_ref)):
                hot = pick_rows([old_pcol_ref[:, k : k + 1]], span, (local - 1) * span)
                picked = part_refs[k][...].astype(F32) + nn(hot, eo_ref[...])
                pick_ref[...] = picked.astype(BF)
                x = x + old_gate_ref[:, k : k + 1] * picked
            xs_ref[...] = x
        hat, _ = normalise(x)
        n1 = (hat * norm_ref[32:33, :] + norm_ref[34:35, :]).astype(BF)
        for c in range(3):
            qkv_ref[:, c * width : (c + 1) * width] = nn(
                n1, pack_ref[:, c * width : (c + 1) * width]
            ).astype(BF)
        lane = lanes((seq, LANES))
        lse_ref[...] = jnp.zeros_like(lse_ref)
        for pair in range(HEADS // 2):
            lo = pair * LANES
            q = qkv_ref[:, lo : lo + LANES]
            k = qkv_ref[:, width + lo : width + lo + LANES]
            v = qkv_ref[:, 2 * width + lo : 2 * width + lo + LANES]
            parts = []
            for half in range(2):
                mine = (lane < HEAD) if half == 0 else (lane >= HEAD)
                scores = nt(k, jnp.where(mine, q, jnp.zeros_like(q))) * HEAD ** (-0.5)
                top = jnp.max(scores, 0, keepdims=True)
                weights = jnp.exp(scores - top)
                total = jnp.sum(weights, 0, keepdims=True)
                lse_ref[2 * pair + half : 2 * pair + half + 1, :] = top + jnp.log(total)
                probs = (weights * (1.0 / total)).astype(BF)
                parts.append(tn(probs, v))
            a_ref[:, lo : lo + LANES] = jnp.where(lane < HEAD, parts[0], parts[1]).astype(BF)
        h = x + nn(a_ref[...], pack_ref[:, 3 * width : 4 * width])
        h_ref[...] = h
        hat, _ = normalise(h)
        n2 = (hat * norm_ref[33:34, :] + norm_ref[35:36, :]).astype(BF)
        logits = nn(n2, pack_ref[:, chunks : chunks + LANES])
        logits = jnp.where(lane < 32, logits, NEG)
        weights = jnp.exp(logits - jnp.max(logits, -1, keepdims=True))
        probs = weights / jnp.sum(weights, -1, keepdims=True)
        gates = []
        for k in range(2):
            chosen = jnp.where(lane == routes_ref[:, k : k + 1], probs, 0.0)
            kept = jnp.where(pcol_ref[:, k : k + 1] >= 0, 1.0, 0.0)
            gates.append(jnp.sum(chosen, -1, keepdims=True) * kept)
            gate_ref[:, k : k + 1] = gates[k]
        store[pl.ds(pl.multiple_of(i * SEQ_PAD, SEQ_PAD), seq), :] = n2
        if want_rows:
            where = lanes((seq, local * span))
            spread = [jnp.where(where == pcol_ref[:, k : k + 1], gates[k], 0.0) for k in range(2)]
            grow_ref[0:1, :] += jnp.sum(spread[0] + spread[1], 0, keepdims=True)

        @pl.when(i == images - 1)
        def _():
            rows = [prow_ref[0:1, :], prow_ref[1:2, :]]
            disp_ref[...] = nn(place_rows(rows, span, 0), store[...]).astype(BF)

    tokens = images * seq
    flops = 2 * tokens * width * (4 * width + 128) + 4 * HEADS * tokens * 256 * 128
    flops += 2 * (1 + 2 * has_prev) * span * tokens * width
    results = pl.pallas_call(
        body,
        grid=(images,),
        in_specs=specs,
        out_specs=ospecs,
        out_shape=shapes,
        scratch_shapes=scratch,
        compiler_params=params(),
        cost_estimate=cost(2 * flops, 20 * tokens * width, HEADS * tokens * seq),
        name="block_forward",
    )(*inputs)
    kept = dict(zip(("qkv", "lse", "a", "h", "gate"), results[:5]))
    rest = results[5:]
    kept["x"] = stream
    if has_prev:
        kept["x"] = rest[0]
        kept["picks"] = (rest[1], rest[2])
        rest = rest[3:]
    return kept, rest[0], rest[1], rest[2:]


def place_chunks(stores, prow, experts, span):
    width = stores[0].shape[1]

    def body(prow_ref, *refs):
        ins, outs = refs[: len(stores)], refs[len(stores) :]
        rows = [prow_ref[0:1, :], prow_ref[1:2, :]]
        for out, j in zip(outs, experts):
            if len(stores) == 1:
                value = nn(place_rows(rows, span, j * span), ins[0][...])
            else:
                value = nn(place_rows(rows[:1], span, j * span), ins[0][...])
                value = value + nn(place_rows(rows[1:], span, j * span), ins[1][...])
            out[...] = value.astype(BF)

    whole = resident((span, width), lambda i: (0, 0))
    work = len(experts) * len(stores) * span * stores[0].shape[0] * width
    return pl.pallas_call(
        body,
        grid=(1,),
        in_specs=[fixed(prow)] + [fixed(a) for a in stores],
        out_specs=[whole] * len(experts),
        out_shape=[jax.ShapeDtypeStruct((span, width), BF)] * len(experts),
        compiler_params=params(),
        cost_estimate=cost(4 * work, 4 * len(experts) * span * width, 0),
        name="place_chunks",
    )(prow, *stores)


def pick_chunks(expert_rows, pcol, summed):
    images, seq, _ = pcol.shape
    span, width = expert_rows[0].shape
    count = len(expert_rows)

    def body(pcol_ref, *refs):
        ins, outs = refs[:count], refs[count:]
        columns = [pcol_ref[:, 0:1], pcol_ref[:, 1:2]]
        for out, wanted in zip(outs, [columns] if summed else [columns[:1], columns[1:]]):
            total = None
            for j in range(count):
                term = nn(pick_rows(wanted, span, j * span), ins[j][...])
                total = term if total is None else total + term
            out[...] = total.astype(out.dtype)

    shape = jax.ShapeDtypeStruct((images, seq, width), F32 if summed else BF)
    outs = 1 if summed else 2
    return pl.pallas_call(
        body,
        grid=(images,),
        in_specs=[per_image(seq, 2)] + [fixed(a) for a in expert_rows],
        out_specs=[per_image(seq, width)] * outs,
        out_shape=[shape] * outs,
        compiler_params=params(),
        cost_estimate=cost(4 * outs * count * span * images * seq * width, 4 * count * span * width, 0),
        name="pick_chunks",
    )(pcol, *expert_rows)


def dispatch(rows, prow, slots, groups):
    images, seq, width = rows.shape
    span = slots[1]
    owners = span // CAP

    def body(rows_ref, prow_ref, *refs):
        outs, store = refs[:-1], refs[-1]
        store[...] = jnp.zeros_like(store)
        for i in range(images):
            store[i * SEQ_PAD : i * SEQ_PAD + seq, :] = rows_ref[i]
        for out, group in zip(outs, groups):
            for n, j in enumerate(group):
                hot = place_rows([prow_ref[0:1, :], prow_ref[1:2, :]], span, j * span)
                out[:, n] = nn(hot, store[...]).astype(BF).reshape(owners, CAP, width)

    shapes = [(owners, len(group), CAP, width) for group in groups]
    return pl.pallas_call(
        body,
        grid=(1,),
        in_specs=[fixed(rows), fixed(prow)],
        out_specs=[resident(shape, lambda i: (0, 0, 0, 0)) for shape in shapes],
        out_shape=[jax.ShapeDtypeStruct(shape, BF) for shape in shapes],
        scratch_shapes=[pltpu.VMEM((images * SEQ_PAD, width), BF)],
        compiler_params=params(),
        cost_estimate=cost(4 * slots[0] * span * images * seq * width, 8 * slots[0] * span * width, 0),
        name="dispatch",
    )(rows, prow)


def route_places(routes, valid, owners, local):
    layers, images, seq, _ = routes.shape

    def body(routes_ref, valid_ref, pcol_ref, prow_ref):
        prow_ref[...] = jnp.full(prow_ref.shape, -1, jnp.int32)
        lane = lanes((seq, LANES))
        below = lax.broadcasted_iota(jnp.int32, (seq, seq), 0) > lanes((seq, seq))
        below = jnp.where(below, 1.0, 0.0).astype(BF)
        base = jnp.zeros((1, LANES), F32)
        for i in range(images):
            hot = [jnp.where(lane == routes_ref[i, :, k : k + 1], 1.0, 0.0) for k in range(2)]
            both = hot[0] + hot[1]
            earlier = nn(below, both.astype(BF)) + base
            base = base + jnp.sum(both, 0, keepdims=True)
            columns = jnp.full((seq, LANES), -1.0, F32)
            for k in range(2):
                slot = jnp.sum(hot[k] * earlier, -1, keepdims=True)
                expert = routes_ref[i, :, k : k + 1]
                owner = expert // local
                start = ((expert - owner * local) * owners + owner) * CAP
                place = jnp.where(valid_ref[i, :, k : k + 1] > 0, start.astype(F32) + slot, -1.0)
                pcol_ref[i, :, k : k + 1] = place.astype(jnp.int32)
                columns = jnp.where(lane == k, place, columns)
            padded = jnp.concatenate([columns, jnp.full((SEQ_PAD - seq, LANES), -1.0, F32)], 0)
            prow_ref[:, i * SEQ_PAD : (i + 1) * SEQ_PAD] = jnp.transpose(padded)[0:8, :].astype(jnp.int32)

    spec = pl.BlockSpec((None, images, seq, 2), lambda l: (l, 0, 0, 0))
    return pl.pallas_call(
        body,
        grid=(layers,),
        in_specs=[spec, spec],
        out_specs=[spec, pl.BlockSpec((None, 8, images * SEQ_PAD), lambda l: (l, 0, 0))],
        out_shape=[
            jax.ShapeDtypeStruct((layers, images, seq, 2), jnp.int32),
            jax.ShapeDtypeStruct((layers, 8, images * SEQ_PAD), jnp.int32),
        ],
        compiler_params=params(),
        cost_estimate=cost(2 * layers * images * seq * seq * LANES, 1 << 20, 0),
        name="route_places",
    )(routes, valid)


def combine_last(h, expert_rows, pcol, gate):
    images, seq, width = h.shape
    owners = expert_rows[0].shape[0]
    span = owners * CAP
    where = [(a, n) for a, array in enumerate(expert_rows) for n in range(array.shape[1])]
    local = len(where)

    def body(h_ref, pcol_ref, gate_ref, *refs):
        eo_refs, out_ref = refs[:-1], refs[-1]
        x = h_ref[...]
        for k in range(2):
            picked = None
            for j in range(local):
                rows = eo_refs[where[j][0]][:, where[j][1]].reshape(span, width)
                term = nn(pick_rows([pcol_ref[:, k : k + 1]], span, j * span), rows)
                picked = term if picked is None else picked + term
            x = x + gate_ref[:, k : k + 1] * picked
        out_ref[...] = x.astype(BF)

    return pl.pallas_call(
        body,
        grid=(images,),
        in_specs=[per_image(seq, width), per_image(seq, 2), per_image(seq, 2)]
        + [fixed(a) for a in expert_rows],
        out_specs=per_image(seq, width),
        out_shape=jax.ShapeDtypeStruct((images, seq, width), BF),
        compiler_params=params(),
        cost_estimate=cost(8 * local * span * images * seq * width, 20 * images * seq * width, 0),
        name="combine_last",
    )(h, pcol, gate, *expert_rows)


def block_backward(grad, kept, pack, routes, pcol, expert_grads, gate_grads, below, slots):
    images, seq, width = grad.shape
    local, span = slots
    has_below = below is not None
    has_gg = gate_grads is not None
    row3, row2 = per_image(seq, width), per_image(seq, 2)
    inputs = [grad, kept["x"], kept["h"], kept["qkv"], kept["lse"], pack, routes, pcol]
    specs = [row3, row3, row3, per_image(seq, 3 * width), per_image(16, seq), fixed(pack), row2, row2]
    inputs += list(expert_grads)
    specs += [row3, fixed(expert_grads[1])]
    if has_gg:
        inputs.append(gate_grads)
        specs.append(fixed(gate_grads))
    else:
        inputs += list(kept["picks"])
        specs += [row3, row3]
    if has_below:
        inputs += [below[0], below[1]]
        specs += [row2, fixed(below[1])]
    shapes, ospecs = [], []

    def out(shape, dtype, spec):
        shapes.append(jax.ShapeDtypeStruct(shape, dtype))
        ospecs.append(spec)

    out((images, seq, width), F32, row3)
    out((images, seq, width), BF, row3)
    out((images, seq, 3 * width), BF, per_image(seq, 3 * width))
    out((images, seq, width), BF, row3)
    out((images, seq, width), BF, row3)
    out((images, seq, LANES), BF, per_image(seq, LANES))
    out((8, width), F32, resident((8, width), lambda i: (0, 0)))
    if has_below:
        for rows in (span, images * SEQ_PAD, images * SEQ_PAD):
            out((rows, width), BF, resident((rows, width), lambda i: (0, 0)))
    scratch = [pltpu.VMEM((LANES, width), F32), pltpu.VMEM((seq, width), BF)]

    def body(*refs):
        refs = list(refs)
        grad_ref, x_ref, h_ref, qkv_ref, lse_ref, pack_ref, routes_ref, pcol_ref = refs[:8]
        at = 8
        part_ref, gbuf_ref = refs[at : at + 2]
        at += 2
        if has_gg:
            gg_ref = refs[at]
            at += 1
        else:
            pick_refs = refs[at : at + 2]
            at += 2
        if has_below:
            below_gate_ref, below_prow_ref = refs[at : at + 2]
            at += 2
        gx_ref, gbr_ref, gqkv_ref, n1_ref, n2_ref, glog_ref, norms_ref = refs[at : at + 7]
        at += 7
        if has_below:
            geo_ref, *stores = refs[at : at + 3]
        norm_ref, ga_ref = refs[-2:]
        i = pl.program_id(0)

        @pl.when(i == 0)
        def _():
            norm_ref[...] = norm_rows(pack_ref, width)
            norms_ref[...] = jnp.zeros_like(norms_ref)
            if has_below:
                for store in stores:
                    store[...] = jnp.zeros_like(store)

        lane = lanes((seq, LANES))
        gy = grad_ref[...].astype(F32)
        columns = [pcol_ref[:, 0:1], pcol_ref[:, 1:2]]
        gn2 = part_ref[...] + nn(pick_rows(columns, span, (local - 1) * span), gbuf_ref[...])
        hat2, inv2 = normalise(h_ref[...])
        gain2 = norm_ref[33:34, :]
        n2 = (hat2 * gain2 + norm_ref[35:36, :]).astype(BF)
        n2_ref[...] = n2
        router = pack_ref[:, 4 * width : 4 * width + LANES]
        logits = jnp.where(lane < 32, nn(n2, router), NEG)
        weights = jnp.exp(logits - jnp.max(logits, -1, keepdims=True))
        probs = weights / jnp.sum(weights, -1, keepdims=True)
        gr = jnp.zeros_like(probs)
        for k in range(2):
            if has_gg:
                gg = 0.0
                for j in range(local):
                    hit = lanes((seq, span)) == columns[k] - j * span
                    gg = gg + jnp.sum(jnp.where(hit, gg_ref[j : j + 1, :], 0.0), -1, keepdims=True)
            else:
                gg = jnp.sum(gy * pick_refs[k][...].astype(F32), -1, keepdims=True)
            gg = jnp.where(columns[k] >= 0, gg, 0.0)
            gr = gr + jnp.where(lane == routes_ref[:, k : k + 1], gg, 0.0)
        glog = (probs * (gr - jnp.sum(probs * gr, -1, keepdims=True))).astype(BF)
        glog_ref[...] = glog
        gn2 = gn2 + nt(glog, jnp.where(lanes((width, LANES)) < 32, router, jnp.zeros_like(router)))
        pulled, ggain2, gshift2 = norm_pull(gn2, hat2, inv2, gain2)
        gh = gy + pulled
        gbr = gh.astype(BF)
        gbr_ref[...] = gbr
        ga_ref[...] = nt(gbr, pack_ref[:, 3 * width : 4 * width]).astype(BF)
        scale = HEAD ** (-0.5)
        for pair in range(HEADS // 2):
            lo = pair * LANES
            q = qkv_ref[:, lo : lo + LANES]
            k = qkv_ref[:, width + lo : width + lo + LANES]
            v = qkv_ref[:, 2 * width + lo : 2 * width + lo + LANES]
            ga = ga_ref[:, lo : lo + LANES]
            gq, gk, gv = None, None, None
            for half in range(2):
                mine = (lane < HEAD) if half == 0 else (lane >= HEAD)
                zero = jnp.zeros_like(q)
                qm, km, gam = jnp.where(mine, q, zero), jnp.where(mine, k, zero), jnp.where(mine, ga, zero)
                scores = nt(k, qm) * scale
                p = jnp.exp(scores - lse_ref[2 * pair + half : 2 * pair + half + 1, :])
                gp = nt(v, gam)
                gs = (p * (gp - jnp.sum(p * gp, 0, keepdims=True))).astype(BF)
                tv = nn(p.astype(BF), gam)
                tk = nn(gs, qm)
                tq = tn(gs, km)
                gq = tq if gq is None else gq + tq
                gk = tk if gk is None else gk + tk
                gv = tv if gv is None else gv + tv
            gqkv_ref[:, lo : lo + LANES] = (gq * scale).astype(BF)
            gqkv_ref[:, width + lo : width + lo + LANES] = (gk * scale).astype(BF)
            gqkv_ref[:, 2 * width + lo : 2 * width + lo + LANES] = gv.astype(BF)
        gn1 = nt(gqkv_ref[:, 0:width], pack_ref[:, 0:width])
        for c in range(1, 3):
            gn1 = gn1 + nt(gqkv_ref[:, c * width : (c + 1) * width], pack_ref[:, c * width : (c + 1) * width])
        hat1, inv1 = normalise(x_ref[...].astype(F32))
        gain1 = norm_ref[32:33, :]
        n1_ref[...] = (hat1 * gain1 + norm_ref[34:35, :]).astype(BF)
        pulled, ggain1, gshift1 = norm_pull(gn1, hat1, inv1, gain1)
        gx = gh + pulled
        gx_ref[...] = gx
        for r, row in enumerate((ggain1, ggain2, gshift1, gshift2)):
            norms_ref[r : r + 1, :] += row
        if has_below:
            at_row = pl.multiple_of(i * SEQ_PAD, SEQ_PAD)
            for k in range(2):
                stores[k][pl.ds(at_row, seq), :] = (below_gate_ref[:, k : k + 1] * gx).astype(BF)

            @pl.when(i == images - 1)
            def _():
                geo_ref[...] = (
                    nn(place_rows([below_prow_ref[0:1, :]], span, 0), stores[0][...])
                    + nn(place_rows([below_prow_ref[1:2, :]], span, 0), stores[1][...])
                ).astype(BF)

    tokens = images * seq
    flops = 2 * tokens * width * (4 * width + 256) + 10 * HEADS * tokens * 256 * 128
    flops += 2 * (1 + 2 * has_below) * span * tokens * width
    results = pl.pallas_call(
        body,
        grid=(images,),
        in_specs=specs,
        out_specs=ospecs,
        out_shape=shapes,
        scratch_shapes=scratch,
        compiler_params=params(),
        cost_estimate=cost(2 * flops, 30 * tokens * width, HEADS * tokens * seq),
        name="block_backward",
    )(*inputs)
    named = dict(zip(("gx", "gbr", "gqkv", "n1", "n2", "glog", "norms"), results[:7]))
    return named, results[7:]


def backward_head(grad, kept, pack, routes, pcol, expert_grads, slots):
    images, seq, width = grad.shape
    local, span = slots
    has_gg = False
    row3, row2 = per_image(seq, width), per_image(seq, 2)
    inputs = [grad, kept["h"], pack, routes, pcol] + list(expert_grads) + list(kept["picks"])
    specs = [row3, row3, fixed(pack), row2, row2, row3, fixed(expert_grads[1]), row3, row3]

    def body(grad_ref, h_ref, pack_ref, routes_ref, pcol_ref, *refs):
        part_ref, gbuf_ref, *pick_refs = refs[:4]
        gh_ref, gbr_ref, n2_ref, glog_ref, norms_ref, norm_ref = refs[4:]
        gg_ref = None
        i = pl.program_id(0)

        @pl.when(i == 0)
        def _():
            norm_ref[...] = norm_rows(pack_ref, width)
            norms_ref[...] = jnp.zeros_like(norms_ref)

        lane = lanes((seq, LANES))
        gy = grad_ref[...].astype(F32)
        columns = [pcol_ref[:, 0:1], pcol_ref[:, 1:2]]
        gn2 = part_ref[...] + nn(pick_rows(columns, span, (local - 1) * span), gbuf_ref[...])
        hat2, inv2 = normalise(h_ref[...])
        gain2 = norm_ref[33:34, :]
        n2 = (hat2 * gain2 + norm_ref[35:36, :]).astype(BF)
        n2_ref[...] = n2
        router = pack_ref[:, 4 * width : 4 * width + LANES]
        logits = jnp.where(lane < 32, nn(n2, router), NEG)
        weights = jnp.exp(logits - jnp.max(logits, -1, keepdims=True))
        probs = weights / jnp.sum(weights, -1, keepdims=True)
        gr = jnp.zeros_like(probs)
        for k in range(2):
            if has_gg:
                gg = 0.0
                for j in range(local):
                    hit = lanes((seq, span)) == columns[k] - j * span
                    gg = gg + jnp.sum(jnp.where(hit, gg_ref[j : j + 1, :], 0.0), -1, keepdims=True)
            else:
                gg = jnp.sum(gy * pick_refs[k][...].astype(F32), -1, keepdims=True)
            gg = jnp.where(columns[k] >= 0, gg, 0.0)
            gr = gr + jnp.where(lane == routes_ref[:, k : k + 1], gg, 0.0)
        glog = (probs * (gr - jnp.sum(probs * gr, -1, keepdims=True))).astype(BF)
        glog_ref[...] = glog
        gn2 = gn2 + nt(glog, jnp.where(lanes((width, LANES)) < 32, router, jnp.zeros_like(router)))
        pulled, ggain2, gshift2 = norm_pull(gn2, hat2, inv2, gain2)
        gh = gy + pulled
        gbr = gh.astype(BF)
        gbr_ref[...] = gbr
        gh_ref[...] = gh
        norms_ref[1:2, :] += ggain2
        norms_ref[3:4, :] += gshift2

    tokens = images * seq
    whole = resident((8, width), lambda i: (0, 0))
    wide = jax.ShapeDtypeStruct((images, seq, width), BF)
    results = pl.pallas_call(
        body,
        grid=(images,),
        in_specs=specs,
        out_specs=[row3, row3, row3, per_image(seq, LANES), whole],
        out_shape=[
            jax.ShapeDtypeStruct((images, seq, width), F32), wide, wide,
            jax.ShapeDtypeStruct((images, seq, LANES), BF), jax.ShapeDtypeStruct((8, width), F32),
        ],
        scratch_shapes=[pltpu.VMEM((LANES, width), F32)],
        compiler_params=params(),
        cost_estimate=cost(4 * local * span * tokens * width, 20 * tokens * width, tokens * LANES),
        name="backward_head",
    )(*inputs)
    return dict(zip(("gh", "gbr", "n2", "glog", "norms"), results))


def backward_rest(head, kept, pack):
    images, seq, width = head["gh"].shape
    row3, row9 = per_image(seq, width), per_image(seq, 3 * width)

    def body(gh_ref, gbr_ref, x_ref, qkv_ref, lse_ref, pack_ref, gx_ref, gqkv_ref, n1_ref, norms_ref, norm_ref, ga_ref):
        i = pl.program_id(0)

        @pl.when(i == 0)
        def _():
            norm_ref[...] = norm_rows(pack_ref, width)
            norms_ref[...] = jnp.zeros_like(norms_ref)

        lane = lanes((seq, LANES))
        ga_ref[...] = nt(gbr_ref[...], pack_ref[:, 3 * width : 4 * width]).astype(BF)
        scale = HEAD ** (-0.5)
        for pair in range(HEADS // 2):
            lo = pair * LANES
            q = qkv_ref[:, lo : lo + LANES]
            k = qkv_ref[:, width + lo : width + lo + LANES]
            v = qkv_ref[:, 2 * width + lo : 2 * width + lo + LANES]
            ga = ga_ref[:, lo : lo + LANES]
            gq, gk, gv = None, None, None
            for half in range(2):
                mine = (lane < HEAD) if half == 0 else (lane >= HEAD)
                zero = jnp.zeros_like(q)
                qm, km, gam = jnp.where(mine, q, zero), jnp.where(mine, k, zero), jnp.where(mine, ga, zero)
                scores = nt(k, qm) * scale
                p = jnp.exp(scores - lse_ref[2 * pair + half : 2 * pair + half + 1, :])
                gp = nt(v, gam)
                gs = (p * (gp - jnp.sum(p * gp, 0, keepdims=True))).astype(BF)
                tv = nn(p.astype(BF), gam)
                tk = nn(gs, qm)
                tq = tn(gs, km)
                gq = tq if gq is None else gq + tq
                gk = tk if gk is None else gk + tk
                gv = tv if gv is None else gv + tv
            gqkv_ref[:, lo : lo + LANES] = (gq * scale).astype(BF)
            gqkv_ref[:, width + lo : width + lo + LANES] = (gk * scale).astype(BF)
            gqkv_ref[:, 2 * width + lo : 2 * width + lo + LANES] = gv.astype(BF)
        gn1 = nt(gqkv_ref[:, 0:width], pack_ref[:, 0:width])
        for c in range(1, 3):
            gn1 = gn1 + nt(gqkv_ref[:, c * width : (c + 1) * width], pack_ref[:, c * width : (c + 1) * width])
        hat1, inv1 = normalise(x_ref[...].astype(F32))
        gain1 = norm_ref[32:33, :]
        n1_ref[...] = (hat1 * gain1 + norm_ref[34:35, :]).astype(BF)
        pulled, ggain1, gshift1 = norm_pull(gn1, hat1, inv1, gain1)
        gx_ref[...] = gh_ref[...] + pulled
        norms_ref[0:1, :] += ggain1
        norms_ref[2:3, :] += gshift1

    tokens = images * seq
    flops = 2 * tokens * width * 4 * width + 10 * HEADS * tokens * 256 * 128
    results = pl.pallas_call(
        body,
        grid=(images,),
        in_specs=[row3, row3, row3, row9, per_image(16, seq), fixed(pack)],
        out_specs=[row3, row9, row3, resident((8, width), lambda i: (0, 0))],
        out_shape=[
            jax.ShapeDtypeStruct((images, seq, width), F32),
            jax.ShapeDtypeStruct((images, seq, 3 * width), BF),
            jax.ShapeDtypeStruct((images, seq, width), BF),
            jax.ShapeDtypeStruct((8, width), F32),
        ],
        scratch_shapes=[pltpu.VMEM((LANES, width), F32), pltpu.VMEM((seq, width), BF)],
        compiler_params=params(),
        cost_estimate=cost(2 * flops, 24 * tokens * width, HEADS * tokens * seq),
        name="backward_rest",
    )(head["gh"], head["gbr"], kept["x"], kept["qkv"], kept["lse"], pack)
    return dict(zip(("gx", "gqkv", "n1", "norms"), results))


def dense_grads(parts, tail, norms, blocks=None):
    images, seq, width = parts[0][0].shape
    widths = [right.shape[2] for _, right in parts]
    total = sum(widths) + LANES
    step = 256
    if blocks is None:
        core, count, shapes = jnp.zeros((1,), jnp.int32), 1, [(width, total)]
    else:
        core, count = blocks
        shapes = [(count // 2, width // count, total)] * 2
    pairs = list(parts) + ([] if tail is None else [tail])

    def body(core_ref, norms_ref, *refs):
        refs = list(refs)
        pair_refs = [(refs[2 * n], refs[2 * n + 1]) for n in range(len(pairs))]
        outs, (rows, flip, wide, extra_ref) = refs[2 * len(pairs) : -4], refs[-4:]

        def load(ref, store, columns):
            store[...] = jnp.zeros_like(store)
            for i in range(images):
                store[i * SEQ_PAD : i * SEQ_PAD + seq, 0:columns] = ref[i]

        def multiply(columns, source, extra=None):
            def value(at):
                found = nn(flip[at, :], wide[:, source]) if source is not None else None
                if extra is None:
                    return found
                return extra[at, :] if found is None else found + extra[at, :]

            if blocks is None:
                outs[0][:, columns] = value(slice(None)).astype(BF)
                return
            height = width // count
            for which in range(2):
                c = core_ref[0] if which == 0 else 1 - core_ref[0]
                for y in range(count // 2):
                    at = pl.ds(pl.multiple_of((2 * y + c) * height, 16), height)
                    outs[which][y, :, columns] = value(at).astype(BF)

        begin = 0
        for (left, right), size in zip(pair_refs, widths):
            load(left, rows, width)
            flip[...] = jnp.transpose(rows[...])
            load(right, wide, size)
            for c in range(size // step):
                multiply(slice(begin + c * step, begin + (c + 1) * step), slice(c * step, (c + 1) * step))
            begin += size
        extra_ref[...] = jnp.transpose(
            jnp.concatenate([jnp.zeros((32, width), F32), norms_ref[...], jnp.zeros((LANES - 40, width), F32)], 0)
        )
        if tail is not None:
            load(pair_refs[-1][0], rows, width)
            flip[...] = jnp.transpose(rows[...])
            load(pair_refs[-1][1], wide, LANES)
        multiply(slice(begin, total), None if tail is None else slice(0, LANES), extra_ref)

    arrays = [norms] + [array for pair in pairs for array in pair]
    tokens = images * seq
    return pl.pallas_call(
        body,
        grid=(1,),
        in_specs=[pl.BlockSpec(memory_space=pltpu.SMEM)] + [fixed(a) for a in arrays],
        out_specs=[resident(shape, lambda i, n=len(shape): (0,) * n) for shape in shapes],
        out_shape=[jax.ShapeDtypeStruct(shape, BF) for shape in shapes],
        scratch_shapes=[
            pltpu.VMEM((images * SEQ_PAD, width), BF),
            pltpu.VMEM((width, images * SEQ_PAD), BF),
            pltpu.VMEM((images * SEQ_PAD, max(widths)), BF),
            pltpu.VMEM((width, LANES), F32),
        ],
        compiler_params=params(),
        cost_estimate=cost(2 * tokens * width * total, 16 * tokens * width, 0),
        name="dense_grads",
    )(core, *arrays)


def ffn_forward(layer, j, xs, win, wdown):
    ny = len(xs)
    rows, width = xs[0].shape
    fs = win[0].shape[3]
    tile = min(256, rows)

    def body(*refs):
        xr, wi, wd, outs = refs[:ny], refs[ny : ny + 2], refs[ny + 2 : ny + 4], refs[ny + 4 :]
        for y in range(ny):
            total = None
            for s in range(2):
                hid = gelu(nn(xr[y][...], wi[s][...])).astype(BF)
                part = nt(hid, wd[s][...])
                total = part if total is None else total + part
            outs[y][...] = total.astype(outs[y].dtype)

    wspec = resident((None, None, width, fs), lambda t: (layer, j, 0, 0))
    rspec = pl.BlockSpec((tile, width), lambda t: (t, 0))
    return pl.pallas_call(
        body,
        grid=(rows // tile,),
        in_specs=[rspec] * ny + [wspec] * 4,
        out_specs=[rspec] * ny,
        out_shape=[jax.ShapeDtypeStruct((rows, width), F32 if y == 0 else BF) for y in range(ny)],
        compiler_params=params(),
        cost_estimate=cost(
            2 * 8 * ny * rows * width * fs, 8 * width * fs + 4 * ny * rows * width, 2 * ny * rows * fs
        ),
        name="ffn_forward",
    )(*xs, *win, *wdown)


def ffn_backward(layer, j, xs, gs, n, win, wdown, gates=None):
    ny = len(xs)
    rows, width = xs[0].shape
    fs = win[0].shape[3]
    fused = gates is not None

    def body(*refs):
        refs = list(refs)

        def take(n):
            taken = refs[:n]
            del refs[:n]
            return taken

        xr, gr, wi, wd = take(ny), take(ny), take(2), take(2)
        tr = take(ny) if fused else None
        gx, outs = take(ny), take(2)
        eo, gg = (take(ny), take(ny)) if fused else (None, None)
        acc = refs[0]
        for y in range(ny):
            x, g = xr[y][...], gr[y][...].reshape(rows, width)
            gated = g
            if fused:
                gate = jnp.transpose(jnp.broadcast_to(tr[y][...], (8, rows)))[:, 0:1]
                gated = (gate * g.astype(F32)).astype(BF)
            back, part, dot = None, None, None
            for s in range(2):
                w1, w2 = wi[s][...], wd[s][...]
                hid, slope = gelu_both(nn(x, w1))
                hid = hid.astype(BF)
                ghid = nn(g, w2)
                if fused:
                    term = jnp.sum(hid.astype(F32) * ghid, -1, keepdims=True)
                    dot = term if dot is None else dot + term
                    term = nt(hid, w2)
                    part = term if part is None else part + term
                    ghid = gate * ghid
                gpre = (ghid * slope).astype(BF)
                term = nt(gpre, w1)
                back = term if back is None else back + term
                for m, grad in enumerate((tn(x, gpre), tn(gated, hid))):
                    if s == 0:
                        outs[0][m] = grad if y == 0 else outs[0][m] + grad
                    elif y < ny - 1:
                        acc[m] = grad if y == 0 else acc[m] + grad
                    else:
                        outs[1][m] = (grad if y == 0 else acc[m] + grad).astype(BF)
            gx[y][...] = back.astype(gx[y].dtype)
            if fused:
                eo[y][...] = part.astype(eo[y].dtype)
                gg[y][...] = jnp.transpose(jnp.broadcast_to(dot, (rows, LANES)))[0:1, :]

    wspec = resident((None, None, width, fs), lambda c: (layer, j, 0, 0))
    rspec = resident((rows, width), lambda c: (0, 0))
    uspec = resident((rows // CAP, None, CAP, width), lambda c: (0, n, 0, 0))
    lspec = resident((1, rows), lambda c: (0, 0))
    gspec = resident((2, width, fs), lambda c: (0, 0, 0))
    parts = [jax.ShapeDtypeStruct((rows, width), F32 if y == 0 else BF) for y in range(ny)]
    shapes = parts + [jax.ShapeDtypeStruct((2, width, fs), F32), jax.ShapeDtypeStruct((2, width, fs), BF)]
    if fused:
        shapes += parts + [jax.ShapeDtypeStruct((1, rows), F32)] * ny
    return pl.pallas_call(
        body,
        grid=(1,),
        in_specs=[rspec] * ny + [uspec] * ny + [wspec] * 4 + [lspec] * (ny if fused else 0),
        out_specs=[rspec] * ny + [gspec] * 2 + ([rspec] * ny + [lspec] * ny if fused else []),
        out_shape=shapes,
        scratch_shapes=[pltpu.VMEM((2, width, fs), F32)],
        compiler_params=params(),
        cost_estimate=cost(
            2 * (24 if fused else 20) * ny * rows * width * fs, 20 * width * fs + 8 * ny * rows * width, 2 * ny * rows * fs
        ),
        name="ffn_backward",
    )(*xs, *gs, *win, *wdown, *(gates if fused else ()))


def store_grads(layer, j, local, own, received, buffers):
    _, width, fs = own.shape
    tile = width // 4

    def body(own_ref, recv_ref, *refs):
        outs = refs[-2:]
        for n in range(2):
            outs[n][...] = own_ref[n] + recv_ref[n].astype(F32)

    pspec = pl.BlockSpec((2, tile, fs), lambda t: (0, t, 0))
    ospec = pl.BlockSpec((None, None, tile, fs), lambda t: (layer, j, t, 0))
    full = jax.ShapeDtypeStruct((2, local, width, fs), F32)
    extra = [] if buffers is None else list(buffers)
    return pl.pallas_call(
        body,
        grid=(4,),
        in_specs=[pspec, pspec] + [pl.BlockSpec(memory_space=pl.ANY)] * len(extra),
        out_specs=[ospec, ospec],
        out_shape=[full, full],
        input_output_aliases={} if buffers is None else {2: 0, 3: 1},
        compiler_params=params(),
        cost_estimate=cost(2 * width * fs, 20 * width * fs, 0),
        name="store_grads",
    )(own, received, *extra)


def rows_shift(count, shift):
    ys = count // 2
    return [(y * 2 + c, ((y + shift) % ys) * 2 + c) for y in range(ys) for c in range(2)]


def spread_rows(mine, count):
    return [mine] + [lax.ppermute(mine, "fsdp", rows_shift(count, s)) for s in range(1, count // 2)]


def return_parts(parts, count):
    return [parts[0]] + [
        lax.ppermute(parts[s], "fsdp", rows_shift(count, -s)) for s in range(1, count // 2)
    ]


def add_parts(parts):
    total = parts[0]
    for part in parts[1:]:
        total = total + part.astype(F32)
    return total.astype(BF)


def step(live, works):
    fresh = dict(live)
    for work in works:
        fresh.update(work(live))
    return lax.optimization_barrier(fresh)


def staged(live, count, stages, extras, pending=()):
    total = count + len(stages) - 1
    waiting = [(0, value) for value in pending]
    for t in range(total):
        works = [
            lambda now, stage=stage, j=t - s: stage(now, j)
            for s, stage in enumerate(stages)
            if 0 <= t - s < count
        ]
        for at, until, work in extras:
            if t == min(at, total - 1):
                if until <= t:
                    works.append(work)
                else:
                    waiting.append((until, work(live)))
        for until, value in waiting:
            if t == until:
                works.append(lambda now, value=value: value)
        live = step(live, works)
    return live, {name: v for until, value in waiting if until >= total for name, v in value.items()}


def exchange(rows):
    return lax.all_to_all(rows, "expert", split_axis=0, concat_axis=0, tiled=True)


def swap_cores(array, count):
    return lax.ppermute(array, "fsdp", [(f, f ^ 1) for f in range(count)])


def shards(tokens_in, routes, valid, qkv_weight, out_weight, router_weight, norm_gain, norm_shift,
           expert_in, expert_down, cotangent):
    owners = lax.axis_size("expert")
    count = lax.axis_size("fsdp")
    local = expert_in.shape[1]
    layers = routes.shape[0]
    tokens, width = tokens_in.shape
    images = tokens // SEQ
    span = owners * CAP
    slots = (local, span)
    experts = router_weight.shape[2]

    packs = []
    for l in range(layers):
        shard = qkv_weight.shape[1]
        pieces = [qkv_weight[l], out_weight[l], router_weight[l], norm_gain[l].T, norm_shift[l].T]
        pieces.append(jnp.zeros((shard, LANES - experts - 4), BF))
        packs.append(jnp.concatenate(pieces, 1))
    win = (expert_in, swap_cores(expert_in, count))
    wdown = (expert_down, swap_cores(expert_down, count))

    def cut(array):
        return array.reshape(array.shape[:-2] + (images, SEQ, array.shape[-1]))

    route_cols = cut(routes)
    pcol, prow = route_places(route_cols, cut(valid), owners, local)
    cot = cut(cotangent)
    top = layers - 1

    def pick(record, *names):
        return {n: record[n] for n in names}

    def swap_y(now, name, out):
        return {out: spread_rows(now[name], count)}

    def send(now, name, out):
        return {out: exchange(now[name])}

    groups = [list(range(j, min(j + 2, local))) for j in range(0, local, 2)]
    where = {j: (g, n) for g, group in enumerate(groups) for n, j in enumerate(group)}
    live = {f"c{g}": rows for g, rows in enumerate(dispatch(cot, prow[top], slots, groups))}
    start = live
    live = step(
        live,
        [
            lambda now: {"pack0": lax.all_gather(packs[0], "fsdp", axis=0, tiled=True)},
        ],
    )
    sending = send(start, "c0", "g0")

    early = list(range(local))

    def enter(l):
        def work(now):
            previous = None
            stream = cut(tokens_in)
            if l > 0:
                previous = (now[f"e{l - 1}_{local - 1}"], pcol[l - 1], now[f"gate{l - 1}"], now[f"part{l - 1}"])
                stream = now[f"h{l - 1}"]
            pack = now[f"pack{l}"]
            record, sent, store, rows = block_forward(
                stream, pack, route_cols[l], pcol[l], prow[l], previous, l == top, slots
            )
            out = {f"{name}{l}": value for name, value in record.items() if name != "picks"}
            if l > 0:
                out[f"picks{l - 1}"] = record["picks"]
            out[f"s{l}_0"], out[f"store{l}"] = sent, store
            if l == top:
                out["grow"] = rows[0][0:1, :]
            return out

        return work

    def more(l):
        def work(now):
            rows = place_chunks([now[f"store{l}"]], prow[l], early[1:], span)
            return {f"s{l}_{j}": r for j, r in zip(early[1:], rows)}

        return work

    def come(l):
        return lambda now, j: send(now, f"s{l}_{j}", f"a{l}_{j}")

    def widen(l):
        return lambda now, j: swap_y(now, f"a{l}_{j}", f"x{l}_{j}")

    def back_y(now, name, out):
        return {out: add_parts(return_parts(now[name], count))}

    live["shards"] = packs[1:]
    before = live["shards"]
    live = step(
        live,
        [enter(0), lambda now: sending],
    )
    pending = [{f"pack{l + 1}": lax.all_gather(p, "fsdp", axis=0, tiled=True)} for l, p in enumerate(before)]
    for l in range(top):
        live, unjoined = staged(
            live,
            local,
            [
                come(l),
                widen(l),
                lambda now, j, l=l: {f"p{l}_{j}": ffn_forward(l, j, now[f"x{l}_{j}"], win, wdown)},
                lambda now, j, l=l: back_y(now, f"p{l}_{j}", f"r{l}_{j}"),
                lambda now, j, l=l: send(now, f"r{l}_{j}", f"e{l}_{j}"),
            ],
            [
                (0, 0, more(l)),
                (local + 3, local + 3, lambda now, l=l: {
                    f"part{l}": pick_chunks([now[f"e{l}_{j}"] for j in early[:-1]], pcol[l], False)
                }),
            ],
            pending if l == 0 else (),
        )
        works = [enter(l + 1)]
        if l + 1 == top:
            works += [lambda now, g=g: send(now, f"c{g}", f"g{g}") for g in range(1, len(groups))]
            works.append(lambda now: swap_y(now, "g0", "gy0"))
        live = step(live, works)

    def send_gates(now):
        rows = now["grow"].reshape(local, owners, CAP).transpose(1, 0, 2).reshape(owners, local * CAP)
        return {"ga": lax.all_to_all(rows, "expert", split_axis=0, concat_axis=0, tiled=True)}

    def widen_gates(now):
        rows = now["ga"].reshape(owners, local, CAP).transpose(1, 0, 2).reshape(local, span)
        return {"gates": spread_rows(rows, count)}

    def fused_rows(now, j):
        gates = [rows[j : j + 1] for rows in now["gates"]]
        ys = count // 2
        g, n = where[j]
        results = ffn_backward(top, j, now[f"x{top}_{j}"], now[f"gy{g}"], n, win, wdown, gates)
        return {
            f"q{top}_{j}": results[:ys],
            f"own{top}_{j}": results[ys],
            f"oth{top}_{j}": results[ys + 1],
            f"f{j}": results[ys + 2 : 2 * ys + 2],
            f"gg{j}": results[2 * ys + 2 :],
        }

    def plain_rows(l):
        def work(now, j):
            ys = count // 2
            gs = [rows.reshape(owners, 1, CAP, width) for rows in now[f"gy{l}_{j}"]]
            results = ffn_backward(l, j, now[f"x{l}_{j}"], gs, 0, win, wdown)
            return {f"q{l}_{j}": results[:ys], f"own{l}_{j}": results[ys], f"oth{l}_{j}": results[ys + 1]}

        return work

    def return_rows(l):
        def work(now, j):
            out = back_y(now, f"q{l}_{j}", f"t{l}_{j}")
            out[f"oth{l}_{j}"] = swap_cores(now[f"oth{l}_{j}"], count)
            return out

        return work

    def leave(l):
        return lambda now, j: send(now, f"t{l}_{j}", f"b{l}_{j}")

    def sum_early(l):
        return lambda now: {f"gpart{l}": pick_chunks([now[f"b{l}_{j}"] for j in early[:-1]], pcol[l], True)[0]}

    def return_gg(now):
        rows = [jnp.concatenate([now[f"gg{j}"][y] for j in range(local)], 0) for y in range(count // 2)]
        parts = return_parts(rows, count)
        total = parts[0]
        for part in parts[1:]:
            total = total + part
        return {"ggr": total}

    def send_gg(now):
        rows = now["ggr"].reshape(local, owners, CAP).transpose(1, 0, 2).reshape(owners, local * CAP)
        rows = lax.all_to_all(rows, "expert", split_axis=0, concat_axis=0, tiled=True)
        return {"ggs": rows.reshape(owners, local, CAP).transpose(1, 0, 2).reshape(local, span)}

    def keep(l, js):
        def work(now):
            buffers = now.get("buffers")
            for j in js:
                buffers = store_grads(l, j, local, now[f"own{l}_{j}"], now[f"oth{l}_{j}"], buffers)
            return {"buffers": buffers}

        return work

    live, unjoined = staged(
        live,
        local,
        [come(top), widen(top), fused_rows, return_rows(top), leave(top)],
        [(0, 0, send_gates), (0, 0, more(top)), (local + 3, local + 3, sum_early(top))]
        + [(0, 0, lambda now, g=g: swap_y(now, f"g{g}", f"gy{g}")) for g in range(1, len(groups))]
        + [(1, 1, widen_gates), (local + 2, local + 2, return_gg), (local + 3, local + 3, send_gg)]
        + [(local + 3, local + 3, lambda now, j=j: back_y(now, f"f{j}", f"fr{j}")) for j in early[:2]],
    )

    def scatter_sum(packed):
        return lax.psum_scatter(packed, "fsdp", scatter_dimension=0, tiled=True)

    def gather_all(rows):
        return lax.all_gather(rows, "expert", axis=0, tiled=True)

    def scatter_all(rows):
        return lax.psum_scatter(rows, "expert", scatter_dimension=0, tiled=True)

    def back_block(l):
        def work(now):
            kept = {name: now[f"{name}{l}"] for name in ("x", "h", "qkv", "lse")}
            if l < top:
                kept["picks"] = now[f"picks{l}"]
            below = None if l == 0 else (now[f"gate{l - 1}"], prow[l - 1])
            pack = now[f"pack{l}"]
            named, geo = block_backward(
                cot if l == top else now["grad"], kept, pack, route_cols[l], pcol[l],
                (now[f"gpart{l}"], now[f"b{l}_{local - 1}"]), now["ggs"] if l == top else None, below, slots
            )
            out = {f"{name}{l}": value for name, value in named.items() if name != "gx"}
            out["grad"] = named["gx"]
            if l > 0:
                out[f"d{l - 1}_0"], out[f"geo{l - 1}"] = geo[0], geo[1:]
            return out

        return work

    def grads_of(now, l):
        parts = [(now[f"n1{l}"], now[f"gqkv{l}"]), (now[f"a{l}"], now[f"gbr{l}"])]
        return dense_grads(parts, (now[f"n2{l}"], now[f"glog{l}"]), now[f"norms{l}"])

    def stack_eo(now, js):
        return jnp.stack([now[f"fr{j}"].reshape(owners, CAP, width) for j in js], 1)

    def send_eo(js):
        return lambda now: {f"eo{js[0]}": exchange(stack_eo(now, js))}

    live = step(
        live, [back_block(top), send_eo(early[:2])] + [lambda now, j=j: back_y(now, f"f{j}", f"fr{j}") for j in early[2:]]
    )
    for l in reversed(range(top)):
        extras = [(0, 0, lambda now, l=l: {f"dense{l + 1}": grads_of(now, l + 1)[0]})]
        extras += [(local + 2, local + 2, keep(l + 1, early[:1])), (1, 1, keep(l + 1, early[1:]))]
        if l == 0 and local > 2:
            extras.append((local + 3, local + 3, lambda now: {"frs": stack_eo(now, early[2:])}))
        extras.append((local + 3, local + 3, sum_early(l)))
        extras.append((0, 0, lambda now, l=l: {
            f"d{l}_{j}": r for j, r in zip(early[1:], place_chunks(now[f"geo{l}"], prow[l], early[1:], span))
        }))
        extras.append((1, local - 1, lambda now, l=l: {f"share{l + 1}": scatter_sum(now[f"dense{l + 1}"])}))
        extras.append((local, local + 2, lambda now, l=l: {f"piece{l + 1}": scatter_all(now[f"share{l + 1}"])}))
        extras.append((local + 3, local + 4, lambda now, l=l: {f"full{l + 1}": gather_all(now[f"piece{l + 1}"])}))
        live, unjoined = staged(
            live,
            local,
            [
                lambda now, j, l=l: send(now, f"d{l}_{j}", f"m{l}_{j}"),
                lambda now, j, l=l: swap_y(now, f"m{l}_{j}", f"gy{l}_{j}"),
                plain_rows(l),
                return_rows(l),
                leave(l),
            ],
            extras,
        )

    ys = count // 2
    place = lax.axis_index("fsdp")
    y_at, core_at = place // 2, place % 2
    blocks = (core_at.reshape(1), count)

    def head(now):
        kept = {"h": now["h0"], "picks": now["picks0"]}
        rows = (now["gpart0"], now[f"b0_{local - 1}"])
        named = backward_head(now["grad"], kept, now["pack0"], route_cols[0], pcol[0], rows, slots)
        return {f"{name}0": value for name, value in named.items()}

    def rest(now):
        kept = {name: now[f"{name}0"] for name in ("x", "qkv", "lse")}
        named = backward_rest({"gh": now["gh0"], "gbr": now["gbr0"]}, kept, now["pack0"])
        return {"gqkv0": named["gqkv"], "n10": named["n1"], "norms1st": named["norms"], "grad": named["gx"]}

    def core_swap(tag):
        return lambda now: {f"other{tag}": swap_cores(now[f"other{tag}"], count)}

    def add_cores(now, tag):
        pair = now[f"kept{tag}"].astype(F32) + now[f"other{tag}"].astype(F32)
        now[f"mine{tag}"] = lax.dynamic_index_in_dim(pair, y_at, 0, False)
        now[f"away{tag}"] = [
            lax.dynamic_index_in_dim(pair, (y_at + s) % ys, 0, False).astype(BF) for s in range(1, ys)
        ]

    def swap_dense(tag):
        def work(now):
            rows = zip(range(1, ys), now[f"away{tag}"])
            return {f"near{tag}": [lax.ppermute(r, "fsdp", rows_shift(count, s)) for s, r in rows]}

        return work

    def add_near(now, tag):
        total = now[f"mine{tag}"]
        for rows in now[f"near{tag}"]:
            total = total + rows.astype(F32)
        now[f"mine{tag}"] = total.astype(BF).reshape(owners, total.shape[0] // owners, total.shape[1])

    def add_far(now, tag):
        total = jnp.sum(now[f"mine{tag}"].astype(F32), 0).astype(BF)
        now[f"mine{tag}"] = jnp.broadcast_to(total[None], (owners,) + total.shape)

    def finish(now):
        eo = [now[f"eo{j}"] for j in early if f"eo{j}" in now]
        return {"out": combine_last(now[f"h{top}"], eo, pcol[top], now[f"gate{top}"])}

    later = send(live, "frs", "eo2") if local > 2 else {}
    live = step(live, [head])
    live["keptA"], live["otherA"] = dense_grads(
        [(live["a0"], live["gbr0"])], (live["n20"], live["glog0"]), live["norms0"], blocks
    )
    live = step(live, [core_swap("A"), rest, lambda now: unjoined])
    add_cores(live, "A")

    def grads_q(now):
        kept, other = dense_grads([(now["n10"], now["gqkv0"])], None, now["norms1st"], blocks)
        return {"keptQ": kept, "otherQ": other}

    live = step(live, [swap_dense("A"), grads_q])
    add_near(live, "A")
    apart = dict(live)
    live = step(live, [core_swap("Q"), lambda now: later])
    apart.update(send(apart, "mineA", "mineA"))
    add_far(apart, "A")
    apart = send(apart, "mineA", "mineA")
    add_cores(live, "Q")
    live = step(live, [swap_dense("Q"), lambda now: apart, keep(0, early[:2])])
    add_near(live, "Q")
    live = step(live, [lambda now: send(now, "mineQ", "mineQ"), keep(0, early[2:]), finish])
    add_far(live, "Q")
    live["grad"] = live["grad"].reshape(tokens, width)
    live["out"] = live["out"].reshape(tokens, width)
    height = width // count
    at = 4 * width + experts
    rest_of = [live[f"full{l}"] for l in range(1, layers)]

    def together(first, begin, end):
        return jnp.stack([first.astype(F32)] + [rows[:, begin:end].astype(F32) for rows in rest_of])

    def unpack(now):
        soon = now["mineA"].reshape(height, width + LANES)
        return {
            "g_out": together(soon[:, :width], 3 * width, 4 * width),
            "g_router": together(soon[:, width : width + experts], 4 * width, at),
            "g_norms": together(soon[:, width + experts : width + experts + 4], at, at + 4),
        }

    live = step(live, [lambda now: send(now, "mineQ", "mineQ"), unpack])
    out = live["out"]
    buffers = live["buffers"]
    grad = live["grad"]
    late = live["mineQ"].reshape(height, 3 * width + LANES)
    norms = live["g_norms"].at[0].add(late[:, 3 * width + experts : 3 * width + experts + 4].astype(F32))
    norms = jnp.swapaxes(norms, 1, 2)
    return (
        out,
        grad,
        together(late[:, : 3 * width], 0, 3 * width),
        live["g_out"],
        live["g_router"],
        norms[:, :2],
        norms[:, 2:],
        buffers[0],
        buffers[1],
    )


def solution(mesh):
    everyone = ("expert", "fsdp")
    return jax.shard_map(
        shards,
        mesh=mesh,
        in_specs=(
            P(everyone, None),
            P(None, everyone, None),
            P(None, everyone, None),
            P(None, "fsdp", None),
            P(None, "fsdp", None),
            P(None, "fsdp", None),
            P(None, None, "fsdp"),
            P(None, None, "fsdp"),
            P(None, "expert", None, "fsdp"),
            P(None, "expert", None, "fsdp"),
            P(everyone, None),
        ),
        out_specs=(
            P(everyone, None),
            P(everyone, None),
            P(None, "fsdp", None),
            P(None, "fsdp", None),
            P(None, "fsdp", None),
            P(None, None, "fsdp"),
            P(None, None, "fsdp"),
            P(None, "expert", None, "fsdp"),
            P(None, "expert", None, "fsdp"),
        ),
        check_vma=False,
    )
```
